32 devices in a mesh: member: 2 (over y), lon: 8 (over z, x), lat: 2 (over core).
Axes of the slice: x: 2, y: 2, z: 4, core: 2. Of those that a mesh axis runs over, the one named last changes fastest.
Arguments:
- state_field: bfloat16 [928, 32768], P('lat', ('member', 'lon')), parts along dimension 1, may hold values from -20 to 20
- skip_gain: float32 [4, 3, 64], replicated, may hold values from 0.25 to 2
- embed_weight: bfloat16 [64, 256], replicated, may hold values from -0.75 to 0.75
- qkv_weight: bfloat16 [256, 768], replicated, may hold values from -0.375 to 0.375
- head_scale: float32 [8], replicated, may hold values from 0.5 to 4
- out_weight: bfloat16 [256, 256], replicated, may hold values from -0.375 to 0.375
- norm_gain: float32 [256], replicated, may hold values from 0.1 to 1.9
- back_weight: bfloat16 [256, 64], replicated, may hold values from -0.375 to 0.375
Outputs:
- forecast: bfloat16 [928, 32768], P('lat', ('member', 'lon')), parts along dimension 1
The draws below stay inside these ranges and needn't reach their ends.
There are 2 independent parts, one for each index of `member`. The reference program is written for one: setup_inputs(seed, part) draws one part's arguments, and reference() takes and returns one part's arrays. A program takes and returns all parts, laid end to end along the dimension named above; an argument that names none is the same for every part. Nothing has to cross between parts.
All inputs are finite; a program needn't handle non-finite values.
Results may differ from the reference program's by a relative error of at most 0.0022.
Values may be sent and summed in bfloat16 or wider, within the bound.
No kernel may reach another device: no remote copies, remote signals or barrier semaphores. Data moves between devices by JAX's collectives and lax.ppermute only.
A program may use at most 128 MiB of HBM per device.

```python
import math
import jax
import jax.numpy as jnp
from jax import lax

C = 64
HEADS = 8
HEAD_DIM = 32
LEVELS = 4
E = 256
LAT = 928
LON = 256


def draw_state_field(key, part):
    base_key = jax.random.fold_in(jax.random.fold_in(key, 17), 0)
    values = jax.random.truncated_normal(base_key, -4.0, 4.0, (LAT, LON * C), jnp.float32)
    return values.astype(jnp.bfloat16)


def gaussian(rng, shape, scale, most, held_as=jnp.bfloat16):
    return jnp.clip(scale * jax.random.normal(rng, shape, jnp.float32), -most, most).astype(held_as)


def setup_inputs(seed: int = 0, part: int = 0) -> dict:
    arg_keys = jax.random.split(jax.random.key(seed), 9)
    part_keys = jax.random.split(jax.random.fold_in(arg_keys[8], part), 9)
    state_field = draw_state_field(jax.random.fold_in(jax.random.fold_in(arg_keys[8], part), 71), part)
    skip_gain = jnp.clip(jnp.exp(jax.random.uniform(arg_keys[1], (LEVELS, 3, C), jnp.float32, math.log(0.25), math.log(2.0))), 0.25, 2.0)
    embed_weight = gaussian(arg_keys[2], (C, E), C ** -0.5, 0.75)
    qkv_weight = gaussian(arg_keys[3], (E, 3 * E), E ** -0.5, 0.375)
    head_scale = jnp.clip(jnp.exp(jax.random.uniform(arg_keys[4], (HEADS,), jnp.float32, math.log(0.5), math.log(4.0))), 0.5, 4.0)
    out_weight = gaussian(arg_keys[5], (E, E), E ** -0.5, 0.375)
    norm_gain = jnp.clip(1.0 + 0.18 * jax.random.normal(arg_keys[6], (E,), jnp.float32), 0.1, 1.9)
    back_weight = gaussian(arg_keys[7], (E, C), E ** -0.5, 0.375)
    return {"state_field": state_field, "skip_gain": skip_gain, "embed_weight": embed_weight, "qkv_weight": qkv_weight, "head_scale": head_scale, "out_weight": out_weight, "norm_gain": norm_gain, "back_weight": back_weight}


low_taps = (-0.010597401784997278, 0.032883011666982945, 0.030841381835986965, -0.18703481171888114, -0.02798376941698385, 0.6308807679295904, 0.7148465705525415, 0.23037781330885523)
high_taps = tuple(((-1.0) ** index * low_taps[7 - index] for index in range(8)))

def split_rows(padded):
    half_count = (padded.shape[0] - 6) // 2
    paired = padded.reshape((padded.shape[0] // 2, 2) + padded.shape[1:])
    lower = jnp.zeros((half_count,) + padded.shape[1:], jnp.float32)
    upper = jnp.zeros((half_count,) + padded.shape[1:], jnp.float32)
    for tap_pair in range(4):
        even_rows = paired[tap_pair:tap_pair + half_count, 0]
        odd_rows = paired[tap_pair:tap_pair + half_count, 1]
        lower = lower + low_taps[2 * tap_pair] * even_rows + low_taps[2 * tap_pair + 1] * odd_rows
        upper = upper + high_taps[2 * tap_pair] * even_rows + high_taps[2 * tap_pair + 1] * odd_rows
    return (lower, upper)

def split_columns(padded):
    row_count = padded.shape[0]
    half_count = padded.shape[1] // (2 * C) - 3
    paired = padded.reshape(row_count, half_count + 3, 2 * C)
    lower = jnp.zeros((row_count, half_count, C), jnp.float32)
    upper = jnp.zeros((row_count, half_count, C), jnp.float32)
    for tap_pair in range(4):
        window = paired[:, tap_pair:tap_pair + half_count]
        even_cells = window[:, :, :C]
        odd_cells = window[:, :, C:]
        lower = lower + low_taps[2 * tap_pair] * even_cells + low_taps[2 * tap_pair + 1] * odd_cells
        upper = upper + high_taps[2 * tap_pair] * even_cells + high_taps[2 * tap_pair + 1] * odd_cells
    return (lower.reshape(row_count, half_count * C), upper.reshape(row_count, half_count * C))

def join_rows(lower, upper):
    half_count = lower.shape[0] - 4
    even_rows = jnp.zeros((half_count,) + lower.shape[1:], jnp.float32)
    odd_rows = jnp.zeros((half_count,) + lower.shape[1:], jnp.float32)
    for tap_pair in range(4):
        even_start = 3 - tap_pair
        odd_start = 4 - tap_pair
        even_rows = even_rows + low_taps[2 * tap_pair + 1] * lower[even_start:even_start + half_count] + high_taps[2 * tap_pair + 1] * upper[even_start:even_start + half_count]
        odd_rows = odd_rows + low_taps[2 * tap_pair] * lower[odd_start:odd_start + half_count] + high_taps[2 * tap_pair] * upper[odd_start:odd_start + half_count]
    return jnp.stack([even_rows, odd_rows], 1).reshape((2 * half_count,) + lower.shape[1:])

def join_columns(lower, upper):
    row_count = lower.shape[0]
    half_count = lower.shape[1] // C - 4
    lower_cells = lower.reshape(row_count, half_count + 4, C)
    upper_cells = upper.reshape(row_count, half_count + 4, C)
    even_cells = jnp.zeros((row_count, half_count, C), jnp.float32)
    odd_cells = jnp.zeros((row_count, half_count, C), jnp.float32)
    for tap_pair in range(4):
        even_start = 3 - tap_pair
        odd_start = 4 - tap_pair
        even_cells = even_cells + low_taps[2 * tap_pair + 1] * lower_cells[:, even_start:even_start + half_count] + high_taps[2 * tap_pair + 1] * upper_cells[:, even_start:even_start + half_count]
        odd_cells = odd_cells + low_taps[2 * tap_pair] * lower_cells[:, odd_start:odd_start + half_count] + high_taps[2 * tap_pair] * upper_cells[:, odd_start:odd_start + half_count]
    return jnp.stack([even_cells, odd_cells], 2).reshape(row_count, 2 * half_count * C)

def wrap_columns(source, margin):
    return jnp.concatenate([source[..., -margin:], source, source[..., :margin]], -1)

def attend_all(queries, keys, values, head_scale):
    query_count = queries.shape[0]
    block_size = math.gcd(query_count, 512)
    factor = head_scale / math.sqrt(HEAD_DIM)
    key_heads = keys.astype(jnp.float32).reshape(-1, HEADS, HEAD_DIM)
    value_heads = values.astype(jnp.float32).reshape(-1, HEADS, HEAD_DIM)

    def one_block(query_block):
        query_heads = query_block.astype(jnp.float32).reshape(block_size, HEADS, HEAD_DIM)
        scores = jnp.einsum('qhd,khd->hqk', query_heads, key_heads, precision=lax.Precision.HIGHEST) * factor[:, None, None]
        row_max = lax.optimization_barrier(jnp.max(scores, -1, keepdims=True))
        weights = jnp.exp(scores - row_max)
        row_total = lax.optimization_barrier(jnp.sum(weights, -1))
        rounded = lax.optimization_barrier(weights.astype(jnp.bfloat16)).astype(jnp.float32)
        weighted = jnp.einsum('hqk,khd->qhd', rounded, value_heads, precision=lax.Precision.HIGHEST)
        weighted = weighted / jnp.transpose(row_total)[:, :, None]
        return weighted.reshape(block_size, E).astype(jnp.bfloat16)
    blocks = queries.reshape(query_count // block_size, block_size, E)
    return lax.map(one_block, blocks).reshape(query_count, E)

def reference(state_field, skip_gain, embed_weight, qkv_weight, head_scale, out_weight, norm_gain, back_weight):
    current_grid = state_field.astype(jnp.float32)
    details = []
    for level_index in range(LEVELS):
        padded = jnp.pad(current_grid, ((3, 3), (0, 0)))
        padded = wrap_columns(padded, 3 * C)
        lon_low, lon_high = split_columns(padded)
        low_low, high_low = split_rows(lon_low)
        low_high, high_high = split_rows(lon_high)
        bands = jnp.stack([low_high, high_low, high_high])
        cell_count = low_low.shape[1] // C
        gains = jnp.tile(skip_gain[level_index], (1, cell_count))[:, None, :]
        details.append(bands * gains)
        current_grid = low_low
    row_count, column_count = current_grid.shape
    tokens = current_grid.reshape(-1, C).astype(jnp.bfloat16)
    embedded = jnp.dot(tokens, embed_weight, preferred_element_type=jnp.float32)
    widened = embedded.astype(jnp.bfloat16)
    projected = jnp.dot(widened, qkv_weight, preferred_element_type=jnp.float32).astype(jnp.bfloat16)
    attended = attend_all(projected[:, :E], projected[:, E:2 * E], projected[:, 2 * E:], head_scale)
    hidden = embedded + jnp.dot(attended, out_weight, preferred_element_type=jnp.float32)
    normed = (hidden * lax.rsqrt(lax.optimization_barrier(jnp.mean(hidden * hidden, -1, keepdims=True)) + 1e-06) * norm_gain).astype(jnp.bfloat16)
    update = jnp.dot(normed, back_weight, preferred_element_type=jnp.float32)
    current_grid = current_grid + update.reshape(row_count, column_count)
    for level_index in reversed(range(LEVELS)):
        stacked = jnp.concatenate([current_grid[None], details[level_index]], 0)
        padded = jnp.pad(stacked, ((0, 0), (2, 2), (0, 0)))
        padded = wrap_columns(padded, 2 * C)
        lon_low = join_rows(padded[0], padded[2])
        lon_high = join_rows(padded[1], padded[3])
        current_grid = join_columns(lon_low, lon_high)
    return current_grid.astype(jnp.bfloat16)
```

```python
import functools
import math

import jax
import jax.numpy as jnp
import numpy as np
from jax import lax
from jax.experimental import pallas as pl
from jax.experimental.pallas import tpu as pltpu
from jax.sharding import PartitionSpec as P

C = 64
HEADS = 8
HEAD_DIM = 32
E = 256
LANES = 128
HALO = 96
LEAD = 16

LOW = np.array(
    [
        -0.010597401784997278,
        0.032883011666982945,
        0.030841381835986965,
        -0.18703481171888114,
        -0.02798376941698385,
        0.6308807679295904,
        0.7148465705525415,
        0.23037781330885523,
    ]
)
HIGH = np.array([(-1.0) ** j * LOW[7 - j] for j in range(8)])
F32 = jnp.float32
BF16 = jnp.bfloat16


def analysis_matrix(taps, out_start, out_rows, in_start, in_rows):
    m = np.zeros((out_rows, in_rows), np.float32)
    for j in range(out_rows):
        for t in range(8):
            r = 2 * (out_start + j) - 3 + t - in_start
            if 0 <= r < in_rows:
                m[j, r] = taps[t]
    return m


def synthesis_matrix(taps, out_start, out_rows, in_start, in_rows):
    m = np.zeros((out_rows, in_rows), np.float32)
    for j in range(out_rows):
        for r in range(in_rows):
            t = out_start + j - 2 * (in_start + r) + 3
            if 0 <= t < 8:
                m[j, r] = taps[t]
    return m


def two_terms(value):
    top = value.astype(BF16)
    return top, (value - top.astype(F32)).astype(BF16)


def masked_rows(matrix, start, count, lat, lats):
    row = lax.broadcasted_iota(jnp.int32, matrix.shape, 0) + (start + lat * count)
    return jnp.where((row >= 0) & (row < count * lats), matrix, 0.0)


def mxu(a, b):
    return jnp.dot(a, b, preferred_element_type=F32)


def dot3(matrix, value):
    mh, ml = two_terms(matrix)
    vh, vl = two_terms(value)
    return mxu(mh, vh) + mxu(mh, vl) + mxu(ml, vh)


def lane_pair(rows, even, odd):
    lane = lax.broadcasted_iota(jnp.int32, (rows, LANES), 1)
    return jnp.where(lane < C, F32(even), F32(odd))


def split_weights(rows, taps):
    def tap(j):
        return float(taps[j]) if 0 <= j < 8 else 0.0

    return [lane_pair(rows, tap(2 * d + 3), tap(2 * d + 4)) for d in range(-2, 3)]


def first_half(rows):
    return lax.broadcasted_iota(jnp.int32, (rows, LANES), 1) < C


def half_turn(value):
    return pltpu.roll(value, C, 1)


def split_pair(cols, start, k, weights, left):
    def one(cell):
        total = None
        for d in range(-2, 3):
            p = cell + d - start
            if 0 <= p < len(cols):
                term = weights[d + 2] * cols[p]
                total = term if total is None else total + term
        return total

    a, b = one(k), one(k + 1)
    zero = jnp.zeros(cols[0].shape, F32)
    a = zero if a is None else a
    b = zero if b is None else b
    return jnp.where(left, a, b) + half_turn(jnp.where(left, b, a))


def both_halves(cols, left):
    cells = []
    for col in cols:
        turned = half_turn(col)
        cells.append(jnp.where(left, col, turned))
        cells.append(jnp.where(left, turned, col))
    return cells


def join_weights(rows, taps, odd_first):
    def tap(t):
        return float(taps[t]) if 0 <= t < 8 else 0.0

    if odd_first:
        return [lane_pair(rows, tap(6 - 2 * i), tap(7 - 2 * i)) for i in range(4)]
    return [lane_pair(rows, tap(7 - 2 * i), tap(8 - 2 * i)) for i in range(5)]


def join_pair(low_cells, high_cells, index, weights_low, weights_high):
    total = None
    for i in range(len(weights_low)):
        term = weights_low[i] * low_cells[index + i] + weights_high[i] * high_cells[index + i]
        total = term if total is None else total + term
    return total


def columns(ref, row, rows, lead=()):
    count = ref.shape[-1] // LANES
    return [ref[lead + (pl.ds(row, rows), pl.ds(LANES * p, LANES))] for p in range(count)]


def put(ref, row, rows, p, value, lead=()):
    ref[lead + (pl.ds(row, rows), pl.ds(LANES * p, LANES))] = value


class Geometry:
    def __init__(self, rows, cells):
        self.rows = [rows >> level for level in range(5)]
        self.cells = [cells >> level for level in range(5)]
        up = lambda value, step: -(-value // step) * step
        self.band = [None, (-4, up(self.rows[1] + 4, 16))]
        self.low = [None, (-52, up(self.rows[1] + 97, 112))]
        self.band.append((-8, up(self.rows[2] + 11, 16)))
        self.low.append((-24, up(self.rows[2] + 45, 8)))
        self.band.append((-3, up(self.rows[3] + 6, 8)))
        self.low.append((-11, up(self.rows[3] + 20, 8)))
        self.band.append((-3, up(self.rows[4] + 6, 8)))
        self.low.append((-3, up(self.rows[4] + 6, 8)))
        self.band_cells = [None, (-2, self.cells[1] // 2 + 2)]
        self.low_cells = [None, (-2, self.cells[1] // 2 + 2)]
        for level in (2, 3, 4):
            self.band_cells.append((-3, self.cells[level] // 2 + 3))
            self.low_cells.append((-4, self.cells[level] // 2 + 4))
        self.extended = LEAD + HALO + rows + HALO
        blocks = self.low[1][1] // 112
        self.extended = max(self.extended, 224 * (blocks - 1) + 256)


STEP = 8


def first_level_kernel(geo, lats, place, x, edge, tl, th, gain, g1, d1, send_e, send_o, ext, la, ha):
    lat, parity = place[0], place[1]
    rows = geo.rows[0]
    low_start, low_rows = geo.low[1]
    band_start, band_rows = geo.band[1]
    width = x.shape[1]
    top = slice(LEAD, LEAD + HALO)
    bottom = slice(LEAD + HALO + rows, LEAD + 2 * HALO + rows)
    ext[0:LEAD, :] = jnp.zeros((LEAD, width), BF16)
    tail = geo.extended - (LEAD + 2 * HALO + rows)
    if tail:
        ext[geo.extended - tail :, :] = jnp.zeros((tail, width), BF16)
    ext[LEAD + HALO : LEAD + HALO + rows, :] = x[...]

    @pl.when(lat == 0)
    def _():
        ext[top, :] = jnp.zeros((HALO, width), BF16)
        ext[bottom, :] = edge[...]

    @pl.when(lat != 0)
    def _():
        ext[top, :] = edge[...]
        ext[bottom, :] = jnp.zeros((HALO, width), BF16)

    for b in range(low_rows // 112):
        mh, ml = two_terms(masked_rows(tl[...], low_start + 112 * b, geo.rows[1], lat, lats))
        data = ext[224 * b : 224 * b + 256, :]
        la[112 * b : 112 * b + 112, :] = mxu(mh, data) + mxu(ml, data)
    for b in range(band_rows // 120):
        mh, ml = two_terms(masked_rows(th[...], band_start + 120 * b, geo.rows[1], lat, lats))
        data = ext[96 + 240 * b : 352 + 240 * b, :]
        ha[120 * b : 120 * b + 120, :] = mxu(mh, data) + mxu(ml, data)

    wl, wh = split_weights(STEP, LOW), split_weights(STEP, HIGH)
    left = first_half(STEP)
    first, pairs = geo.low_cells[1]

    def lows(c, carry):
        row = pl.multiple_of(c * STEP, STEP)
        cols = columns(la, row, STEP)
        for q in range(pairs):
            put(g1, row, STEP, q, split_pair(cols, 0, first + 2 * q, wl, left))
        return carry

    lax.fori_loop(0, low_rows // STEP, lows, 0)
    bfirst, bpairs = geo.band_cells[1]
    skip = band_start - low_start

    def details(c, carry):
        row = pl.multiple_of(c * STEP, STEP)
        cols = columns(la, row + skip, STEP)
        g = [jnp.broadcast_to(gain[b : b + 1, :], (STEP, LANES)) for b in range(3)]
        for q in range(bpairs):
            put(d1, row, STEP, q, split_pair(cols, 0, bfirst + 2 * q, wh, left) * g[0], (0,))
        cols = columns(ha, row, STEP)
        for q in range(bpairs):
            put(d1, row, STEP, q, split_pair(cols, 0, bfirst + 2 * q, wl, left) * g[1], (1,))
            put(d1, row, STEP, q, split_pair(cols, 0, bfirst + 2 * q, wh, left) * g[2], (2,))
        return carry

    lax.fori_loop(0, band_rows // STEP, details, 0)
    edge_lanes = 2 * LANES
    shift = (geo.cells[1] // 2) * LANES

    def fill(to_left, to_right):
        for b in range(3):
            at = slice(b * edge_lanes, (b + 1) * edge_lanes)
            to_left[:, at] = d1[b, :, 0:edge_lanes].astype(BF16)
            to_right[:, at] = d1[b, :, shift : shift + edge_lanes].astype(BF16)

    @pl.when(parity == 0)
    def _():
        fill(send_o, send_e)

    @pl.when(parity != 0)
    def _():
        fill(send_e, send_o)


def deep_kernel(geo, lats, place, g1, *refs):
    lat, parity = place[0], place[1]
    mats, refs = refs[:6], refs[6:]
    gain, refs = refs[0], refs[1:]
    d = {2: refs[0], 3: refs[1], 4: refs[2]}
    ll4, send_e, send_o, p2, m2, p3, m3 = refs[3:10]
    scratch = refs[10:]
    grids = {1: g1, 2: scratch[0], 3: scratch[1], 4: ll4}
    lo = {2: scratch[2], 3: scratch[4], 4: scratch[6]}
    hi = {2: scratch[3], 3: scratch[5], 4: scratch[7]}
    wl, wh = split_weights(STEP, LOW), split_weights(STEP, HIGH)
    left = first_half(STEP)
    for level in (2, 3, 4):
        n = geo.rows[level]
        low_start, low_rows = geo.low[level]
        band_start, band_rows = geo.band[level]
        source = grids[level - 1]
        vh, vl = two_terms(source[...])
        for matrix, start, out in (
            (mats[2 * (level - 2)], low_start, lo[level]),
            (mats[2 * (level - 2) + 1], band_start, hi[level]),
        ):
            mh, ml = two_terms(masked_rows(matrix[...], start, n, lat, lats))
            out[...] = mxu(mh, vh) + mxu(mh, vl) + mxu(ml, vh)
        in_start = geo.low_cells[level - 1][0] // 2
        first, pairs = geo.low_cells[level]
        bfirst, bpairs = geo.band_cells[level]
        skip = band_start - low_start
        target = grids[level]
        bands = d[level]

        def lows(c, carry):
            row = pl.multiple_of(c * STEP, STEP)
            cols = columns(lo[level], row, STEP)
            for q in range(pairs):
                put(target, row, STEP, q, split_pair(cols, in_start, first + 2 * q, wl, left))
            return carry

        lax.fori_loop(0, low_rows // STEP, lows, 0)

        def details(c, carry):
            row = pl.multiple_of(c * STEP, STEP)
            g = [
                jnp.broadcast_to(gain[3 * (level - 2) + b : 3 * (level - 2) + b + 1, :], (STEP, LANES))
                for b in range(3)
            ]
            cols = columns(lo[level], row + skip, STEP)
            for q in range(bpairs):
                out = split_pair(cols, in_start, bfirst + 2 * q, wh, left) * g[0]
                put(bands, row, STEP, q, out, (0,))
            cols = columns(hi[level], row, STEP)
            for q in range(bpairs):
                out = split_pair(cols, in_start, bfirst + 2 * q, wl, left) * g[1]
                put(bands, row, STEP, q, out, (1,))
                out = split_pair(cols, in_start, bfirst + 2 * q, wh, left) * g[2]
                put(bands, row, STEP, q, out, (2,))
            return carry

        lax.fori_loop(0, band_rows // STEP, details, 0)

    def fill(distance, to_left, to_right):
        for at, level, count, row in exchange_plan(geo)[distance]:
            n = geo.band[level][1]
            move = distance * geo.cells[level] // 2
            for b in range(3):
                lanes = slice(b * count * LANES, (b + 1) * count * LANES)
                to_left[row : row + n, lanes] = d[level][b, :, 0 : count * LANES].astype(BF16)
                to_right[row : row + n, lanes] = d[level][
                    b, :, move * LANES : (move + count) * LANES
                ].astype(BF16)

    @pl.when(parity == 0)
    def _():
        fill(1, send_o, send_e)

    @pl.when(parity != 0)
    def _():
        fill(1, send_e, send_o)

    fill(2, m2, p2)
    fill(3, m3, p3)


def exchange_plan(geo):
    plan = {}
    for distance in (1, 2, 3):
        entries, row = [], 0
        for level in (2, 3, 4):
            count = geo.band_cells[level][1] - distance * geo.cells[level] // 2
            if count > 0:
                entries.append((len(entries), level, count, row))
                row += -(-geo.band[level][1] // 16) * 16
        plan[distance] = entries
    return plan


def plan_shape(geo, distance):
    entries = exchange_plan(geo)[distance]
    rows = sum(-(-geo.band[level][1] // 16) * 16 for _, level, _, _ in entries)
    return (rows, max(count for _, _, count, _ in entries) * 3 * LANES)


def attention_kernel(geo, lats, blocks, place, keys, grid, we, wqkv, scale, wo, gain, wb, out):
    lat = place[0]
    rows, width = grid.shape
    cells = width // C
    field = grid[...]
    own = jnp.concatenate([field[:, C * c : C * (c + 1)] for c in range(cells)], 0)
    count = own.shape[0]
    embedded = mxu(own.astype(BF16), we[...])
    queries = mxu(embedded.astype(BF16), wqkv[:, 0:E]).astype(BF16)
    lane = lax.broadcasted_iota(jnp.int32, (1, E), 1)
    block = keys.shape[0] // blocks
    factor = [scale[h] * (1.0 / math.sqrt(HEAD_DIM)) for h in range(HEADS)]

    def keyvals(start):
        spread = mxu(keys[pl.ds(start, block), :], we[...]).astype(BF16)
        both = mxu(spread, wqkv[:, E : 3 * E]).astype(BF16)
        return both[:, 0:E], both[:, E : 2 * E]

    def scores_of(h, k):
        mine = (lane >= h * HEAD_DIM) & (lane < (h + 1) * HEAD_DIM)
        q = jnp.where(mine, queries, jnp.zeros_like(queries))
        s = lax.dot_general(q, k, (((1,), (1,)), ((), ())), preferred_element_type=F32)
        return s * factor[h]

    def masked(h, value):
        mine = (lane >= h * HEAD_DIM) & (lane < (h + 1) * HEAD_DIM)
        return jnp.where(mine, value, jnp.zeros_like(value))

    if blocks == 1:
        k, v = keyvals(0)
        attended = jnp.zeros((count, E), F32)
        for h in range(HEADS):
            s = scores_of(h, k)
            w = jnp.exp(s - jnp.max(s, -1, keepdims=True))
            total = jnp.sum(w, -1, keepdims=True)
            attended = attended + masked(h, mxu(w.astype(BF16), v) / total)
    else:

        def one_block(b, carry):
            peaks, totals, sums = carry
            k, v = keyvals(pl.multiple_of(b * block, 16))
            new_peaks, new_totals = [], []
            shrunk = jnp.zeros((count, E), F32)
            for h in range(HEADS):
                s = scores_of(h, k)
                peak = jnp.maximum(peaks[h], jnp.max(s, -1, keepdims=True))
                shrink = jnp.exp(peaks[h] - peak)
                w = jnp.exp(s - peak)
                new_peaks.append(peak)
                new_totals.append(totals[h] * shrink + jnp.sum(w, -1, keepdims=True))
                shrunk = shrunk + masked(h, sums * shrink + mxu(w.astype(BF16), v))
            return tuple(new_peaks), tuple(new_totals), shrunk

        start = (
            tuple(jnp.full((count, 1), -1e30, F32) for _ in range(HEADS)),
            tuple(jnp.zeros((count, 1), F32) for _ in range(HEADS)),
            jnp.zeros((count, E), F32),
        )
        _, totals, sums = lax.fori_loop(0, blocks, one_block, start)
        attended = jnp.zeros((count, E), F32)
        for h in range(HEADS):
            attended = attended + masked(h, sums / totals[h])
    hidden = embedded + mxu(attended.astype(BF16), wo[...])
    square = jnp.mean(hidden * hidden, -1, keepdims=True)
    normed = (hidden * lax.rsqrt(square + 1e-06) * gain[...]).astype(BF16)
    update = mxu(normed, wb[...])
    back = [
        jnp.concatenate(
            [update[rows * c : rows * (c + 1), :], update[rows * (c + 1) : rows * (c + 2), :]], 1
        )
        for c in range(0, cells, 2)
    ]
    start = geo.band[4][0]
    for q, value in enumerate(back):
        at = slice(q * LANES, (q + 1) * LANES)
        out[:, at] = masked_rows(field[:, at] + value, start, geo.rows[4], lat, lats)


def synthesis_kernel(geo, lats, place, coarse, d1, d2, d3, d4, *refs):
    lat, parity = place[0], place[1]
    e1, o1, e2, o2, from_m2, from_p2, from_m3, from_p3 = refs[:8]
    mats, refs = refs[8:16], refs[16:]
    out, up3, up2, up1, sides, xh, xl, ylow, yhigh = refs
    bands = {2: d2, 3: d3, 4: d4}
    plan = exchange_plan(geo)
    left = first_half(STEP)

    def from_sides(level, b):
        n = geo.band[level][1]
        pairs = geo.band_cells[level][1]
        cols = [bands[level][b, :, LANES * p : LANES * (p + 1)] for p in range(pairs)]
        for distance in (1, 2, 3):
            for at, which, count, row in plan[distance]:
                if which != level:
                    continue
                move = distance * geo.cells[level] // 2
                for p in range(count):
                    lanes = slice((b * count + p) * LANES, (b * count + p + 1) * LANES)
                    if distance == 1:
                        even, odd = e2[row : row + n, lanes], o2[row : row + n, lanes]
                        low = jnp.where(parity == 0, odd.astype(F32), even.astype(F32))
                        high = jnp.where(parity == 0, even.astype(F32), odd.astype(F32))
                    else:
                        lows, highs = {2: (from_m2, from_p2), 3: (from_m3, from_p3)}[distance]
                        low = lows[row : row + n, lanes].astype(F32)
                        high = highs[row : row + n, lanes].astype(F32)
                    cols[p] = cols[p] + low
                    cols[p + move] = cols[p + move] + high
        return cols

    uppers = {4: coarse, 3: up3, 2: up2, 1: up1}
    for level in (4, 3, 2):
        pairs = geo.band_cells[level][1]
        m_low, m_high = mats[2 * (4 - level)], mats[2 * (4 - level) + 1]
        below = level - 1
        start, rows = geo.band[below]
        s_low = masked_rows(m_low[...], start, geo.rows[below], lat, lats)
        s_high = masked_rows(m_high[...], start, geo.rows[below], lat, lats)
        source = uppers[level][...]
        lonlow = dot3(s_low, source) + dot3(s_high, jnp.concatenate(from_sides(level, 1), 1))
        lonhigh = dot3(s_low, jnp.concatenate(from_sides(level, 0), 1)) + dot3(
            s_high, jnp.concatenate(from_sides(level, 2), 1)
        )
        width = pairs * LANES
        ylow[0:rows, 0:width] = lonlow
        yhigh[0:rows, 0:width] = lonhigh
        odd = below > 1
        wl, wh = join_weights(STEP, LOW, odd), join_weights(STEP, HIGH, odd)
        target = uppers[below]
        first, out_pairs = geo.band_cells[below]
        begin = geo.band_cells[level][0]

        def joined(c, carry):
            row = pl.multiple_of(c * STEP, STEP)
            lo = both_halves([ylow[pl.ds(row, STEP), pl.ds(LANES * p, LANES)] for p in range(pairs)], left)
            hi = both_halves([yhigh[pl.ds(row, STEP), pl.ds(LANES * p, LANES)] for p in range(pairs)], left)
            for q in range(out_pairs):
                m = first + 2 * q
                a = (m - 1) // 2 if odd else m // 2
                index = (a - 1 if odd else a - 2) - begin
                put(target, row, STEP, q, join_pair(lo, hi, index, wl, wh))
            return carry

        lax.fori_loop(0, rows // STEP, joined, 0)

    n = geo.band[1][1]
    pairs = geo.band_cells[1][1]
    edge = 2 * LANES
    shift = (geo.cells[1] // 2) * LANES
    for b in range(3):
        at = slice(b * edge, (b + 1) * edge)
        even, odd = e1[:, at].astype(F32), o1[:, at].astype(F32)
        sides[b, 0] = jnp.where(parity == 0, odd, even)
        sides[b, 1] = jnp.where(parity == 0, even, odd)
    half = geo.rows[0] // 2
    for block in range(2):
        w = 0 if block == 0 else n - LANES
        window = slice(w, w + LANES)
        sh, sl = two_terms(mats[6 + block][...])
        for pieces, y in (((None, 1), ylow), ((0, 2), yhigh)):
            for i, b in enumerate(pieces):
                place_rows = slice(i * LANES, (i + 1) * LANES)
                if b is None:
                    h, l = two_terms(up1[window, :])
                    xh[place_rows, :], xl[place_rows, :] = h, l
                else:
                    for lanes, extra in (
                        (slice(0, edge), sides[b, 0, window, :]),
                        (slice(edge, shift), None),
                        (slice(shift, shift + edge), sides[b, 1, window, :]),
                    ):
                        value = d1[b, window, lanes]
                        h, l = two_terms(value if extra is None else value + extra)
                        xh[place_rows, lanes], xl[place_rows, lanes] = h, l
            y[half * block : half * (block + 1), :] = (
                mxu(sh, xh[...]) + mxu(sh, xl[...]) + mxu(sl, xh[...])
            )
    rows16 = 16
    left16 = first_half(rows16)
    wl, wh = join_weights(rows16, LOW, False), join_weights(rows16, HIGH, False)

    def last(c, carry):
        row = pl.multiple_of(c * rows16, rows16)
        lo = both_halves(columns(ylow, row, rows16), left16)
        hi = both_halves(columns(yhigh, row, rows16), left16)
        for q in range(geo.cells[0] // 2):
            put(out, row, rows16, q, join_pair(lo, hi, q, wl, wh).astype(BF16))
        return carry

    lax.fori_loop(0, geo.rows[0] // rows16, last, 0)


def call(kernel, out_shape, scratch, *args, cost=20_000_000):
    vmem = pl.BlockSpec(memory_space=pltpu.VMEM)
    smem = pl.BlockSpec(memory_space=pltpu.SMEM)
    specs = [smem if a.ndim == 1 else vmem for a in args]
    outs = jax.tree.map(lambda _: vmem, out_shape)
    return pl.pallas_call(
        kernel,
        out_shape=out_shape,
        in_specs=specs,
        out_specs=outs,
        scratch_shapes=scratch,
        compiler_params=pltpu.CompilerParams(vmem_limit_bytes=56 << 20),
        cost_estimate=pl.CostEstimate(flops=cost, bytes_accessed=1 << 20, transcendentals=0),
    )(*args)


def shape(dims, dtype=F32):
    return jax.ShapeDtypeStruct(dims, dtype)


def per_device(mesh_shape, state_field, skip_gain, embed_weight, qkv_weight, head_scale, out_weight, norm_gain, back_weight):
    lons, lats = mesh_shape["lon"], mesh_shape["lat"]
    rows, width = state_field.shape
    geo = Geometry(rows, width // C)
    lat, lon = lax.axis_index("lat"), lax.axis_index("lon")
    place = jnp.stack([lat, lon % 2]).astype(jnp.int32)
    gains = jnp.tile(skip_gain, (1, 1, 2)).reshape(-1, LANES)

    even_pairs = [(i, i ^ 1) for i in range(lons)]
    odd_pairs = [(i, (i + 1 if i % 2 else i - 1) % lons) for i in range(lons)]
    swap = [(i, lats - 1 - i) for i in range(lats)]

    def shifted(value, by):
        return lax.ppermute(value, "lon", [(i, (i + by) % lons) for i in range(lons)])

    edge = jnp.where(lat == 0, state_field[rows - HALO :], state_field[:HALO])
    edge = lax.ppermute(edge, "lat", swap)

    low_rows, band_rows = geo.low[1][1], geo.band[1][1]
    tl = analysis_matrix(LOW, geo.low[1][0], 112, 0 - LEAD - HALO, 256)
    th = analysis_matrix(HIGH, geo.band[1][0], 120, 96 - LEAD - HALO, 256)
    w1 = geo.low_cells[1][1] * LANES
    g1, d1, send_e, send_o = call(
        functools.partial(first_level_kernel, geo, lats),
        (
            shape((low_rows, w1)),
            shape((3, band_rows, geo.band_cells[1][1] * LANES)),
            shape((band_rows, 6 * LANES), BF16),
            shape((band_rows, 6 * LANES), BF16),
        ),
        [
            pltpu.VMEM((geo.extended, width), BF16),
            pltpu.VMEM((low_rows, width), F32),
            pltpu.VMEM((band_rows, width), F32),
        ],
        place,
        state_field,
        edge,
        jnp.asarray(tl),
        jnp.asarray(th),
        gains[:3],
    )
    e1 = lax.ppermute(send_e, "lon", even_pairs)
    o1 = lax.ppermute(send_o, "lon", odd_pairs)

    mats = []
    for level in (2, 3, 4):
        in_start, in_rows = geo.low[level - 1]
        mats.append(analysis_matrix(LOW, *geo.low[level], in_start, in_rows))
        mats.append(analysis_matrix(HIGH, *geo.band[level], in_start, in_rows))
    scratch = [
        pltpu.VMEM((geo.low[level][1], geo.low_cells[level][1] * LANES), F32) for level in (2, 3)
    ]
    for level in (2, 3, 4):
        w = geo.low_cells[level - 1][1] * LANES
        scratch += [pltpu.VMEM((geo.low[level][1], w), F32), pltpu.VMEM((geo.band[level][1], w), F32)]
    deep = call(
        functools.partial(deep_kernel, geo, lats),
        tuple(
            shape((3, geo.band[level][1], geo.band_cells[level][1] * LANES)) for level in (2, 3, 4)
        )
        + (shape((geo.low[4][1], geo.low_cells[4][1] * LANES)),)
        + tuple(shape(plan_shape(geo, d), BF16) for d in (1, 1, 2, 2, 3, 3)),
        scratch,
        place,
        g1,
        *[jnp.asarray(m) for m in mats],
        gains[3:],
    )
    d2, d3, d4, ll4, deep_e, deep_o, p2, m2, p3, m3 = deep

    merged, size = ll4, 1
    while size < lons:
        other = lax.ppermute(merged, "lon", [(i, i ^ size) for i in range(lons)])
        lower_half = (lon // size) % 2 == 0
        lower = jnp.where(lower_half, merged, other)
        upper = jnp.where(lower_half, other, merged)
        wide = geo.cells[4] * C * size
        merged = jnp.pad(lower, ((0, 0), (0, wide))) + jnp.pad(upper, ((0, 0), (wide, 0)))
        size *= 2
    around = geo.cells[4] * lons * C
    w = 4 * C
    core = merged[:, w : w + around]
    grid4 = jnp.concatenate(
        [
            core[:, :w] + merged[:, w + around :],
            core[:, w : around - w],
            core[:, around - w :] + merged[:, :w],
        ],
        1,
    )
    skip = -geo.low[4][0]
    tokens = grid4[skip : skip + geo.rows[4]].astype(BF16)
    others = lax.ppermute(tokens, "lat", swap)
    keys = jnp.concatenate([tokens, others], 0).reshape(-1, C)

    e2 = lax.ppermute(deep_e, "lon", even_pairs)
    o2 = lax.ppermute(deep_o, "lon", odd_pairs)
    from_m2, from_p2 = shifted(p2, 2), shifted(m2, -2)
    from_m3, from_p3 = shifted(p3, 3), shifted(m3, -3)

    ring = jnp.concatenate([grid4[:, around - w :], grid4, grid4[:, :w]], 1)
    own = lax.dynamic_slice(
        ring,
        (0, lon * geo.cells[4] * C + C),
        (geo.low[4][1], geo.band_cells[4][1] * LANES),
    )
    blocks = max(1, keys.shape[0] // 928) if keys.shape[0] % 928 == 0 else 1
    coarse = call(
        functools.partial(attention_kernel, geo, lats, blocks),
        shape(own.shape),
        [],
        place,
        keys,
        own,
        embed_weight,
        qkv_weight,
        head_scale,
        out_weight,
        norm_gain[None],
        back_weight,
        cost=200_000_000,
    )

    synth = []
    for level in (4, 3, 2):
        for taps in (LOW, HIGH):
            synth.append(synthesis_matrix(taps, *geo.band[level - 1], *geo.band[level]))
    half = rows // 2
    for block in range(2):
        begin = geo.band[1][0] + (0 if block == 0 else band_rows - LANES)
        synth.append(
            np.concatenate(
                [synthesis_matrix(taps, half * block, half, begin, LANES) for taps in (LOW, HIGH)], 1
            )
        )
    y_width = geo.band_cells[1][1] * LANES
    return call(
        functools.partial(synthesis_kernel, geo, lats),
        shape((rows, width), BF16),
        [pltpu.VMEM((geo.band[level][1], geo.band_cells[level][1] * LANES), F32) for level in (3, 2, 1)]
        + [
            pltpu.VMEM((3, 2, band_rows, 2 * LANES), F32),
            pltpu.VMEM((2 * LANES, y_width), BF16),
            pltpu.VMEM((2 * LANES, y_width), BF16),
            pltpu.VMEM((rows, y_width), F32),
            pltpu.VMEM((rows, y_width), F32),
        ],
        place,
        coarse,
        d1,
        d2,
        d3,
        d4,
        e1,
        o1,
        e2,
        o2,
        from_m2,
        from_p2,
        from_m3,
        from_p3,
        *[jnp.asarray(m) for m in synth],
    )


def solution(mesh):
    in_specs = (P("lat", ("member", "lon")), P(), P(), P(), P(), P(), P(), P())
    out_specs = P("lat", ("member", "lon"))
    return jax.shard_map(
        functools.partial(per_device, dict(mesh.shape)),
        mesh=mesh,
        in_specs=in_specs,
        out_specs=out_specs,
        check_vma=False,
    )
```

```python
import functools
import math

import jax
import jax.numpy as jnp
import numpy as np
from jax import lax
from jax.experimental import pallas as pl
from jax.experimental.pallas import tpu as pltpu
from jax.sharding import PartitionSpec as P


C = 64
HEADS = 8
HEAD_DIM = 32
E = 256
LANES = 128
HALO = 96
LEAD = 16

LOW = np.array(
    [
        -0.010597401784997278,
        0.032883011666982945,
        0.030841381835986965,
        -0.18703481171888114,
        -0.02798376941698385,
        0.6308807679295904,
        0.7148465705525415,
        0.23037781330885523,
    ]
)
HIGH = np.array([(-1.0) ** j * LOW[7 - j] for j in range(8)])


def lattice_factors():
    a = np.array([(LOW[2 * (3 - j)], LOW[2 * (3 - j) + 1]) for j in range(4)])
    b = np.array([(HIGH[2 * (3 - j)], HIGH[2 * (3 - j) + 1]) for j in range(4)])
    factors = {}
    for s in (3, 2, 1):
        k = (a[s] @ b[s]) / (b[s] @ b[s])
        a, b = (a - k * b) / (1 + k * k), (k * a + b) / (1 + k * k)
        a, b = a[:s], b[1 : s + 1]
        factors[s] = float(k)
    factors[0] = float(a[0][1] / a[0][0])
    return factors, float(a[0][0]), float(np.sign(b[0][1] / a[0][0]))


TURN, SCALE, SIGN = lattice_factors()
F32 = jnp.float32
BF16 = jnp.bfloat16


def analysis_matrix(taps, out_start, out_rows, in_start, in_rows):
    m = np.zeros((out_rows, in_rows), np.float32)
    for j in range(out_rows):
        for t in range(8):
            r = 2 * (out_start + j) - 3 + t - in_start
            if 0 <= r < in_rows:
                m[j, r] = taps[t]
    return m


def synthesis_matrix(taps, out_start, out_rows, in_start, in_rows):
    m = np.zeros((out_rows, in_rows), np.float32)
    for j in range(out_rows):
        for r in range(in_rows):
            t = out_start + j - 2 * (in_start + r) + 3
            if 0 <= t < 8:
                m[j, r] = taps[t]
    return m


def two_terms(value):
    top = value.astype(BF16)
    return top, (value - top.astype(F32)).astype(BF16)


def masked_rows(matrix, start, count, lat, lats):
    row = lax.broadcasted_iota(jnp.int32, matrix.shape, 0) + (start + lat * count)
    return jnp.where((row >= 0) & (row < count * lats), matrix, 0.0)


def mxu(a, b):
    return jnp.dot(a, b, preferred_element_type=F32)


def dot3(matrix, vh, vl):
    mh, ml = two_terms(matrix)
    return mxu(mh, vh) + mxu(mh, vl) + mxu(ml, vh)


def first_half(rows):
    return lax.broadcasted_iota(jnp.int32, (rows, LANES), 1) < C


def half_turn(value):
    return None if value is None else pltpu.roll(value, C, 1)


def pick(left, a, b):
    if a is None and b is None:
        return None
    return jnp.where(left, 0.0 if a is None else a, 0.0 if b is None else b)


def plus(a, b, factor):
    if b is None:
        return a
    if a is None:
        return b * factor
    return a + b * factor


class Memo:
    def __init__(self, make):
        self.make, self.known = make, {}

    def __call__(self, n):
        if n not in self.known:
            self.known[n] = self.make(n)
        return self.known[n]


def analysis(cols, start, left):
    turned = Memo(lambda i: half_turn(cols[i]) if 0 <= i < len(cols) else None)
    plain = lambda i: cols[i] if 0 <= i < len(cols) else None
    if start % 2 == 0:
        at = lambda n: n - 1 - start // 2
        u = Memo(lambda n: pick(left, turned(at(n) - 1), plain(at(n))))
        w = Memo(lambda n: pick(left, plain(at(n)), turned(at(n) + 1)))
    else:
        at = lambda n: n - (start + 3) // 2
        u = Memo(lambda n: pick(left, plain(at(n)), turned(at(n) + 1)))
        w = Memo(lambda n: pick(left, turned(at(n)), plain(at(n) + 1)))
    a = Memo(lambda n: plus(u(n), w(n), TURN[0]))
    if SIGN < 0:
        minus = lambda v: None if v is None else -v
        b = Memo(lambda n: plus(minus(w(n)), u(n), TURN[0]))
    else:
        b = Memo(lambda n: plus(w(n), u(n), -TURN[0]))

    def stage(a, b, factor):
        rolled = Memo(lambda n: half_turn(b(n)))
        late = Memo(lambda n: pick(left, rolled(n - 2), rolled(n)))
        return (
            Memo(lambda n: plus(a(n), late(n), factor)),
            Memo(lambda n: plus(late(n), a(n), -factor)),
        )

    for s in (1, 2, 3):
        a, b = stage(a, b, TURN[s])
    return (lambda k: a(k + 3)), (lambda k: b(k + 3))


def synthesis(lows, highs, start, left):
    def cells(cols):
        return lambda n: cols[(n - 3 - start) // 2] if 0 <= n - 3 - start < 2 * len(cols) else None

    a, b = cells(lows), cells(highs)

    def stage(a, b, factor):
        early = Memo(lambda n: half_turn(plus(b(n), a(n), factor)))
        return (
            Memo(lambda n: plus(a(n), b(n), -factor)),
            Memo(lambda n: pick(left, early(n), early(n + 2))),
        )

    for s in (3, 2, 1):
        a, b = stage(a, b, TURN[s])
    last_a, last_b = a, b
    u = Memo(lambda n: plus(last_a(n), last_b(n), -TURN[0] * SIGN))
    if SIGN < 0:
        w = Memo(lambda n: plus(last_a(n) * TURN[0] if last_a(n) is not None else None, last_b(n), -1.0))
    else:
        w = Memo(lambda n: plus(last_b(n), last_a(n), TURN[0]))
    u_turned, w_turned = Memo(lambda n: half_turn(u(n))), Memo(lambda n: half_turn(w(n)))
    parity = (start + 3) % 2

    def pair(m):
        if m % 2:
            n = (m + 3) // 2
            if n % 2 == parity:
                return pick(left, u(n), w_turned(n))
            return pick(left, u_turned(n - 1), w(n - 1))
        n = m // 2 + 1
        if n % 2 == parity:
            return pick(left, w(n), u(n))
        return pick(left, w_turned(n - 1), u_turned(n + 1))

    return pair


def columns(ref, row, rows, count=None):
    count = ref.shape[-1] // LANES if count is None else count
    return [ref[pl.ds(row, rows), pl.ds(LANES * p, LANES)] for p in range(count)]


def put(ref, row, p, value, lead=()):
    ref[lead + (pl.ds(row, value.shape[0]), pl.ds(LANES * p, LANES))] = value


class Geometry:
    def __init__(self, rows, cells):
        self.rows = [rows >> level for level in range(5)]
        self.cells = [cells >> level for level in range(5)]
        up = lambda value, step: -(-value // step) * step
        self.band = [
            None,
            (-4, up(self.rows[1] + 4, 120)),
            (-8, up(self.rows[2] + 11, 16)),
            (-3, up(self.rows[3] + 6, 8)),
            (-3, up(self.rows[4] + 6, 8)),
        ]
        self.low = [
            None,
            (-52, up(self.rows[1] + 97, 112)),
            (-24, up(self.rows[2] + 45, 88)),
            (-11, up(self.rows[3] + 20, 8)),
            (-3, up(self.rows[4] + 6, 8)),
        ]
        self.span = [None, (-2, self.cells[1] // 2 + 2)]
        for level in (2, 3, 4):
            self.span.append((-3, self.cells[level] // 2 + 3))
        self.extended = max(
            LEAD + 2 * HALO + rows, 2 * (self.low[1][1] - 112) + 256
        )


STEP = 8


def levels_loop(geo, level, lo, hi, source_start, gain, target, bands, extra):
    left = first_half(STEP)
    first, pairs = geo.span[level]
    low_start, low_rows = geo.low[level]
    band_start, band_rows = geo.band[level]
    skip = (band_start - low_start) // STEP
    if extra:
        def lows(c, carry):
            row = pl.multiple_of(c * STEP, STEP)
            low, _ = analysis(columns(lo, row, STEP), source_start, left)
            for q in range(pairs):
                put(target, row, q, low(first + 2 * q))
            return carry

        lax.fori_loop(0, skip, lows, 0)
        lax.fori_loop(skip + band_rows // STEP, low_rows // STEP, lows, 0)

    def both(c, carry):
        row = pl.multiple_of(c * STEP, STEP)
        g = [jnp.broadcast_to(gain[b : b + 1, :], (STEP, LANES)) for b in range(3)]
        low, high = analysis(columns(lo, row + skip * STEP, STEP), source_start, left)
        for q in range(pairs):
            put(target, row + skip * STEP, q, low(first + 2 * q))
            put(bands, row, q, high(first + 2 * q) * g[0], (0,))
        low, high = analysis(columns(hi, row, STEP), source_start, left)
        for q in range(pairs):
            put(bands, row, q, low(first + 2 * q) * g[1], (1,))
            put(bands, row, q, high(first + 2 * q) * g[2], (2,))
        return carry

    lax.fori_loop(0, band_rows // STEP, both, 0)


def first_level_kernel(geo, lats, place, edge, tl, th, gain, x, g1, d1, send_e, send_o, ext, la, ha, sems):
    lat, parity = place[0], place[1]
    rows = geo.rows[0]
    low_start, low_rows = geo.low[1]
    band_start, band_rows = geo.band[1]
    width = x.shape[1]
    begin = LEAD + HALO
    cuts = [0] + [min(rows, 224 * b + 256 - begin) for b in range(low_rows // 112 - 1)] + [rows]
    copies = []
    for i in range(len(cuts) - 1):
        part = pl.ds(cuts[i], cuts[i + 1] - cuts[i])
        to = pl.ds(begin + cuts[i], cuts[i + 1] - cuts[i])
        copies.append(pltpu.make_async_copy(x.at[part, :], ext.at[to, :], sems.at[i]))
        copies[-1].start()
    top = slice(LEAD, begin)
    bottom = slice(begin + rows, begin + rows + HALO)
    ext[0:LEAD, :] = jnp.zeros((LEAD, width), BF16)
    tail = geo.extended - (LEAD + 2 * HALO + rows)
    if tail:
        ext[geo.extended - tail :, :] = jnp.zeros((tail, width), BF16)

    @pl.when(lat == 0)
    def _():
        ext[top, :] = jnp.zeros((HALO, width), BF16)
        ext[bottom, :] = edge[...]

    @pl.when(lat != 0)
    def _():
        ext[top, :] = edge[...]
        ext[bottom, :] = jnp.zeros((HALO, width), BF16)

    for b in range(low_rows // 112):
        copies[b].wait()
        mh, ml = two_terms(masked_rows(tl[...], low_start + 112 * b, geo.rows[1], lat, lats))
        data = ext[224 * b : 224 * b + 256, :]
        la[112 * b : 112 * b + 112, :] = mxu(mh, data) + mxu(ml, data)
    for b in range(band_rows // 120):
        mh, ml = two_terms(masked_rows(th[...], band_start + 120 * b, geo.rows[1], lat, lats))
        data = ext[96 + 240 * b : 352 + 240 * b, :]
        ha[120 * b : 120 * b + 120, :] = mxu(mh, data) + mxu(ml, data)

    levels_loop(geo, 1, la, ha, 0, gain, g1, d1, True)
    edge_lanes = 2 * LANES
    shift = (geo.cells[1] // 2) * LANES

    def fill(to_left, to_right):
        for b in range(3):
            at = slice(b * edge_lanes, (b + 1) * edge_lanes)
            to_left[:, at] = d1[b, :, 0:edge_lanes].astype(BF16)
            to_right[:, at] = d1[b, :, shift : shift + edge_lanes].astype(BF16)

    @pl.when(parity == 0)
    def _():
        fill(send_o, send_e)

    @pl.when(parity != 0)
    def _():
        fill(send_e, send_o)


def deep_blocks(geo):
    in_rows = geo.low[1][1]
    lows, highs = [], []
    for b in range(geo.low[2][1] // 88):
        lows.append((88 * b, 88, min(176 * b, in_rows - 192), 192))
    half = geo.band[2][1] // 2
    for b in range(2):
        first = 2 * (geo.band[2][0] + half * b) - 3 - geo.low[1][0]
        highs.append((half * b, half, first // 16 * 16, 2 * half + 16))
    return lows, highs


def deep_kernel(geo, lats, mat_count, place, gain, g1, *refs):
    lat, parity = place[0], place[1]
    mats, refs = list(refs[:mat_count]), refs[mat_count:]
    d = {2: refs[0], 3: refs[1], 4: refs[2]}
    ll4, send_e, send_o, p2, m2, p3, m3 = refs[3:10]
    g2, g3, lo2, hi2, lo3, hi3, lo4, hi4, gh, gl = refs[10:]
    lo, hi = {2: lo2, 3: lo3, 4: lo4}, {2: hi2, 3: hi3, 4: hi4}
    grids = {1: g1, 2: g2, 3: g3, 4: ll4}
    gh[...], gl[...] = two_terms(g1[...])
    for starts, blocks, out in zip((geo.low[2][0], geo.band[2][0]), deep_blocks(geo), (lo2, hi2)):
        for at, count, begin, size in blocks:
            matrix = masked_rows(mats.pop(0)[...], starts + at, geo.rows[2], lat, lats)
            window = slice(begin, begin + size)
            out[at : at + count, :] = dot3(matrix, gh[window, :], gl[window, :])
    for level in (2, 3, 4):
        if level > 2:
            vh, vl = two_terms(grids[level - 1][...])
            for starts, out in ((geo.low[level][0], lo[level]), (geo.band[level][0], hi[level])):
                matrix = masked_rows(mats.pop(0)[...], starts, geo.rows[level], lat, lats)
                out[...] = dot3(matrix, vh, vl)
        start = geo.span[level - 1][0]
        rows = gain[3 * (level - 2) : 3 * (level - 2) + 3, :]
        levels_loop(geo, level, lo[level], hi[level], start, rows, grids[level], d[level], level < 4)

    def fill(distance, to_left, to_right):
        for level, count, row in exchange_plan(geo)[distance]:
            n = geo.band[level][1]
            move = distance * geo.cells[level] // 2
            for b in range(3):
                lanes = slice(b * count * LANES, (b + 1) * count * LANES)
                to_left[row : row + n, lanes] = d[level][b, :, 0 : count * LANES].astype(BF16)
                to_right[row : row + n, lanes] = d[level][
                    b, :, move * LANES : (move + count) * LANES
                ].astype(BF16)

    @pl.when(parity == 0)
    def _():
        fill(1, send_o, send_e)

    @pl.when(parity != 0)
    def _():
        fill(1, send_e, send_o)

    fill(2, m2, p2)
    fill(3, m3, p3)


def exchange_plan(geo):
    plan = {}
    for distance in (1, 2, 3):
        entries, row = [], 0
        for level in (2, 3, 4):
            count = geo.span[level][1] - distance * geo.cells[level] // 2
            if count > 0:
                entries.append((level, count, row))
                row += -(-geo.band[level][1] // 16) * 16
        plan[distance] = entries
    return plan


def plan_shape(geo, distance):
    entries = exchange_plan(geo)[distance]
    rows = sum(-(-geo.band[level][1] // 16) * 16 for level, _, _ in entries)
    return (rows, max(count for _, count, _ in entries) * 3 * LANES)


def attention_kernel(geo, lats, blocks, place, keys, grid, we, wqkv, scale, wo, gain, wb, out):
    lat = place[0]
    rows, width = grid.shape
    cells = width // C
    field = grid[...]
    own = jnp.concatenate([field[:, C * c : C * (c + 1)] for c in range(cells)], 0)
    count = own.shape[0]
    embedded = mxu(own.astype(BF16), we[...])
    queries = mxu(embedded.astype(BF16), wqkv[:, 0:E]).astype(BF16)
    lane = lax.broadcasted_iota(jnp.int32, (1, E), 1)
    block = keys.shape[0] // blocks
    factor = [scale[h] * (1.0 / math.sqrt(HEAD_DIM)) for h in range(HEADS)]

    def keyvals(start):
        spread = mxu(keys[pl.ds(start, block), :], we[...]).astype(BF16)
        both = mxu(spread, wqkv[:, E : 3 * E]).astype(BF16)
        return both[:, 0:E], both[:, E : 2 * E]

    def scores_of(h, k):
        mine = (lane >= h * HEAD_DIM) & (lane < (h + 1) * HEAD_DIM)
        q = jnp.where(mine, queries, jnp.zeros_like(queries))
        s = lax.dot_general(q, k, (((1,), (1,)), ((), ())), preferred_element_type=F32)
        return s * factor[h]

    def masked(h, value):
        mine = (lane >= h * HEAD_DIM) & (lane < (h + 1) * HEAD_DIM)
        return jnp.where(mine, value, jnp.zeros_like(value))

    if blocks == 1:
        k, v = keyvals(0)
        attended = jnp.zeros((count, E), F32)
        for h in range(HEADS):
            s = scores_of(h, k)
            w = jnp.exp(s - jnp.max(s, -1, keepdims=True))
            total = jnp.sum(w, -1, keepdims=True)
            attended = attended + masked(h, mxu(w.astype(BF16), v) / total)
    else:

        def one_block(b, carry):
            peaks, totals, sums = carry
            k, v = keyvals(pl.multiple_of(b * block, 16))
            new_peaks, new_totals = [], []
            shrunk = jnp.zeros((count, E), F32)
            for h in range(HEADS):
                s = scores_of(h, k)
                peak = jnp.maximum(peaks[h], jnp.max(s, -1, keepdims=True))
                shrink = jnp.exp(peaks[h] - peak)
                w = jnp.exp(s - peak)
                new_peaks.append(peak)
                new_totals.append(totals[h] * shrink + jnp.sum(w, -1, keepdims=True))
                shrunk = shrunk + masked(h, sums * shrink + mxu(w.astype(BF16), v))
            return tuple(new_peaks), tuple(new_totals), shrunk

        start = (
            tuple(jnp.full((count, 1), -1e30, F32) for _ in range(HEADS)),
            tuple(jnp.zeros((count, 1), F32) for _ in range(HEADS)),
            jnp.zeros((count, E), F32),
        )
        _, totals, sums = lax.fori_loop(0, blocks, one_block, start)
        attended = jnp.zeros((count, E), F32)
        for h in range(HEADS):
            attended = attended + masked(h, sums / totals[h])
    hidden = embedded + mxu(attended.astype(BF16), wo[...])
    square = jnp.mean(hidden * hidden, -1, keepdims=True)
    normed = (hidden * lax.rsqrt(square + 1e-06) * gain[...]).astype(BF16)
    update = mxu(normed, wb[...])
    back = [
        jnp.concatenate(
            [update[rows * c : rows * (c + 1), :], update[rows * (c + 1) : rows * (c + 2), :]], 1
        )
        for c in range(0, cells, 2)
    ]
    start = geo.band[4][0]
    for q, value in enumerate(back):
        at = slice(q * LANES, (q + 1) * LANES)
        out[:, at] = masked_rows(field[:, at] + value, start, geo.rows[4], lat, lats)


def synthesis_kernel(geo, lats, place, coarse, d1, d2, d3, d4, *refs):
    lat, parity = place[0], place[1]
    e1, o1, e2, o2, from_m2, from_p2, from_m3, from_p3 = refs[:8]
    mats, refs = refs[8:13], refs[13:]
    out, up3, up2, up1, sides, xh, xl, ylow, yhigh, done, sems = refs
    bands = {2: d2, 3: d3, 4: d4}
    plan = exchange_plan(geo)

    def from_sides(level, b):
        n = geo.band[level][1]
        cols = [bands[level][b, :, LANES * p : LANES * (p + 1)] for p in range(geo.span[level][1])]
        for distance in (1, 2, 3):
            for which, count, row in plan[distance]:
                if which != level:
                    continue
                move = distance * geo.cells[level] // 2
                for p in range(count):
                    lanes = slice((b * count + p) * LANES, (b * count + p + 1) * LANES)
                    if distance == 1:
                        even = e2[row : row + n, lanes].astype(F32)
                        odd = o2[row : row + n, lanes].astype(F32)
                        low = jnp.where(parity == 0, odd, even)
                        high = jnp.where(parity == 0, even, odd)
                    else:
                        lows, highs = {2: (from_m2, from_p2), 3: (from_m3, from_p3)}[distance]
                        low = lows[row : row + n, lanes].astype(F32)
                        high = highs[row : row + n, lanes].astype(F32)
                    cols[p] = cols[p] + low
                    cols[p + move] = cols[p + move] + high
        return jnp.concatenate(cols, 1)

    uppers = {4: coarse, 3: up3, 2: up2, 1: up1}
    left = first_half(STEP)
    for level in (4, 3, 2):
        begin, pairs = geo.span[level]
        below = level - 1
        start, rows = geo.band[below]
        matrix = masked_rows(mats[4 - level][...], start, geo.rows[below], lat, lats)
        width = pairs * LANES
        for one, two, y in (
            (uppers[level][...], from_sides(level, 1), ylow),
            (from_sides(level, 0), from_sides(level, 2), yhigh),
        ):
            h, l = two_terms(jnp.concatenate([one, two], 0))
            y[0:rows, 0:width] = dot3(matrix, h, l)
        target = uppers[below]
        first, out_pairs = geo.span[below]

        def joined(c, carry):
            row = pl.multiple_of(c * STEP, STEP)
            pair = synthesis(
                columns(ylow, row, STEP, pairs), columns(yhigh, row, STEP, pairs), begin, left
            )
            for q in range(out_pairs):
                put(target, row, q, pair(first + 2 * q))
            return carry

        lax.fori_loop(0, rows // STEP, joined, 0)

    n = geo.band[1][1]
    edge = 2 * LANES
    shift = (geo.cells[1] // 2) * LANES
    for b in range(3):
        at = slice(b * edge, (b + 1) * edge)
        even, odd = e1[:, at].astype(F32), o1[:, at].astype(F32)
        sides[b, 0] = jnp.where(parity == 0, odd, even)
        sides[b, 1] = jnp.where(parity == 0, even, odd)
    half = geo.rows[0] // 2
    for block in range(2):
        w = 0 if block == 0 else n - LANES
        window = slice(w, w + LANES)
        sh, sl = two_terms(mats[3 + block][...])
        for pieces, y in (((None, 1), ylow), ((0, 2), yhigh)):
            for i, b in enumerate(pieces):
                place_rows = slice(i * LANES, (i + 1) * LANES)
                if b is None:
                    h, l = two_terms(up1[window, :])
                    xh[place_rows, :], xl[place_rows, :] = h, l
                else:
                    for lanes, extra in (
                        (slice(0, edge), sides[b, 0, window, :]),
                        (slice(edge, shift), None),
                        (slice(shift, shift + edge), sides[b, 1, window, :]),
                    ):
                        value = d1[b, window, lanes]
                        h, l = two_terms(value if extra is None else value + extra)
                        xh[place_rows, lanes], xl[place_rows, lanes] = h, l
            y[half * block : half * (block + 1), :] = (
                mxu(sh, xh[...]) + mxu(sh, xl[...]) + mxu(sl, xh[...])
            )
    rows16 = 16
    left16 = first_half(rows16)
    begin, pairs = geo.span[1]

    def last(c, carry):
        row = pl.multiple_of(c * rows16, rows16)
        pair = synthesis(columns(ylow, row, rows16), columns(yhigh, row, rows16), begin, left16)
        for q in range(geo.cells[0] // 2):
            put(done, row, q, pair(2 * q).astype(BF16))
        return carry

    chunks = geo.rows[0] // rows16
    cuts = [chunks * i // 4 for i in range(5)]
    copies = []
    for i in range(4):
        lax.fori_loop(cuts[i], cuts[i + 1], last, 0)
        part = pl.ds(cuts[i] * rows16, (cuts[i + 1] - cuts[i]) * rows16)
        copies.append(pltpu.make_async_copy(done.at[part, :], out.at[part, :], sems.at[i]))
        copies[-1].start()
    for copy in copies:
        copy.wait()


def call(kernel, out_shape, scratch, *args, cost=20_000_000, grant=24, raw=0, raw_out=False):
    vmem = pl.BlockSpec(memory_space=pltpu.VMEM)
    smem = pl.BlockSpec(memory_space=pltpu.SMEM)
    anywhere = pl.BlockSpec(memory_space=pl.ANY)
    specs = [smem if a.ndim == 1 and a.size < 16 else vmem for a in args]
    if raw:
        specs[-raw:] = [anywhere] * raw
    outs = jax.tree.map(lambda _: anywhere if raw_out else vmem, out_shape)
    return pl.pallas_call(
        kernel,
        out_shape=out_shape,
        in_specs=specs,
        out_specs=outs,
        scratch_shapes=scratch,
        compiler_params=pltpu.CompilerParams(vmem_limit_bytes=grant << 20),
        cost_estimate=pl.CostEstimate(flops=cost, bytes_accessed=1 << 20, transcendentals=0),
    )(*args)


def shape(dims, dtype=F32):
    return pltpu.VMEM(dims, dtype)


def constant(matrix):
    return jnp.asarray(matrix)


def per_device(mesh_shape, state_field, skip_gain, embed_weight, qkv_weight, head_scale, out_weight, norm_gain, back_weight):
    return program(
        mesh_shape, state_field, skip_gain, embed_weight, qkv_weight, head_scale, out_weight, norm_gain, back_weight
    )


def program(mesh_shape, state_field, skip_gain, embed_weight, qkv_weight, head_scale, out_weight, norm_gain, back_weight):
    lons, lats = mesh_shape["lon"], mesh_shape["lat"]
    rows, width = state_field.shape
    geo = Geometry(rows, width // C)
    lat, lon = lax.axis_index("lat"), lax.axis_index("lon")
    place = jnp.stack([lat, lon % 2]).astype(jnp.int32)
    gains = jnp.concatenate([skip_gain, skip_gain], 2).reshape(-1, LANES)

    even_pairs = [(i, i ^ 1) for i in range(lons)]
    odd_pairs = [(i, (i + 1 if i % 2 else i - 1) % lons) for i in range(lons)]
    swap = [(i, lats - 1 - i) for i in range(lats)]

    def shifted(value, by):
        return lax.ppermute(value, "lon", [(i, (i + by) % lons) for i in range(lons)])

    edge = jnp.where(lat == 0, state_field[rows - HALO :], state_field[:HALO])
    edge = lax.ppermute(edge, "lat", swap)

    low_rows, band_rows = geo.low[1][1], geo.band[1][1]
    tl = SCALE * analysis_matrix(LOW, geo.low[1][0], 112, 0 - LEAD - HALO, 256)
    th = SCALE * analysis_matrix(HIGH, geo.band[1][0], 120, 96 - LEAD - HALO, 256)
    w1 = geo.span[1][1] * LANES
    g1, d1, send_e, send_o = call(
        functools.partial(first_level_kernel, geo, lats),
        (
            shape((low_rows, w1)),
            shape((3, band_rows, w1)),
            shape((band_rows, 6 * LANES), BF16),
            shape((band_rows, 6 * LANES), BF16),
        ),
        [
            pltpu.VMEM((geo.extended, width), BF16),
            pltpu.VMEM((low_rows, width), F32),
            pltpu.VMEM((band_rows, width), F32),
            pltpu.SemaphoreType.DMA((low_rows // 112,)),
        ],
        place,
        edge,
        constant(tl),
        constant(th),
        gains[:3],
        state_field,
        raw=1,
    )
    e1 = lax.ppermute(send_e, "lon", even_pairs)
    o1 = lax.ppermute(send_o, "lon", odd_pairs)

    mats = []
    for taps, start, blocks in zip((LOW, HIGH), (geo.low[2][0], geo.band[2][0]), deep_blocks(geo)):
        for at, count, begin, size in blocks:
            mats.append(analysis_matrix(taps, start + at, count, geo.low[1][0] + begin, size))
    for level in (3, 4):
        in_start, in_rows = geo.low[level - 1]
        mats.append(analysis_matrix(LOW, *geo.low[level], in_start, in_rows))
        mats.append(analysis_matrix(HIGH, *geo.band[level], in_start, in_rows))
    scratch = [pltpu.VMEM((geo.low[level][1], geo.span[level][1] * LANES), F32) for level in (2, 3)]
    for level in (2, 3, 4):
        w = geo.span[level - 1][1] * LANES
        scratch += [pltpu.VMEM((geo.low[level][1], w), F32), pltpu.VMEM((geo.band[level][1], w), F32)]
    scratch += [pltpu.VMEM((low_rows, w1), BF16), pltpu.VMEM((low_rows, w1), BF16)]
    deep = call(
        functools.partial(deep_kernel, geo, lats, len(mats)),
        tuple(shape((3, geo.band[level][1], geo.span[level][1] * LANES)) for level in (2, 3, 4))
        + (shape((geo.low[4][1], geo.span[4][1] * LANES)),)
        + tuple(shape(plan_shape(geo, d), BF16) for d in (1, 1, 2, 2, 3, 3)),
        scratch,
        place,
        gains[3:],
        g1,
        *[constant(SCALE * m) for m in mats],
    )
    d2, d3, d4, ll4, deep_e, deep_o, p2, m2, p3, m3 = deep

    merged, size = ll4, 1
    while size < lons:
        other = lax.ppermute(merged, "lon", [(i, i ^ size) for i in range(lons)])
        lower_half = (lon // size) % 2 == 0
        lower = jnp.where(lower_half, merged, other)
        upper = jnp.where(lower_half, other, merged)
        wide = geo.cells[4] * C * size
        merged = jnp.pad(lower, ((0, 0), (0, wide))) + jnp.pad(upper, ((0, 0), (wide, 0)))
        size = 2 * size
    around = geo.cells[4] * lons * C
    w = 6 * C
    ring = jnp.concatenate([merged[:, :w] + merged[:, around:], merged[:, w:around]], 1)
    skip = -geo.low[4][0]
    tokens = ring[skip : skip + geo.rows[4]].astype(BF16)
    others = lax.ppermute(tokens, "lat", swap)
    keys = jnp.concatenate([tokens, others], 0).reshape(-1, C)

    e2 = lax.ppermute(deep_e, "lon", even_pairs)
    o2 = lax.ppermute(deep_o, "lon", odd_pairs)
    from_m2, from_p2 = shifted(p2, 2), shifted(m2, -2)
    from_m3, from_p3 = shifted(p3, 3), shifted(m3, -3)

    own = lax.dynamic_slice(
        jnp.concatenate([ring, ring[:, :w]], 1),
        (0, lon * geo.cells[4] * C),
        (geo.low[4][1], geo.span[4][1] * LANES),
    )
    blocks = max(1, keys.shape[0] // 928) if keys.shape[0] % 928 == 0 else 1
    coarse = call(
        functools.partial(attention_kernel, geo, lats, blocks),
        shape(own.shape),
        [],
        place,
        keys,
        own,
        embed_weight,
        qkv_weight,
        head_scale,
        out_weight,
        norm_gain[None],
        back_weight,
        cost=200_000_000,
    )

    synth = []
    for level in (4, 3, 2):
        synth.append(
            np.concatenate(
                [synthesis_matrix(t, *geo.band[level - 1], *geo.band[level]) for t in (LOW, HIGH)], 1
            )
        )
    half = rows // 2
    for block in range(2):
        begin = geo.band[1][0] + (0 if block == 0 else band_rows - LANES)
        synth.append(
            np.concatenate(
                [synthesis_matrix(t, half * block, half, begin, LANES) for t in (LOW, HIGH)], 1
            )
        )
    return call(
        functools.partial(synthesis_kernel, geo, lats),
        jax.ShapeDtypeStruct((rows, width), BF16),
        [pltpu.VMEM((geo.band[level][1], geo.span[level][1] * LANES), F32) for level in (3, 2, 1)]
        + [
            pltpu.VMEM((3, 2, band_rows, 2 * LANES), F32),
            pltpu.VMEM((2 * LANES, w1), BF16),
            pltpu.VMEM((2 * LANES, w1), BF16),
            pltpu.VMEM((rows, w1), F32),
            pltpu.VMEM((rows, w1), F32),
            pltpu.VMEM((rows, width), BF16),
            pltpu.SemaphoreType.DMA((4,)),
        ],
        place,
        coarse,
        d1,
        d2,
        d3,
        d4,
        e1,
        o1,
        e2,
        o2,
        from_m2,
        from_p2,
        from_m3,
        from_p3,
        *[constant(SCALE * m) for m in synth],
        raw_out=True,
    )


def solution(mesh):
    in_specs = (P("lat", ("member", "lon")), P(), P(), P(), P(), P(), P(), P())
    out_specs = P("lat", ("member", "lon"))
    return jax.shard_map(
        functools.partial(per_device, dict(mesh.shape)),
        mesh=mesh,
        in_specs=in_specs,
        out_specs=out_specs,
        check_vma=False,
    )
```

```python
import functools
import math

import jax
import jax.numpy as jnp
import numpy as np
from jax import lax
from jax.experimental import pallas as pl
from jax.experimental.pallas import tpu as pltpu
from jax.sharding import PartitionSpec as P


C = 64
HEADS = 8
HEAD_DIM = 32
E = 256
LANES = 128
HALO = 96
LEAD = 16

LOW = np.array(
    [
        -0.010597401784997278,
        0.032883011666982945,
        0.030841381835986965,
        -0.18703481171888114,
        -0.02798376941698385,
        0.6308807679295904,
        0.7148465705525415,
        0.23037781330885523,
    ]
)
HIGH = np.array([(-1.0) ** j * LOW[7 - j] for j in range(8)])


def lattice_factors():
    a = np.array([(LOW[2 * (3 - j)], LOW[2 * (3 - j) + 1]) for j in range(4)])
    b = np.array([(HIGH[2 * (3 - j)], HIGH[2 * (3 - j) + 1]) for j in range(4)])
    factors = {}
    for s in (3, 2, 1):
        k = (a[s] @ b[s]) / (b[s] @ b[s])
        a, b = (a - k * b) / (1 + k * k), (k * a + b) / (1 + k * k)
        a, b = a[:s], b[1 : s + 1]
        factors[s] = float(k)
    factors[0] = float(a[0][1] / a[0][0])
    return factors, float(a[0][0]), float(np.sign(b[0][1] / a[0][0]))


TURN, SCALE, SIGN = lattice_factors()
F32 = jnp.float32
BF16 = jnp.bfloat16


def two_terms(value):
    top = value.astype(BF16)
    return top, (value - top.astype(F32)).astype(BF16)


def masked_rows(matrix, start, count, lat, lats):
    row = lax.broadcasted_iota(jnp.int32, matrix.shape, 0) + (start + lat * count)
    return jnp.where((row >= 0) & (row < count * lats), matrix, 0.0)


def banded(shape, low, high, row_factor, column_factor, offset):
    row = lax.broadcasted_iota(jnp.int32, shape, 0)
    column = lax.broadcasted_iota(jnp.int32, shape, 1)
    tap = row_factor * row + column_factor * column + offset
    if high is not None:
        second = column >= shape[1] // 2
        tap = jnp.where(second, tap - column_factor * (shape[1] // 2), tap)
    matrix = jnp.zeros(shape, F32)
    for t in range(8):
        value = F32(low[t]) if high is None else jnp.where(second, F32(high[t]), F32(low[t]))
        matrix = jnp.where(tap == t, value, matrix)
    return matrix


def analysis_matrix(taps, out_start, out_rows, in_start, in_rows):
    return banded((out_rows, in_rows), taps, None, -2, 1, in_start + 3 - 2 * out_start)


def synthesis_matrix(out_start, out_rows, in_start, in_rows):
    shape = (out_rows, 2 * in_rows)
    return banded(shape, SCALE * LOW, SCALE * HIGH, 1, -2, out_start - 2 * in_start + 3)


def mxu(a, b):
    return jnp.dot(a, b, preferred_element_type=F32)


def dot3(matrix, vh, vl):
    mh, ml = two_terms(matrix)
    return mxu(mh, vh) + mxu(mh, vl) + mxu(ml, vh)


def first_half(rows):
    return lax.broadcasted_iota(jnp.int32, (rows, LANES), 1) < C


def half_turn(value):
    return None if value is None else pltpu.roll(value, C, 1)


def pick(left, a, b):
    if a is None and b is None:
        return None
    return jnp.where(left, 0.0 if a is None else a, 0.0 if b is None else b)


def plus(a, b, factor):
    if b is None:
        return a
    if a is None:
        return b * factor
    return a + b * factor


class Memo:
    def __init__(self, make):
        self.make, self.known = make, {}

    def __call__(self, n):
        if n not in self.known:
            self.known[n] = self.make(n)
        return self.known[n]


def analysis(cols, start, left):
    turned = Memo(lambda i: half_turn(cols[i]) if 0 <= i < len(cols) else None)
    plain = lambda i: cols[i] if 0 <= i < len(cols) else None
    if start % 2 == 0:
        at = lambda n: n - 1 - start // 2
        u = Memo(lambda n: pick(left, turned(at(n) - 1), plain(at(n))))
        w = Memo(lambda n: pick(left, plain(at(n)), turned(at(n) + 1)))
    else:
        at = lambda n: n - (start + 3) // 2
        u = Memo(lambda n: pick(left, plain(at(n)), turned(at(n) + 1)))
        w = Memo(lambda n: pick(left, turned(at(n)), plain(at(n) + 1)))

    def band(taps):
        def make(k):
            total = None
            for step in range(4):
                total = plus(total, u(k + step), float(taps[2 * step]))
                total = plus(total, w(k + step), float(taps[2 * step + 1]))
            return total

        return make

    return band(LOW), band(HIGH)


def synthesis(lows, highs, start, left):
    def cells(cols):
        return lambda n: cols[(n - 3 - start) // 2] if 0 <= n - 3 - start < 2 * len(cols) else None

    a, b = cells(lows), cells(highs)

    def stage(a, b, factor):
        early = Memo(lambda n: half_turn(plus(b(n), a(n), factor)))
        return (
            Memo(lambda n: plus(a(n), b(n), -factor)),
            Memo(lambda n: pick(left, early(n), early(n + 2))),
        )

    for s in (3, 2, 1):
        a, b = stage(a, b, TURN[s])
    last_a, last_b = a, b
    u = Memo(lambda n: plus(last_a(n), last_b(n), -TURN[0] * SIGN))
    if SIGN < 0:
        w = Memo(lambda n: plus(last_a(n) * TURN[0] if last_a(n) is not None else None, last_b(n), -1.0))
    else:
        w = Memo(lambda n: plus(last_b(n), last_a(n), TURN[0]))
    u_turned, w_turned = Memo(lambda n: half_turn(u(n))), Memo(lambda n: half_turn(w(n)))
    parity = (start + 3) % 2

    def pair(m):
        if m % 2:
            n = (m + 3) // 2
            if n % 2 == parity:
                return pick(left, u(n), w_turned(n))
            return pick(left, u_turned(n - 1), w(n - 1))
        n = m // 2 + 1
        if n % 2 == parity:
            return pick(left, w(n), u(n))
        return pick(left, w_turned(n - 1), u_turned(n + 1))

    return pair


def columns(ref, row, rows, count=None):
    count = ref.shape[-1] // LANES if count is None else count
    return [ref[pl.ds(row, rows), pl.ds(LANES * p, LANES)] for p in range(count)]


def put(ref, row, p, value, lead=()):
    ref[lead + (pl.ds(row, value.shape[0]), pl.ds(LANES * p, LANES))] = value


class Geometry:
    def __init__(self, rows, cells):
        self.rows = [rows >> level for level in range(5)]
        self.cells = [cells >> level for level in range(5)]
        up = lambda value, step: -(-value // step) * step
        self.band = [
            None,
            (-4, up(self.rows[1] + 4, 120)),
            (-8, up(self.rows[2] + 11, 16)),
            (-3, up(self.rows[3] + 6, 8)),
            (-3, up(self.rows[4] + 6, 8)),
        ]
        self.low = [
            None,
            (-52, up(self.rows[1] + 97, 112)),
            (-24, up(self.rows[2] + 45, 88)),
            (-11, up(self.rows[3] + 20, 8)),
            (-3, up(self.rows[4] + 6, 8)),
        ]
        self.span = [None, (-2, self.cells[1] // 2 + 2)]
        for level in (2, 3, 4):
            self.span.append((-3, self.cells[level] // 2 + 3))
        self.extended = max(
            LEAD + 2 * HALO + rows, 2 * (self.low[1][1] - 112) + 256
        )


STEP = 240
SIDE = 8
NEAR = 16


def best_step(rows, most=None):
    return max(s for s in range(8, (most or STEP) + 1, 8) if rows % s == 0)


def low_rows(geo, level, source, source_start, target):
    first, pairs = geo.span[level]
    rows = geo.low[level][1]
    step = best_step(rows, 168)
    left = first_half(step)

    def body(c, carry):
        row = pl.multiple_of(c * step, step)
        low, _ = analysis(columns(source, row, step), source_start, left)
        for q in range(pairs):
            put(target, row, q, low(first + 2 * q))
        return carry

    lax.fori_loop(0, rows // step, body, 0)


def band_rows(geo, level, lo, skip, hi, source_start, gain, bands):
    first, pairs = geo.span[level]
    rows = geo.band[level][1]
    step = best_step(rows)
    left = first_half(step)

    def body(c, carry):
        row = pl.multiple_of(c * step, step)
        g = [jnp.broadcast_to(gain[b : b + 1, :], (step, LANES)) for b in range(3)]
        _, high = analysis(columns(lo, row + skip, step), source_start, left)
        for q in range(pairs):
            put(bands, row, q, high(first + 2 * q) * g[0], (0,))
        low, high = analysis(columns(hi, row, step), source_start, left)
        for q in range(pairs):
            put(bands, row, q, low(first + 2 * q) * g[1], (1,))
            put(bands, row, q, high(first + 2 * q) * g[2], (2,))
        return carry

    lax.fori_loop(0, rows // step, body, 0)


def coarse_kernel(geo, lats, place, edge, x, *refs):
    lat = place[0]
    weights, copies_of = refs[:4], refs[4:8]
    g1, lo2, g2, lo3, g3, lo4, ll4, ext, la, gh, gl, sems, weight_sems = refs[8:]
    for i in range(4):
        pltpu.make_async_copy(weights[i], copies_of[i], weight_sems.at[i]).start()
    rows = geo.rows[0]
    start, count = geo.low[1]
    width = x.shape[1]
    begin = LEAD + HALO
    blocks = count // 112
    cuts = [0] + [min(rows, 224 * b + 256 - begin) for b in range(blocks - 1)] + [rows]
    copies = []
    for i in range(blocks):
        part = pl.ds(cuts[i], cuts[i + 1] - cuts[i])
        to = pl.ds(begin + cuts[i], cuts[i + 1] - cuts[i])
        copies.append(pltpu.make_async_copy(x.at[part, :], ext.at[to, :], sems.at[i]))
        copies[-1].start()
    top = slice(LEAD, begin)
    bottom = slice(begin + rows, begin + rows + HALO)
    ext[0:LEAD, :] = jnp.zeros((LEAD, width), BF16)
    tail = geo.extended - (LEAD + 2 * HALO + rows)
    if tail:
        ext[geo.extended - tail :, :] = jnp.zeros((tail, width), BF16)

    @pl.when(lat == 0)
    def _():
        ext[top, :] = jnp.zeros((HALO, width), BF16)
        ext[bottom, :] = edge[...]

    @pl.when(lat != 0)
    def _():
        ext[top, :] = edge[...]
        ext[bottom, :] = jnp.zeros((HALO, width), BF16)

    base = analysis_matrix(LOW, start, 112, 0 - LEAD - HALO, 256)
    for b in range(blocks):
        copies[b].wait()
        mh, ml = two_terms(masked_rows(base, start + 112 * b, geo.rows[1], lat, lats))
        data = ext[224 * b : 224 * b + 256, :]
        la[112 * b : 112 * b + 112, :] = mxu(mh, data) + mxu(ml, data)
    low_rows(geo, 1, la, 0, g1)
    gh[...], gl[...] = two_terms(g1[...])
    out_start, out_rows = geo.low[2]
    for b in range(out_rows // 88):
        at = min(176 * b, count - 192)
        window = slice(at, at + 192)
        matrix = analysis_matrix(LOW, out_start + 88 * b, 88, start + at, 192)
        matrix = masked_rows(matrix, out_start + 88 * b, geo.rows[2], lat, lats)
        lo2[88 * b : 88 * b + 88, :] = dot3(matrix, gh[window, :], gl[window, :])
    low_rows(geo, 2, lo2, geo.span[1][0], g2)
    for level, source, lo, target in ((3, g2, lo3, g3), (4, g3, lo4, ll4)):
        vh, vl = two_terms(source[...])
        matrix = analysis_matrix(LOW, *geo.low[level], *geo.low[level - 1])
        matrix = masked_rows(matrix, geo.low[level][0], geo.rows[level], lat, lats)
        lo[...] = dot3(matrix, vh, vl)
        low_rows(geo, level, lo, geo.span[level - 1][0], target)
    for i in range(4):
        pltpu.make_async_copy(weights[i], copies_of[i], weight_sems.at[i]).wait()


def first_bands_kernel(geo, lats, place, edge, side_e, side_o, gain, x, d1, ext, la, ha, sem):
    lat, parity = place[0], place[1]
    rows, width = x.shape
    lanes = SIDE * C
    copy = pltpu.make_async_copy(x, ext.at[pl.ds(NEAR, rows), pl.ds(lanes, width)], sem)
    copy.start()
    own = slice(lanes, lanes + width)

    @pl.when(lat == 0)
    def _():
        ext[0:NEAR, own] = jnp.zeros((NEAR, width), BF16)
        ext[NEAR + rows :, own] = edge[0:NEAR, :]

    @pl.when(lat != 0)
    def _():
        ext[0:NEAR, own] = edge[HALO - NEAR :, :]
        ext[NEAR + rows :, own] = jnp.zeros((NEAR, width), BF16)

    @pl.when(parity == 0)
    def _():
        ext[:, 0:lanes] = side_o[...]
        ext[:, lanes + width :] = side_e[...]

    @pl.when(parity != 0)
    def _():
        ext[:, 0:lanes] = side_e[...]
        ext[:, lanes + width :] = side_o[...]

    start, count = geo.band[1]
    low = analysis_matrix(LOW, start, 120, -NEAR, 256)
    high = analysis_matrix(HIGH, start, 120, -NEAR, 256)
    copy.wait()
    for b in range(count // 120):
        data = ext[240 * b : 240 * b + 256, :]
        for matrix, out in ((low, la), (high, ha)):
            mh, ml = two_terms(masked_rows(matrix, start + 120 * b, geo.rows[1], lat, lats))
            out[120 * b : 120 * b + 120, :] = mxu(mh, data) + mxu(ml, data)
    band_rows(geo, 1, la, 0, ha, -SIDE, gain, d1)


def deep_kernel(geo, lats, place, gain, *refs):
    lat, parity = place[0], place[1]
    g1, lo2, g2, lo3, g3, lo4 = refs[:6]
    d = {2: refs[6], 3: refs[7], 4: refs[8]}
    send_e, send_o, p2, m2, p3, m3, hi2, hi3, hi4 = refs[9:]
    grids = {1: g1, 2: g2, 3: g3}
    los, his = {2: lo2, 3: lo3, 4: lo4}, {2: hi2, 3: hi3, 4: hi4}
    for level in (2, 3, 4):
        start, count = geo.band[level]
        source, in_start = grids[level - 1], geo.low[level - 1][0]
        parts = 2 if level == 2 else 1
        half = count // parts
        for b in range(parts):
            if parts == 1:
                at, size = 0, source.shape[0]
            else:
                at = (2 * (start + half * b) - 3 - in_start) // 16 * 16
                size = 2 * half + 16
            vh, vl = two_terms(source[at : at + size, :])
            matrix = analysis_matrix(HIGH, start + half * b, half, in_start + at, size)
            matrix = masked_rows(matrix, start + half * b, geo.rows[level], lat, lats)
            his[level][half * b : half * (b + 1), :] = dot3(matrix, vh, vl)
        rows = gain[3 * (level - 2) : 3 * (level - 2) + 3, :]
        skip = start - geo.low[level][0]
        begin = geo.span[level - 1][0]
        band_rows(geo, level, los[level], skip, his[level], begin, rows, d[level])

    def fill(distance, to_left, to_right):
        for level, count, row in exchange_plan(geo)[distance]:
            n = geo.band[level][1]
            move = distance * geo.cells[level] // 2
            for b in range(3):
                lanes = slice(b * count * LANES, (b + 1) * count * LANES)
                to_left[row : row + n, lanes] = d[level][b, :, 0 : count * LANES].astype(BF16)
                to_right[row : row + n, lanes] = d[level][
                    b, :, move * LANES : (move + count) * LANES
                ].astype(BF16)

    @pl.when(parity == 0)
    def _():
        fill(1, send_o, send_e)

    @pl.when(parity != 0)
    def _():
        fill(1, send_e, send_o)

    fill(2, m2, p2)
    fill(3, m3, p3)


def exchange_plan(geo):
    plan = {}
    for distance in (1, 2, 3):
        entries, row = [], 0
        for level in (2, 3, 4):
            count = geo.span[level][1] - distance * geo.cells[level] // 2
            if count > 0:
                entries.append((level, count, row))
                row += -(-geo.band[level][1] // 16) * 16
        plan[distance] = entries
    return plan


def plan_shape(geo, distance):
    entries = exchange_plan(geo)[distance]
    rows = sum(-(-geo.band[level][1] // 16) * 16 for level, _, _ in entries)
    return (rows, max(count for _, count, _ in entries) * 3 * LANES)


def attention_kernel(geo, lats, blocks, place, keys, grid, we, wqkv, scale, wo, gain, wb, out):
    lat = place[0]
    rows, width = grid.shape
    cells = width // C
    field = grid[...]
    own = jnp.concatenate([field[:, C * c : C * (c + 1)] for c in range(cells)], 0)
    count = own.shape[0]
    embedded = mxu(own.astype(BF16), we[...])
    queries = mxu(embedded.astype(BF16), wqkv[:, 0:E]).astype(BF16)
    lane = lax.broadcasted_iota(jnp.int32, (1, E), 1)
    block = keys.shape[0] // blocks
    factor = [scale[h] * (1.0 / math.sqrt(HEAD_DIM)) for h in range(HEADS)]

    def keyvals(start):
        spread = mxu(keys[pl.ds(start, block), :], we[...]).astype(BF16)
        both = mxu(spread, wqkv[:, E : 3 * E]).astype(BF16)
        return both[:, 0:E], both[:, E : 2 * E]

    def scores_of(h, k):
        mine = (lane >= h * HEAD_DIM) & (lane < (h + 1) * HEAD_DIM)
        q = jnp.where(mine, queries, jnp.zeros_like(queries))
        s = lax.dot_general(q, k, (((1,), (1,)), ((), ())), preferred_element_type=F32)
        return s * factor[h]

    def masked(h, value):
        mine = (lane >= h * HEAD_DIM) & (lane < (h + 1) * HEAD_DIM)
        return jnp.where(mine, value, jnp.zeros_like(value))

    if blocks == 1:
        k, v = keyvals(0)
        attended = jnp.zeros((count, E), F32)
        for h in range(HEADS):
            s = scores_of(h, k)
            w = jnp.exp(s - jnp.max(s, -1, keepdims=True))
            total = jnp.sum(w, -1, keepdims=True)
            attended = attended + masked(h, mxu(w.astype(BF16), v) / total)
    else:

        def one_block(b, carry):
            peaks, totals, sums = carry
            k, v = keyvals(pl.multiple_of(b * block, 16))
            new_peaks, new_totals = [], []
            shrunk = jnp.zeros((count, E), F32)
            for h in range(HEADS):
                s = scores_of(h, k)
                peak = jnp.maximum(peaks[h], jnp.max(s, -1, keepdims=True))
                shrink = jnp.exp(peaks[h] - peak)
                w = jnp.exp(s - peak)
                new_peaks.append(peak)
                new_totals.append(totals[h] * shrink + jnp.sum(w, -1, keepdims=True))
                shrunk = shrunk + masked(h, sums * shrink + mxu(w.astype(BF16), v))
            return tuple(new_peaks), tuple(new_totals), shrunk

        start = (
            tuple(jnp.full((count, 1), -1e30, F32) for _ in range(HEADS)),
            tuple(jnp.zeros((count, 1), F32) for _ in range(HEADS)),
            jnp.zeros((count, E), F32),
        )
        _, totals, sums = lax.fori_loop(0, blocks, one_block, start)
        attended = jnp.zeros((count, E), F32)
        for h in range(HEADS):
            attended = attended + masked(h, sums / totals[h])
    hidden = embedded + mxu(attended.astype(BF16), wo[...])
    square = jnp.mean(hidden * hidden, -1, keepdims=True)
    normed = (hidden * lax.rsqrt(square + 1e-06) * gain[...]).astype(BF16)
    update = lax.dot_general(
        normed, wb[...], (((1,), (1,)), ((), ())), preferred_element_type=F32
    )
    back = [
        jnp.concatenate(
            [update[rows * c : rows * (c + 1), :], update[rows * (c + 1) : rows * (c + 2), :]], 1
        )
        for c in range(0, cells, 2)
    ]
    start = geo.band[4][0]
    for q, value in enumerate(back):
        at = slice(q * LANES, (q + 1) * LANES)
        out[:, at] = masked_rows(field[:, at] + value, start, geo.rows[4], lat, lats)


def synthesis_kernel(geo, lats, place, coarse, d1, d2, d3, d4, *refs):
    lat, parity = place[0], place[1]
    e2, o2, from_m2, from_p2, from_m3, from_p3 = refs[:6]
    out, up3, up2, up1, xh, xl, ylow, yhigh, done, sems = refs[6:]
    bands = {2: d2, 3: d3, 4: d4}
    plan = exchange_plan(geo)

    def from_sides(level, b):
        n = geo.band[level][1]
        cols = [bands[level][b, :, LANES * p : LANES * (p + 1)] for p in range(geo.span[level][1])]
        for distance in (1, 2, 3):
            for which, count, row in plan[distance]:
                if which != level:
                    continue
                move = distance * geo.cells[level] // 2
                for p in range(count):
                    lanes = slice((b * count + p) * LANES, (b * count + p + 1) * LANES)
                    if distance == 1:
                        even = e2[row : row + n, lanes].astype(F32)
                        odd = o2[row : row + n, lanes].astype(F32)
                        low = jnp.where(parity == 0, odd, even)
                        high = jnp.where(parity == 0, even, odd)
                    else:
                        lows, highs = {2: (from_m2, from_p2), 3: (from_m3, from_p3)}[distance]
                        low = lows[row : row + n, lanes].astype(F32)
                        high = highs[row : row + n, lanes].astype(F32)
                    cols[p] = cols[p] + low
                    cols[p + move] = cols[p + move] + high
        return jnp.concatenate(cols, 1)

    uppers = {4: coarse, 3: up3, 2: up2, 1: up1}
    for level in (4, 3, 2):
        begin, pairs = geo.span[level]
        below = level - 1
        start, rows = geo.band[below]
        matrix = synthesis_matrix(start, rows, *geo.band[level])
        matrix = masked_rows(matrix, start, geo.rows[below], lat, lats)
        width = pairs * LANES
        for one, two, y in (
            (uppers[level][...], from_sides(level, 1), ylow),
            (from_sides(level, 0), from_sides(level, 2), yhigh),
        ):
            h, l = two_terms(jnp.concatenate([one, two], 0))
            y[0:rows, 0:width] = dot3(matrix, h, l)
        target = uppers[below]
        first, out_pairs = geo.span[below]

        step = best_step(rows)
        left = first_half(step)

        def joined(c, carry):
            row = pl.multiple_of(c * step, step)
            pair = synthesis(
                columns(ylow, row, step, pairs), columns(yhigh, row, step, pairs), begin, left
            )
            for q in range(out_pairs):
                put(target, row, q, pair(first + 2 * q))
            return carry

        lax.fori_loop(0, rows // step, joined, 0)

    n = geo.band[1][1]
    half = geo.rows[0] // 2
    for block in range(2):
        w = 0 if block == 0 else n - LANES
        window = slice(w, w + LANES)
        sh, sl = two_terms(synthesis_matrix(half * block, half, geo.band[1][0] + w, LANES))
        for one, two, y in (
            (up1[window, :], d1[1, window, :], ylow),
            (d1[0, window, :], d1[2, window, :], yhigh),
        ):
            xh[0:LANES, :], xl[0:LANES, :] = two_terms(one)
            xh[LANES:, :], xl[LANES:, :] = two_terms(two)
            y[half * block : half * (block + 1), :] = (
                mxu(sh, xh[...]) + mxu(sh, xl[...]) + mxu(sl, xh[...])
            )
    begin, pairs = geo.span[1]
    most = 112

    def last(row, count):
        left = first_half(count)
        pair = synthesis(columns(ylow, row, count), columns(yhigh, row, count), begin, left)
        for q in range(geo.cells[0] // 2):
            put(done, row, q, pair(2 * q).astype(BF16))

    def store(i, count):
        part = pl.ds(pl.multiple_of(i * most, 16), count)
        return pltpu.make_async_copy(done.at[part, :], out.at[part, :], sems.at[i])

    whole, rest = geo.rows[0] // most, geo.rows[0] % most

    def chunk(i, carry):
        last(pl.multiple_of(i * most, 16), most)
        store(i, most).start()
        return carry

    lax.fori_loop(0, whole, chunk, 0)
    if rest:
        last(whole * most, rest)
        store(whole, rest).start()
    for i in range(whole):
        store(i, most).wait()
    if rest:
        store(whole, rest).wait()


def call(kernel, out_shape, scratch, *args, cost=20_000_000, grant=24, raw=(), raw_out=False):
    vmem = pl.BlockSpec(memory_space=pltpu.VMEM)
    smem = pl.BlockSpec(memory_space=pltpu.SMEM)
    specs = [smem if a.ndim == 1 and a.size < 16 else vmem for a in args]
    for at in raw:
        specs[at] = pl.BlockSpec(memory_space=pltpu.HBM)
    outs = jax.tree.map(lambda _: pl.BlockSpec(memory_space=pl.ANY) if raw_out else vmem, out_shape)
    return pl.pallas_call(
        kernel,
        out_shape=out_shape,
        in_specs=specs,
        out_specs=outs,
        scratch_shapes=scratch,
        compiler_params=pltpu.CompilerParams(vmem_limit_bytes=grant << 20),
        cost_estimate=pl.CostEstimate(flops=cost, bytes_accessed=1 << 20, transcendentals=0),
    )(*args)


def shape(dims, dtype=F32):
    return pltpu.VMEM(dims, dtype)


def per_device(mesh_shape, state_field, skip_gain, embed_weight, qkv_weight, head_scale, out_weight, norm_gain, back_weight):
    return program(
        mesh_shape, state_field, skip_gain, embed_weight, qkv_weight, head_scale, out_weight, norm_gain, back_weight
    )


def program(mesh_shape, state_field, skip_gain, embed_weight, qkv_weight, head_scale, out_weight, norm_gain, back_weight):
    lons, lats = mesh_shape["lon"], mesh_shape["lat"]
    rows, width = state_field.shape
    geo = Geometry(rows, width // C)
    lat, lon = lax.axis_index("lat"), lax.axis_index("lon")
    place = jnp.stack([lat, lon % 2]).astype(jnp.int32)
    gains = jnp.concatenate([skip_gain, skip_gain], 2).reshape(-1, LANES)

    even_pairs = [(i, i ^ 1) for i in range(lons)]
    odd_pairs = [(i, (i + 1 if i % 2 else i - 1) % lons) for i in range(lons)]
    swap = [(i, lats - 1 - i) for i in range(lats)]

    def shifted(value, by):
        return lax.ppermute(value, "lon", [(i, (i + by) % lons) for i in range(lons)])

    edge = jnp.where(lat == 0, state_field[rows - HALO :], state_field[:HALO])
    edge = lax.ppermute(edge, "lat", swap)

    even_lon = lon % 2 == 0
    wide = SIDE * C

    def beside(value, first):
        return jnp.where(first, value[:, width - wide :], value[:, :wide])

    def with_rows(first):
        near = beside(edge, first)
        none = jnp.zeros((NEAR, wide), BF16)
        top = jnp.where(lat == 0, none, near[HALO - NEAR :])
        bottom = jnp.where(lat == 0, near[:NEAR], none)
        return jnp.concatenate([top, beside(state_field, first), bottom], 0)

    side_e = lax.ppermute(with_rows(even_lon), "lon", even_pairs)
    side_o = lax.ppermute(with_rows(~even_lon), "lon", odd_pairs)

    w = [None] + [geo.span[level][1] * LANES for level in (1, 2, 3, 4)]
    weights = (embed_weight, qkv_weight, out_weight, back_weight.T)
    low = lambda level, lanes: shape((geo.low[level][1], w[lanes]))
    *weights, g1, lo2, g2, lo3, g3, lo4, ll4 = call(
        functools.partial(coarse_kernel, geo, lats),
        tuple(shape(a.shape, BF16) for a in weights)
        + (low(1, 1), low(2, 1), low(2, 2), low(3, 2), low(3, 3), low(4, 3), low(4, 4)),
        [
            pltpu.VMEM((geo.extended, width), BF16),
            pltpu.VMEM((geo.low[1][1], width), F32),
            pltpu.VMEM((geo.low[1][1], w[1]), BF16),
            pltpu.VMEM((geo.low[1][1], w[1]), BF16),
            pltpu.SemaphoreType.DMA((geo.low[1][1] // 112,)),
            pltpu.SemaphoreType.DMA((4,)),
        ],
        place,
        edge,
        state_field,
        *weights,
        raw=(2, 3, 4, 5, 6),
    )
    extended = NEAR + rows + NEAR
    d1 = call(
        functools.partial(first_bands_kernel, geo, lats),
        shape((3, geo.band[1][1], w[1])),
        [
            pltpu.VMEM((extended, width + 2 * wide), BF16),
            pltpu.VMEM((geo.band[1][1], width + 2 * wide), F32),
            pltpu.VMEM((geo.band[1][1], width + 2 * wide), F32),
            pltpu.SemaphoreType.DMA,
        ],
        place,
        edge,
        side_e,
        side_o,
        gains[:3],
        state_field,
        raw=(5,),
    )
    d2, d3, d4, deep_e, deep_o, p2, m2, p3, m3 = call(
        functools.partial(deep_kernel, geo, lats),
        tuple(shape((3, geo.band[level][1], w[level])) for level in (2, 3, 4))
        + tuple(shape(plan_shape(geo, d), BF16) for d in (1, 1, 2, 2, 3, 3)),
        [pltpu.VMEM((geo.band[level][1], w[level - 1]), F32) for level in (2, 3, 4)],
        place,
        gains[3:],
        g1,
        lo2,
        g2,
        lo3,
        g3,
        lo4,
    )

    merged, size = ll4, 1
    while size < lons:
        other = lax.ppermute(merged, "lon", [(i, i ^ size) for i in range(lons)])
        lower_half = (lon // size) % 2 == 0
        lower = jnp.where(lower_half, merged, other)
        upper = jnp.where(lower_half, other, merged)
        more = geo.cells[4] * C * size
        merged = jnp.pad(lower, ((0, 0), (0, more))) + jnp.pad(upper, ((0, 0), (more, 0)))
        size = 2 * size
    around = geo.cells[4] * lons * C
    fold = 6 * C
    ring = jnp.concatenate([merged[:, :fold] + merged[:, around:], merged[:, fold:around]], 1)
    skip = -geo.low[4][0]
    tokens = ring[skip : skip + geo.rows[4]].astype(BF16)
    others = lax.ppermute(tokens, "lat", swap)
    keys = jnp.concatenate([tokens, others], 0).reshape(-1, C)

    deep_e = lax.ppermute(deep_e, "lon", even_pairs)
    deep_o = lax.ppermute(deep_o, "lon", odd_pairs)
    from_m2, from_p2 = shifted(p2, 2), shifted(m2, -2)
    from_m3, from_p3 = shifted(p3, 3), shifted(m3, -3)

    own = lax.dynamic_slice(
        jnp.concatenate([ring, ring[:, :fold]], 1),
        (0, lon * geo.cells[4] * C),
        (geo.low[4][1], geo.span[4][1] * LANES),
    )
    blocks = max(1, keys.shape[0] // 928) if keys.shape[0] % 928 == 0 else 1
    coarse = call(
        functools.partial(attention_kernel, geo, lats, blocks),
        shape(own.shape),
        [],
        place,
        keys,
        own,
        weights[0],
        weights[1],
        head_scale,
        weights[2],
        norm_gain[None],
        weights[3],
        cost=200_000_000,
    )

    return call(
        functools.partial(synthesis_kernel, geo, lats),
        jax.ShapeDtypeStruct((rows, width), BF16),
        [pltpu.VMEM((geo.band[level][1], w[level]), F32) for level in (3, 2, 1)]
        + [
            pltpu.VMEM((2 * LANES, w[1]), BF16),
            pltpu.VMEM((2 * LANES, w[1]), BF16),
            pltpu.VMEM((rows, w[1]), F32),
            pltpu.VMEM((rows, w[1]), F32),
            pltpu.VMEM((rows, width), BF16),
            pltpu.SemaphoreType.DMA((rows // 112 + 1,)),
        ],
        place,
        coarse,
        d1,
        d2,
        d3,
        d4,
        deep_e,
        deep_o,
        from_m2,
        from_p2,
        from_m3,
        from_p3,
        raw_out=True,
    )


def solution(mesh):
    in_specs = (P("lat", ("member", "lon")), P(), P(), P(), P(), P(), P(), P())
    out_specs = P("lat", ("member", "lon"))
    return jax.shard_map(
        functools.partial(per_device, dict(mesh.shape)),
        mesh=mesh,
        in_specs=in_specs,
        out_specs=out_specs,
        check_vma=False,
    )
```

```python
import functools
import math

import jax
import jax.numpy as jnp
import numpy as np
from jax import lax
from jax.experimental import pallas as pl
from jax.experimental.pallas import tpu as pltpu
from jax.sharding import PartitionSpec as P


C = 64
HEADS = 8
HEAD_DIM = 32
E = 256
LANES = 128
HALO = 96
LEAD = 16

LOW = np.array(
    [
        -0.010597401784997278,
        0.032883011666982945,
        0.030841381835986965,
        -0.18703481171888114,
        -0.02798376941698385,
        0.6308807679295904,
        0.7148465705525415,
        0.23037781330885523,
    ]
)
HIGH = np.array([(-1.0) ** j * LOW[7 - j] for j in range(8)])


def lattice_factors():
    a = np.array([(LOW[2 * (3 - j)], LOW[2 * (3 - j) + 1]) for j in range(4)])
    b = np.array([(HIGH[2 * (3 - j)], HIGH[2 * (3 - j) + 1]) for j in range(4)])
    factors = {}
    for s in (3, 2, 1):
        k = (a[s] @ b[s]) / (b[s] @ b[s])
        a, b = (a - k * b) / (1 + k * k), (k * a + b) / (1 + k * k)
        a, b = a[:s], b[1 : s + 1]
        factors[s] = float(k)
    factors[0] = float(a[0][1] / a[0][0])
    return factors, float(a[0][0]), float(np.sign(b[0][1] / a[0][0]))


TURN, SCALE, SIGN = lattice_factors()
F32 = jnp.float32
BF16 = jnp.bfloat16


def two_terms(value):
    top = value.astype(BF16)
    return top, (value - top.astype(F32)).astype(BF16)


def masked_rows(matrix, start, count, lat, lats):
    row = lax.broadcasted_iota(jnp.int32, matrix.shape, 0) + (start + lat * count)
    return jnp.where((row >= 0) & (row < count * lats), matrix, 0.0)


def banded(shape, low, high, row_factor, column_factor, offset):
    row = lax.broadcasted_iota(jnp.int32, shape, 0)
    column = lax.broadcasted_iota(jnp.int32, shape, 1)
    tap = row_factor * row + column_factor * column + offset
    if high is not None:
        second = column >= shape[1] // 2
        tap = jnp.where(second, tap - column_factor * (shape[1] // 2), tap)
    matrix = jnp.zeros(shape, F32)
    for t in range(8):
        value = F32(low[t]) if high is None else jnp.where(second, F32(high[t]), F32(low[t]))
        matrix = jnp.where(tap == t, value, matrix)
    return matrix


def analysis_matrix(taps, out_start, out_rows, in_start, in_rows):
    return banded((out_rows, in_rows), taps, None, -2, 1, in_start + 3 - 2 * out_start)


def synthesis_matrix(out_start, out_rows, in_start, in_rows):
    shape = (out_rows, 2 * in_rows)
    return banded(shape, SCALE * LOW, SCALE * HIGH, 1, -2, out_start - 2 * in_start + 3)


def mxu(a, b):
    return jnp.dot(a, b, preferred_element_type=F32)


def dot3(matrix, vh, vl):
    mh, ml = two_terms(matrix)
    return mxu(mh, vh) + mxu(mh, vl) + mxu(ml, vh)


def first_half(rows):
    return lax.broadcasted_iota(jnp.int32, (rows, LANES), 1) < C


def half_turn(value):
    return None if value is None else pltpu.roll(value, C, 1)


def pick(left, a, b):
    if a is None and b is None:
        return None
    return jnp.where(left, 0.0 if a is None else a, 0.0 if b is None else b)


def plus(a, b, factor):
    if b is None:
        return a
    if a is None:
        return b * factor
    return a + b * factor


class Memo:
    def __init__(self, make):
        self.make, self.known = make, {}

    def __call__(self, n):
        if n not in self.known:
            self.known[n] = self.make(n)
        return self.known[n]


def analysis(cols, start, left):
    turned = Memo(lambda i: half_turn(cols[i]) if 0 <= i < len(cols) else None)
    plain = lambda i: cols[i] if 0 <= i < len(cols) else None
    if start % 2 == 0:
        at = lambda n: n - 1 - start // 2
        u = Memo(lambda n: pick(left, turned(at(n) - 1), plain(at(n))))
        w = Memo(lambda n: pick(left, plain(at(n)), turned(at(n) + 1)))
    else:
        at = lambda n: n - (start + 3) // 2
        u = Memo(lambda n: pick(left, plain(at(n)), turned(at(n) + 1)))
        w = Memo(lambda n: pick(left, turned(at(n)), plain(at(n) + 1)))

    def band(taps):
        def make(k):
            total = None
            for step in range(4):
                total = plus(total, u(k + step), float(taps[2 * step]))
                total = plus(total, w(k + step), float(taps[2 * step + 1]))
            return total

        return make

    return band(LOW), band(HIGH)


def synthesis(lows, highs, start, left):
    def cells(cols):
        return lambda n: cols[(n - 3 - start) // 2] if 0 <= n - 3 - start < 2 * len(cols) else None

    a, b = cells(lows), cells(highs)

    def stage(a, b, factor):
        early = Memo(lambda n: half_turn(plus(b(n), a(n), factor)))
        return (
            Memo(lambda n: plus(a(n), b(n), -factor)),
            Memo(lambda n: pick(left, early(n), early(n + 2))),
        )

    for s in (3, 2, 1):
        a, b = stage(a, b, TURN[s])
    last_a, last_b = a, b
    u = Memo(lambda n: plus(last_a(n), last_b(n), -TURN[0] * SIGN))
    if SIGN < 0:
        w = Memo(lambda n: plus(last_a(n) * TURN[0] if last_a(n) is not None else None, last_b(n), -1.0))
    else:
        w = Memo(lambda n: plus(last_b(n), last_a(n), TURN[0]))
    u_turned, w_turned = Memo(lambda n: half_turn(u(n))), Memo(lambda n: half_turn(w(n)))
    parity = (start + 3) % 2

    def pair(m):
        if m % 2:
            n = (m + 3) // 2
            if n % 2 == parity:
                return pick(left, u(n), w_turned(n))
            return pick(left, u_turned(n - 1), w(n - 1))
        n = m // 2 + 1
        if n % 2 == parity:
            return pick(left, w(n), u(n))
        return pick(left, w_turned(n - 1), u_turned(n + 1))

    return pair


def columns(ref, row, rows, count=None):
    count = ref.shape[-1] // LANES if count is None else count
    return [ref[pl.ds(row, rows), pl.ds(LANES * p, LANES)] for p in range(count)]


def put(ref, row, p, value, lead=()):
    ref[lead + (pl.ds(row, value.shape[0]), pl.ds(LANES * p, LANES))] = value


class Geometry:
    def __init__(self, rows, cells):
        self.rows = [rows >> level for level in range(5)]
        self.cells = [cells >> level for level in range(5)]
        up = lambda value, step: -(-value // step) * step
        self.band = [
            None,
            (-4, up(self.rows[1] + 4, 120)),
            (-8, up(self.rows[2] + 11, 16)),
            (-3, up(self.rows[3] + 6, 8)),
            (-3, up(self.rows[4] + 6, 8)),
        ]
        self.low = [
            None,
            (-52, up(self.rows[1] + 97, 112)),
            (-24, up(self.rows[2] + 45, 88)),
            (-11, up(self.rows[3] + 20, 8)),
            (-3, up(self.rows[4] + 6, 8)),
        ]
        self.span = [None, (-2, self.cells[1] // 2 + 2)]
        for level in (2, 3, 4):
            self.span.append((-3, self.cells[level] // 2 + 3))
        self.extended = max(
            LEAD + 2 * HALO + rows, 2 * (self.low[1][1] - 112) + 256
        )


STEP = 240
SIDE = 8
NEAR = 16


def best_step(rows, most=None):
    return max(s for s in range(8, (most or STEP) + 1, 8) if rows % s == 0)


def low_rows(geo, level, source, source_start, target):
    first, pairs = geo.span[level]
    rows = geo.low[level][1]
    step = best_step(rows, 168)
    left = first_half(step)

    def body(c, carry):
        row = pl.multiple_of(c * step, step)
        low, _ = analysis(columns(source, row, step), source_start, left)
        for q in range(pairs):
            put(target, row, q, low(first + 2 * q))
        return carry

    lax.fori_loop(0, rows // step, body, 0)


def band_rows(geo, level, lo, skip, hi, source_start, gain, bands):
    first, pairs = geo.span[level]
    rows = geo.band[level][1]
    step = best_step(rows)
    left = first_half(step)

    def body(c, carry):
        row = pl.multiple_of(c * step, step)
        g = []
        for b in range(3):
            one = gain[level - 1, b : b + 1, :]
            g.append(jnp.broadcast_to(jnp.concatenate([one, one], 1), (step, LANES)))
        _, high = analysis(columns(lo, row + skip, step), source_start, left)
        for q in range(pairs):
            put(bands, row, q, high(first + 2 * q) * g[0], (0,))
        low, high = analysis(columns(hi, row, step), source_start, left)
        for q in range(pairs):
            put(bands, row, q, low(first + 2 * q) * g[1], (1,))
            put(bands, row, q, high(first + 2 * q) * g[2], (2,))
        return carry

    lax.fori_loop(0, rows // step, body, 0)


def analysis_kernel(geo, lats, place, edge, gain, x, *refs):
    lat, parity = place[0], place[1] % 2
    ll4, out2, out3, out4, send_e, send_o, p2, m2, p3, m3 = refs[:10]
    ext, la, g1, gh, gl, lo2, g2, lo3, g3, lo4, hi2, hi3, hi4, d2, d3, d4, sems, out_sems = refs[10:]
    outs = {2: (d2, out2), 3: (d3, out3), 4: (d4, out4)}
    rows = geo.rows[0]
    start, count = geo.low[1]
    width = x.shape[1]
    begin = LEAD + HALO
    blocks = count // 112
    cuts = [0] + [min(rows, 224 * b + 256 - begin) for b in range(blocks - 1)] + [rows]
    copies = []
    for i in range(blocks):
        part = pl.ds(cuts[i], cuts[i + 1] - cuts[i])
        to = pl.ds(begin + cuts[i], cuts[i + 1] - cuts[i])
        copies.append(pltpu.make_async_copy(x.at[part, :], ext.at[to, :], sems.at[i]))
        copies[-1].start()
    top = slice(LEAD, begin)
    bottom = slice(begin + rows, begin + rows + HALO)
    ext[0:LEAD, :] = jnp.zeros((LEAD, width), BF16)
    tail = geo.extended - (LEAD + 2 * HALO + rows)
    if tail:
        ext[geo.extended - tail :, :] = jnp.zeros((tail, width), BF16)

    @pl.when(lat == 0)
    def _():
        ext[top, :] = jnp.zeros((HALO, width), BF16)
        ext[bottom, :] = edge[...]

    @pl.when(lat != 0)
    def _():
        ext[top, :] = edge[...]
        ext[bottom, :] = jnp.zeros((HALO, width), BF16)

    base = analysis_matrix(LOW, start, 112, 0 - LEAD - HALO, 256)
    for b in range(blocks):
        copies[b].wait()
        mh, ml = two_terms(masked_rows(base, start + 112 * b, geo.rows[1], lat, lats))
        data = ext[224 * b : 224 * b + 256, :]
        la[112 * b : 112 * b + 112, :] = mxu(mh, data) + mxu(ml, data)
    low_rows(geo, 1, la, 0, g1)
    gh[...], gl[...] = two_terms(g1[...])
    out_start, out_rows = geo.low[2]
    for b in range(out_rows // 88):
        at = min(176 * b, count - 192)
        window = slice(at, at + 192)
        matrix = analysis_matrix(LOW, out_start + 88 * b, 88, start + at, 192)
        matrix = masked_rows(matrix, out_start + 88 * b, geo.rows[2], lat, lats)
        lo2[88 * b : 88 * b + 88, :] = dot3(matrix, gh[window, :], gl[window, :])
    low_rows(geo, 2, lo2, geo.span[1][0], g2)
    for level, source, lo, target in ((3, g2, lo3, g3), (4, g3, lo4, ll4)):
        vh, vl = two_terms(source[...])
        matrix = analysis_matrix(LOW, *geo.low[level], *geo.low[level - 1])
        matrix = masked_rows(matrix, geo.low[level][0], geo.rows[level], lat, lats)
        lo[...] = dot3(matrix, vh, vl)
        low_rows(geo, level, lo, geo.span[level - 1][0], target)
    copies = []
    for level, lo, hi in ((2, lo2, hi2), (3, lo3, hi3), (4, lo4, hi4)):
        deep_bands(geo, lats, lat, level, {2: (gh, gl), 3: g2, 4: g3}[level], lo, hi, gain, outs[level][0])
        copies.append(pltpu.make_async_copy(*outs[level], out_sems.at[level - 2]))
        copies[-1].start()
    d = {2: d2, 3: d3, 4: d4}

    def fill(distance, to_left, to_right):
        for level, count, row in exchange_plan(geo)[distance]:
            n = geo.band[level][1]
            move = distance * geo.cells[level] // 2
            for b in range(3):
                lanes = slice(b * count * LANES, (b + 1) * count * LANES)
                to_left[row : row + n, lanes] = d[level][b, :, 0 : count * LANES].astype(BF16)
                to_right[row : row + n, lanes] = d[level][
                    b, :, move * LANES : (move + count) * LANES
                ].astype(BF16)

    @pl.when(parity == 0)
    def _():
        fill(1, send_o, send_e)

    @pl.when(parity != 0)
    def _():
        fill(1, send_e, send_o)

    fill(2, m2, p2)
    fill(3, m3, p3)
    for copy in copies:
        copy.wait()


def deep_bands(geo, lats, lat, level, source, lo, hi, gain, bands):
    start, count = geo.band[level]
    in_start = geo.low[level - 1][0]
    parts = 2 if level == 2 else 1
    half = count // parts
    for b in range(parts):
        if parts == 1:
            at, size = 0, source.shape[0]
            vh, vl = two_terms(source[...])
        else:
            at = (2 * (start + half * b) - 3 - in_start) // 16 * 16
            size = 2 * half + 16
            vh, vl = source[0][at : at + size, :], source[1][at : at + size, :]
        matrix = analysis_matrix(HIGH, start + half * b, half, in_start + at, size)
        matrix = masked_rows(matrix, start + half * b, geo.rows[level], lat, lats)
        hi[half * b : half * (b + 1), :] = dot3(matrix, vh, vl)
    skip = start - geo.low[level][0]
    band_rows(geo, level, lo, skip, hi, geo.span[level - 1][0], gain, bands)


def sides_kernel(place, edge, x, side_e, side_o, sems):
    lat, parity = place[0], place[1] % 2
    rows, width = x.shape
    lanes = SIDE * C
    own = pl.ds(NEAR, rows)

    def fill(side, begin, sem):
        copy = pltpu.make_async_copy(x.at[:, pl.ds(begin, lanes)], side.at[own, :], sem)
        copy.start()
        cols = slice(begin, begin + lanes)

        @pl.when(lat == 0)
        def _():
            side[0:NEAR, :] = jnp.zeros((NEAR, lanes), BF16)
            side[NEAR + rows :, :] = edge[0:NEAR, cols]

        @pl.when(lat != 0)
        def _():
            side[0:NEAR, :] = edge[HALO - NEAR :, cols]
            side[NEAR + rows :, :] = jnp.zeros((NEAR, lanes), BF16)

        return copy

    def both(low, high):
        one, two = fill(low, 0, sems.at[0]), fill(high, width - lanes, sems.at[1])
        one.wait()
        two.wait()

    @pl.when(parity == 0)
    def _():
        both(side_o, side_e)

    @pl.when(parity != 0)
    def _():
        both(side_e, side_o)


def merge_kernel(size, more, place, mine, other, out):
    width = mine.shape[1]

    def add(lower, upper):
        out[:, 0:more] = lower[:, 0:more]
        out[:, more:width] = lower[:, more:] + upper[:, 0 : width - more]
        out[:, width:] = upper[:, width - more :]

    lower_half = (place[1] // size) % 2 == 0

    @pl.when(lower_half)
    def _():
        add(mine, other)

    @pl.when(jnp.logical_not(lower_half))
    def _():
        add(other, mine)


def last_merge_kernel(geo, size, more, place, mine, other, ring, tokens, merged):
    merge_kernel(size, more, place, mine, other, merged)
    around = ring.shape[1]
    fold = merged.shape[1] - around
    ring[:, 0:fold] = merged[:, 0:fold] + merged[:, around:]
    ring[:, fold:] = merged[:, fold:around]
    skip = -geo.low[4][0]
    tokens[...] = ring[skip : skip + geo.rows[4], :].astype(BF16)


def first_bands_kernel(geo, lats, place, edge, side_e, side_o, gain, x, held, ext, la, ha, d1, sem):
    lat, parity = place[0], place[1] % 2
    rows, width = x.shape
    lanes = SIDE * C
    copy = pltpu.make_async_copy(x, ext.at[pl.ds(NEAR, rows), pl.ds(lanes, width)], sem)
    copy.start()
    own = slice(lanes, lanes + width)

    @pl.when(lat == 0)
    def _():
        ext[0:NEAR, own] = jnp.zeros((NEAR, width), BF16)
        ext[NEAR + rows :, own] = edge[0:NEAR, :]

    @pl.when(lat != 0)
    def _():
        ext[0:NEAR, own] = edge[HALO - NEAR :, :]
        ext[NEAR + rows :, own] = jnp.zeros((NEAR, width), BF16)

    @pl.when(parity == 0)
    def _():
        ext[:, 0:lanes] = side_o[...]
        ext[:, lanes + width :] = side_e[...]

    @pl.when(parity != 0)
    def _():
        ext[:, 0:lanes] = side_e[...]
        ext[:, lanes + width :] = side_o[...]

    start, count = geo.band[1]
    low = analysis_matrix(LOW, start, 120, -NEAR, 256)
    high = analysis_matrix(HIGH, start, 120, -NEAR, 256)
    copy.wait()
    for b in range(count // 120):
        data = ext[240 * b : 240 * b + 256, :]
        for matrix, out in ((low, la), (high, ha)):
            mh, ml = two_terms(masked_rows(matrix, start + 120 * b, geo.rows[1], lat, lats))
            out[120 * b : 120 * b + 120, :] = mxu(mh, data) + mxu(ml, data)
    band_rows(geo, 1, la, 0, ha, -SIDE, gain, d1)
    copy = pltpu.make_async_copy(d1, held, sem)
    copy.start()
    copy.wait()


def exchange_plan(geo):
    plan = {}
    for distance in (1, 2, 3):
        entries, row = [], 0
        for level in (2, 3, 4):
            count = geo.span[level][1] - distance * geo.cells[level] // 2
            if count > 0:
                entries.append((level, count, row))
                row += -(-geo.band[level][1] // 16) * 16
        plan[distance] = entries
    return plan


def plan_shape(geo, distance):
    entries = exchange_plan(geo)[distance]
    rows = sum(-(-geo.band[level][1] // 16) * 16 for level, _, _ in entries)
    return (rows, max(count for _, count, _ in entries) * 3 * LANES)


def attention_kernel(geo, lats, blocks, place, ring, own, others, we, wqkv, scale, wo, gain, wb, out, around, listed, keys):
    lat, lon = place[0], place[1]
    rows, width = out.shape
    cells = width // C
    total = ring.shape[1]
    around[:, 0:total] = ring[...]
    around[:, total:] = ring[:, 0 : around.shape[1] - total]
    field = around[:, pl.ds(pl.multiple_of(lon * (geo.cells[4] * C), LANES), width)]
    count = geo.rows[4]
    for source, shift in ((own, 0), (others, count)):
        for pair in range(total // LANES):
            value = source[:, pair * LANES : (pair + 1) * LANES].astype(F32)
            for side in range(2):
                at = 2 * count * (2 * pair + side) + shift
                listed[at : at + count, :] = value[:, side * C : (side + 1) * C]
    keys[...] = listed[...].astype(BF16)
    own = jnp.concatenate([field[:, C * c : C * (c + 1)] for c in range(cells)], 0)
    count = own.shape[0]
    embedded = mxu(own.astype(BF16), we[...])
    queries = mxu(embedded.astype(BF16), wqkv[:, 0:E]).astype(BF16)
    lane = lax.broadcasted_iota(jnp.int32, (1, E), 1)
    block = keys.shape[0] // blocks
    factor = [scale[h] * (1.0 / math.sqrt(HEAD_DIM)) for h in range(HEADS)]

    def keyvals(start):
        spread = mxu(keys[pl.ds(start, block), :], we[...]).astype(BF16)
        both = mxu(spread, wqkv[:, E : 3 * E]).astype(BF16)
        return both[:, 0:E], both[:, E : 2 * E]

    def scores_of(h, k):
        mine = (lane >= h * HEAD_DIM) & (lane < (h + 1) * HEAD_DIM)
        q = jnp.where(mine, queries, jnp.zeros_like(queries))
        s = lax.dot_general(q, k, (((1,), (1,)), ((), ())), preferred_element_type=F32)
        return s * factor[h]

    def masked(h, value):
        mine = (lane >= h * HEAD_DIM) & (lane < (h + 1) * HEAD_DIM)
        return jnp.where(mine, value, jnp.zeros_like(value))

    if blocks == 1:
        k, v = keyvals(0)
        attended = jnp.zeros((count, E), F32)
        for h in range(HEADS):
            s = scores_of(h, k)
            w = jnp.exp(s - jnp.max(s, -1, keepdims=True))
            total = jnp.sum(w, -1, keepdims=True)
            attended = attended + masked(h, mxu(w.astype(BF16), v) / total)
    else:

        def one_block(b, carry):
            peaks, totals, sums = carry
            k, v = keyvals(pl.multiple_of(b * block, 16))
            new_peaks, new_totals = [], []
            shrunk = jnp.zeros((count, E), F32)
            for h in range(HEADS):
                s = scores_of(h, k)
                peak = jnp.maximum(peaks[h], jnp.max(s, -1, keepdims=True))
                shrink = jnp.exp(peaks[h] - peak)
                w = jnp.exp(s - peak)
                new_peaks.append(peak)
                new_totals.append(totals[h] * shrink + jnp.sum(w, -1, keepdims=True))
                shrunk = shrunk + masked(h, sums * shrink + mxu(w.astype(BF16), v))
            return tuple(new_peaks), tuple(new_totals), shrunk

        start = (
            tuple(jnp.full((count, 1), -1e30, F32) for _ in range(HEADS)),
            tuple(jnp.zeros((count, 1), F32) for _ in range(HEADS)),
            jnp.zeros((count, E), F32),
        )
        _, totals, sums = lax.fori_loop(0, blocks, one_block, start)
        attended = jnp.zeros((count, E), F32)
        for h in range(HEADS):
            attended = attended + masked(h, sums / totals[h])
    hidden = embedded + mxu(attended.astype(BF16), wo[...])
    square = jnp.mean(hidden * hidden, -1, keepdims=True)
    normed = (hidden * lax.rsqrt(square + 1e-06) * gain[...]).astype(BF16)
    update = lax.dot_general(
        normed, wb[...], (((1,), (1,)), ((), ())), preferred_element_type=F32
    )
    back = [
        jnp.concatenate(
            [update[rows * c : rows * (c + 1), :], update[rows * (c + 1) : rows * (c + 2), :]], 1
        )
        for c in range(0, cells, 2)
    ]
    start = geo.band[4][0]
    for q, value in enumerate(back):
        at = slice(q * LANES, (q + 1) * LANES)
        out[:, at] = masked_rows(field[:, at] + value, start, geo.rows[4], lat, lats)


def synthesis_kernel(geo, lats, place, coarse, e2, o2, from_m2, from_p2, from_m3, from_p3, *refs):
    lat, parity = place[0], place[1] % 2
    held, (out, up3, up2, up1, xh, xl, ylow, yhigh, done), refs = refs[:4], refs[4:13], refs[13:]
    d1, d2, d3, d4, sems, in_sems = refs
    arrive = [
        pltpu.make_async_copy(source, to, in_sems.at[i])
        for i, (source, to) in enumerate(zip(held, (d1, d2, d3, d4)))
    ]
    for level in (4, 3, 2, 1):
        arrive[level - 1].start()
    bands = {2: d2, 3: d3, 4: d4}
    plan = exchange_plan(geo)

    def from_sides(level, b):
        n = geo.band[level][1]
        cols = [bands[level][b, :, LANES * p : LANES * (p + 1)] for p in range(geo.span[level][1])]
        for distance in (1, 2, 3):
            for which, count, row in plan[distance]:
                if which != level:
                    continue
                move = distance * geo.cells[level] // 2
                for p in range(count):
                    lanes = slice((b * count + p) * LANES, (b * count + p + 1) * LANES)
                    if distance == 1:
                        even = e2[row : row + n, lanes].astype(F32)
                        odd = o2[row : row + n, lanes].astype(F32)
                        low = jnp.where(parity == 0, odd, even)
                        high = jnp.where(parity == 0, even, odd)
                    else:
                        lows, highs = {2: (from_m2, from_p2), 3: (from_m3, from_p3)}[distance]
                        low = lows[row : row + n, lanes].astype(F32)
                        high = highs[row : row + n, lanes].astype(F32)
                    cols[p] = cols[p] + low
                    cols[p + move] = cols[p + move] + high
        return jnp.concatenate(cols, 1)

    uppers = {4: coarse, 3: up3, 2: up2, 1: up1}
    for level in (4, 3, 2):
        arrive[level - 1].wait()
        begin, pairs = geo.span[level]
        below = level - 1
        start, rows = geo.band[below]
        matrix = synthesis_matrix(start, rows, *geo.band[level])
        matrix = masked_rows(matrix, start, geo.rows[below], lat, lats)
        width = pairs * LANES
        for one, two, y in (
            (uppers[level][...], from_sides(level, 1), ylow),
            (from_sides(level, 0), from_sides(level, 2), yhigh),
        ):
            h, l = two_terms(jnp.concatenate([one, two], 0))
            y[0:rows, 0:width] = dot3(matrix, h, l)
        target = uppers[below]
        first, out_pairs = geo.span[below]

        step = best_step(rows)
        left = first_half(step)

        def joined(c, carry):
            row = pl.multiple_of(c * step, step)
            pair = synthesis(
                columns(ylow, row, step, pairs), columns(yhigh, row, step, pairs), begin, left
            )
            for q in range(out_pairs):
                put(target, row, q, pair(first + 2 * q))
            return carry

        lax.fori_loop(0, rows // step, joined, 0)

    arrive[0].wait()
    n = geo.band[1][1]
    half = geo.rows[0] // 2
    for block in range(2):
        w = 0 if block == 0 else n - LANES
        window = slice(w, w + LANES)
        sh, sl = two_terms(synthesis_matrix(half * block, half, geo.band[1][0] + w, LANES))
        for one, two, y in (
            (up1[window, :], d1[1, window, :], ylow),
            (d1[0, window, :], d1[2, window, :], yhigh),
        ):
            xh[0:LANES, :], xl[0:LANES, :] = two_terms(one)
            xh[LANES:, :], xl[LANES:, :] = two_terms(two)
            y[half * block : half * (block + 1), :] = (
                mxu(sh, xh[...]) + mxu(sh, xl[...]) + mxu(sl, xh[...])
            )
    begin, pairs = geo.span[1]
    most = 112

    def last(row, count):
        left = first_half(count)
        pair = synthesis(columns(ylow, row, count), columns(yhigh, row, count), begin, left)
        for q in range(geo.cells[0] // 2):
            put(done, row, q, pair(2 * q).astype(BF16))

    def store(i, count):
        part = pl.ds(pl.multiple_of(i * most, 16), count)
        return pltpu.make_async_copy(done.at[part, :], out.at[part, :], sems.at[i])

    whole, rest = geo.rows[0] // most, geo.rows[0] % most

    def chunk(i, carry):
        last(pl.multiple_of(i * most, 16), most)
        store(i, most).start()
        return carry

    lax.fori_loop(0, whole, chunk, 0)
    if rest:
        last(whole * most, rest)
        store(whole, rest).start()
    for i in range(whole):
        store(i, most).wait()
    if rest:
        store(whole, rest).wait()


def call(kernel, out_shape, scratch, *args, cost=20_000_000, grant=24, raw=(), raw_out=()):
    vmem = pl.BlockSpec(memory_space=pltpu.VMEM)
    smem = pl.BlockSpec(memory_space=pltpu.SMEM)
    anywhere = pl.BlockSpec(memory_space=pl.ANY)
    specs = [smem if a.ndim == 1 and a.size < 16 else vmem for a in args]
    for at in raw:
        specs[at] = anywhere
    outs = [anywhere if i in raw_out else vmem for i in range(len(out_shape))]
    return pl.pallas_call(
        kernel,
        out_shape=tuple(out_shape),
        in_specs=specs,
        out_specs=tuple(outs),
        scratch_shapes=scratch,
        compiler_params=pltpu.CompilerParams(vmem_limit_bytes=grant << 20),
        cost_estimate=pl.CostEstimate(flops=cost, bytes_accessed=1 << 20, transcendentals=0),
    )(*args)


def shape(dims, dtype=F32):
    return jax.ShapeDtypeStruct(dims, dtype)


def per_device(mesh_shape, state_field, skip_gain, embed_weight, qkv_weight, head_scale, out_weight, norm_gain, back_weight):
    return program(
        mesh_shape, state_field, skip_gain, embed_weight, qkv_weight, head_scale, out_weight, norm_gain, back_weight
    )


def program(mesh_shape, state_field, skip_gain, embed_weight, qkv_weight, head_scale, out_weight, norm_gain, back_weight):
    lons, lats = mesh_shape["lon"], mesh_shape["lat"]
    rows, width = state_field.shape
    geo = Geometry(rows, width // C)
    lat, lon = lax.axis_index("lat"), lax.axis_index("lon")
    place = jnp.stack([lat, lon]).astype(jnp.int32)

    even_pairs = [(i, i ^ 1) for i in range(lons)]
    odd_pairs = [(i, (i + 1 if i % 2 else i - 1) % lons) for i in range(lons)]
    swap = [(i, lats - 1 - i) for i in range(lats)]

    def shifted(value, by):
        return lax.ppermute(value, "lon", [(i, (i + by) % lons) for i in range(lons)])

    edge = lax.dynamic_slice(
        state_field, (jnp.where(lat == 0, rows - HALO, 0), 0), (HALO, width)
    )
    edge = lax.ppermute(edge, "lat", swap)

    wide = SIDE * C
    extended = NEAR + rows + NEAR
    side_e, side_o = call(
        sides_kernel,
        [shape((extended, wide), BF16)] * 2,
        [pltpu.SemaphoreType.DMA((2,))],
        place,
        edge,
        state_field,
        raw=(2,),
        cost=1_000_000,
    )
    side_e = lax.ppermute(side_e, "lon", even_pairs)
    side_o = lax.ppermute(side_o, "lon", odd_pairs)

    w = [None] + [geo.span[level][1] * LANES for level in (1, 2, 3, 4)]
    low = lambda level, lanes: pltpu.VMEM((geo.low[level][1], w[lanes]), F32)
    bands = [(3, geo.band[level][1], w[level]) for level in (1, 2, 3, 4)]
    ll4, d2, d3, d4, deep_e, deep_o, p2, m2, p3, m3 = call(
        functools.partial(analysis_kernel, geo, lats),
        [shape((geo.low[4][1], w[4]))]
        + [shape(dims) for dims in bands[1:]]
        + [shape(plan_shape(geo, d), BF16) for d in (1, 1, 2, 2, 3, 3)],
        [
            pltpu.VMEM((geo.extended, width), BF16),
            pltpu.VMEM((geo.low[1][1], width), F32),
            low(1, 1),
            pltpu.VMEM((geo.low[1][1], w[1]), BF16),
            pltpu.VMEM((geo.low[1][1], w[1]), BF16),
            low(2, 1),
            low(2, 2),
            low(3, 2),
            low(3, 3),
            low(4, 3),
        ]
        + [pltpu.VMEM((geo.band[level][1], w[level - 1]), F32) for level in (2, 3, 4)]
        + [pltpu.VMEM(dims, F32) for dims in bands[1:]]
        + [
            pltpu.SemaphoreType.DMA((geo.low[1][1] // 112,)),
            pltpu.SemaphoreType.DMA((3,)),
        ],
        place,
        edge,
        skip_gain,
        state_field,
        raw=(3,),
        raw_out=(1, 2, 3),
    )
    (d1,) = call(
        functools.partial(first_bands_kernel, geo, lats),
        [shape(bands[0])],
        [
            pltpu.VMEM((extended, width + 2 * wide), BF16),
            pltpu.VMEM((geo.band[1][1], width + 2 * wide), F32),
            pltpu.VMEM((geo.band[1][1], width + 2 * wide), F32),
            pltpu.VMEM(bands[0], F32),
            pltpu.SemaphoreType.DMA,
        ],
        place,
        edge,
        side_e,
        side_o,
        skip_gain,
        state_field,
        raw=(5,),
        raw_out=(0,),
    )

    merged, size = ll4, 1
    total = geo.cells[4] * lons * C
    while size < lons:
        other = lax.ppermute(merged, "lon", [(i, i ^ size) for i in range(lons)])
        more = geo.cells[4] * C * size
        dims = (merged.shape[0], merged.shape[1] + more)
        if 2 * size < lons:
            (merged,) = call(
                functools.partial(merge_kernel, size, more), [shape(dims)], [], place, merged, other, cost=100_000
            )
        else:
            ring, tokens = call(
                functools.partial(last_merge_kernel, geo, size, more),
                [shape((dims[0], total)), shape((geo.rows[4], total), BF16)],
                [pltpu.VMEM(dims, F32)],
                place,
                merged,
                other,
                cost=100_000,
            )
        size = 2 * size
    others = lax.ppermute(tokens, "lat", swap)

    deep_e = lax.ppermute(deep_e, "lon", even_pairs)
    deep_o = lax.ppermute(deep_o, "lon", odd_pairs)
    from_m2, from_p2 = shifted(p2, 2), shifted(m2, -2)
    from_m3, from_p3 = shifted(p3, 3), shifted(m3, -3)

    key_count = 2 * geo.rows[4] * geo.cells[4] * lons
    blocks = key_count // 928 if key_count % 928 == 0 else 1
    (coarse,) = call(
        functools.partial(attention_kernel, geo, lats, blocks),
        [shape((geo.low[4][1], w[4]))],
        [
            pltpu.VMEM((geo.low[4][1], total + 6 * C), F32),
            pltpu.VMEM((key_count, C), F32),
            pltpu.VMEM((key_count, C), BF16),
        ],
        place,
        ring,
        tokens,
        others,
        embed_weight,
        qkv_weight,
        head_scale,
        out_weight,
        norm_gain[None],
        back_weight.T,
        cost=200_000_000,
        grant=40,
    )

    (out,) = call(
        functools.partial(synthesis_kernel, geo, lats),
        [shape((rows, width), BF16)],
        [pltpu.VMEM((geo.band[level][1], w[level]), F32) for level in (3, 2, 1)]
        + [
            pltpu.VMEM((2 * LANES, w[1]), BF16),
            pltpu.VMEM((2 * LANES, w[1]), BF16),
            pltpu.VMEM((rows, w[1]), F32),
            pltpu.VMEM((rows, w[1]), F32),
            pltpu.VMEM((rows, width), BF16),
        ]
        + [pltpu.VMEM(dims, F32) for dims in bands]
        + [
            pltpu.SemaphoreType.DMA((rows // 112 + 1,)),
            pltpu.SemaphoreType.DMA((4,)),
        ],
        place,
        coarse,
        deep_e,
        deep_o,
        from_m2,
        from_p2,
        from_m3,
        from_p3,
        d1,
        d2,
        d3,
        d4,
        raw=(8, 9, 10, 11),
        raw_out=(0,),
        grant=40,
    )
    return out


def solution(mesh):
    in_specs = (P("lat", ("member", "lon")), P(), P(), P(), P(), P(), P(), P())
    out_specs = P("lat", ("member", "lon"))
    return jax.shard_map(
        functools.partial(per_device, dict(mesh.shape)),
        mesh=mesh,
        in_specs=in_specs,
        out_specs=out_specs,
        check_vma=False,
    )
```

```python
import functools
import math

import jax
import jax.numpy as jnp
import numpy as np
from jax import lax
from jax.experimental import pallas as pl
from jax.experimental.pallas import tpu as pltpu
from jax.sharding import PartitionSpec as P


C = 64
HEADS = 8
HEAD_DIM = 32
E = 256
LANES = 128
HALO = 96
LEAD = 16

LOW = np.array(
    [
        -0.010597401784997278,
        0.032883011666982945,
        0.030841381835986965,
        -0.18703481171888114,
        -0.02798376941698385,
        0.6308807679295904,
        0.7148465705525415,
        0.23037781330885523,
    ]
)
HIGH = np.array([(-1.0) ** j * LOW[7 - j] for j in range(8)])


def lattice_factors():
    a = np.array([(LOW[2 * (3 - j)], LOW[2 * (3 - j) + 1]) for j in range(4)])
    b = np.array([(HIGH[2 * (3 - j)], HIGH[2 * (3 - j) + 1]) for j in range(4)])
    factors = {}
    for s in (3, 2, 1):
        k = (a[s] @ b[s]) / (b[s] @ b[s])
        a, b = (a - k * b) / (1 + k * k), (k * a + b) / (1 + k * k)
        a, b = a[:s], b[1 : s + 1]
        factors[s] = float(k)
    factors[0] = float(a[0][1] / a[0][0])
    return factors, float(a[0][0]), float(np.sign(b[0][1] / a[0][0]))


TURN, SCALE, SIGN = lattice_factors()
F32 = jnp.float32
BF16 = jnp.bfloat16


def two_terms(value):
    top = value.astype(BF16)
    return top, (value - top.astype(F32)).astype(BF16)


def masked_rows(matrix, start, count, lat, lats):
    row = lax.broadcasted_iota(jnp.int32, matrix.shape, 0) + (start + lat * count)
    return jnp.where((row >= 0) & (row < count * lats), matrix, 0.0)


def banded(shape, low, high, row_factor, column_factor, offset):
    row = lax.broadcasted_iota(jnp.int32, shape, 0)
    column = lax.broadcasted_iota(jnp.int32, shape, 1)
    tap = row_factor * row + column_factor * column + offset
    if high is not None:
        second = column >= shape[1] // 2
        tap = jnp.where(second, tap - column_factor * (shape[1] // 2), tap)
    matrix = jnp.zeros(shape, F32)
    for t in range(8):
        value = F32(low[t]) if high is None else jnp.where(second, F32(high[t]), F32(low[t]))
        matrix = jnp.where(tap == t, value, matrix)
    return matrix


def analysis_matrix(taps, out_start, out_rows, in_start, in_rows):
    return banded((out_rows, in_rows), taps, None, -2, 1, in_start + 3 - 2 * out_start)


def synthesis_matrix(out_start, out_rows, in_start, in_rows):
    shape = (out_rows, 2 * in_rows)
    return banded(shape, SCALE * LOW, SCALE * HIGH, 1, -2, out_start - 2 * in_start + 3)


def mxu(a, b):
    return jnp.dot(a, b, preferred_element_type=F32)


def dot3(matrix, vh, vl):
    mh, ml = two_terms(matrix)
    return mxu(mh, vh) + mxu(mh, vl) + mxu(ml, vh)


def first_half(rows):
    return lax.broadcasted_iota(jnp.int32, (rows, LANES), 1) < C


def half_turn(value):
    return None if value is None else pltpu.roll(value, C, 1)


def pick(left, a, b):
    if a is None and b is None:
        return None
    return jnp.where(left, 0.0 if a is None else a, 0.0 if b is None else b)


def plus(a, b, factor):
    if b is None:
        return a
    if a is None:
        return b * factor
    return a + b * factor


class Memo:
    def __init__(self, make):
        self.make, self.known = make, {}

    def __call__(self, n):
        if n not in self.known:
            self.known[n] = self.make(n)
        return self.known[n]


def analysis(cols, start, left):
    turned = Memo(lambda i: half_turn(cols[i]) if 0 <= i < len(cols) else None)
    plain = lambda i: cols[i] if 0 <= i < len(cols) else None
    if start % 2 == 0:
        at = lambda n: n - 1 - start // 2
        u = Memo(lambda n: pick(left, turned(at(n) - 1), plain(at(n))))
        w = Memo(lambda n: pick(left, plain(at(n)), turned(at(n) + 1)))
    else:
        at = lambda n: n - (start + 3) // 2
        u = Memo(lambda n: pick(left, plain(at(n)), turned(at(n) + 1)))
        w = Memo(lambda n: pick(left, turned(at(n)), plain(at(n) + 1)))

    def band(taps):
        def make(k):
            total = None
            for step in range(4):
                total = plus(total, u(k + step), float(taps[2 * step]))
                total = plus(total, w(k + step), float(taps[2 * step + 1]))
            return total

        return make

    return band(LOW), band(HIGH)


def synthesis(lows, highs, start, left):
    def cells(cols):
        if cols is None:
            return lambda n: None
        return lambda n: cols[(n - 3 - start) // 2] if 0 <= n - 3 - start < 2 * len(cols) else None

    a, b = cells(lows), cells(highs)

    def stage(a, b, factor):
        early = Memo(lambda n: half_turn(plus(b(n), a(n), factor)))
        return (
            Memo(lambda n: plus(a(n), b(n), -factor)),
            Memo(lambda n: pick(left, early(n), early(n + 2))),
        )

    for s in (3, 2, 1):
        a, b = stage(a, b, TURN[s])
    last_a, last_b = a, b
    u = Memo(lambda n: plus(last_a(n), last_b(n), -TURN[0] * SIGN))
    if SIGN < 0:
        w = Memo(lambda n: plus(last_a(n) * TURN[0] if last_a(n) is not None else None, last_b(n), -1.0))
    else:
        w = Memo(lambda n: plus(last_b(n), last_a(n), TURN[0]))
    u_turned, w_turned = Memo(lambda n: half_turn(u(n))), Memo(lambda n: half_turn(w(n)))
    parity = (start + 3) % 2

    def pair(m):
        if m % 2:
            n = (m + 3) // 2
            if n % 2 == parity:
                return pick(left, u(n), w_turned(n))
            return pick(left, u_turned(n - 1), w(n - 1))
        n = m // 2 + 1
        if n % 2 == parity:
            return pick(left, w(n), u(n))
        return pick(left, w_turned(n - 1), u_turned(n + 1))

    return pair


def columns(ref, row, rows, count=None):
    count = ref.shape[-1] // LANES if count is None else count
    return [ref[pl.ds(row, rows), pl.ds(LANES * p, LANES)] for p in range(count)]


def put(ref, row, p, value, lead=()):
    ref[lead + (pl.ds(row, value.shape[0]), pl.ds(LANES * p, LANES))] = value


class Geometry:
    def __init__(self, rows, cells):
        self.rows = [rows >> level for level in range(5)]
        self.cells = [cells >> level for level in range(5)]
        up = lambda value, step: -(-value // step) * step
        self.band = [
            None,
            (-4, up(self.rows[1] + 4, 120)),
            (-8, up(self.rows[2] + 11, 16)),
            (-3, up(self.rows[3] + 6, 8)),
            (-3, up(self.rows[4] + 6, 8)),
        ]
        self.low = [
            None,
            (-52, up(self.rows[1] + 97, 112)),
            (-24, up(self.rows[2] + 45, 88)),
            (-11, up(self.rows[3] + 20, 8)),
            (-3, up(self.rows[4] + 6, 8)),
        ]
        self.span = [None, (-2, self.cells[1] // 2 + 2)]
        for level in (2, 3, 4):
            self.span.append((-3, self.cells[level] // 2 + 3))
        self.extended = max(
            LEAD + 2 * HALO + rows, 2 * (self.low[1][1] - 112) + 256
        )


STEP = 240
SIDE = 8
NEAR = 16


def best_step(rows, most=None):
    return max(s for s in range(8, (most or STEP) + 1, 8) if rows % s == 0)


def low_rows(geo, level, source, source_start, target):
    first, pairs = geo.span[level]
    rows = geo.low[level][1]
    step = best_step(rows, 168)
    left = first_half(step)

    def body(c, carry):
        row = pl.multiple_of(c * step, step)
        low, _ = analysis(columns(source, row, step), source_start, left)
        for q in range(pairs):
            put(target, row, q, low(first + 2 * q))
        return carry

    lax.fori_loop(0, rows // step, body, 0)


def band_rows(geo, level, lo, skip, hi, source_start, gain, bands):
    first, pairs = geo.span[level]
    rows = geo.band[level][1]
    step = best_step(rows)
    left = first_half(step)

    def body(c, carry):
        row = pl.multiple_of(c * step, step)
        g = []
        for b in range(3):
            one = gain[level - 1, b : b + 1, :]
            g.append(jnp.broadcast_to(jnp.concatenate([one, one], 1), (step, LANES)))
        _, high = analysis(columns(lo, row + skip, step), source_start, left)
        for q in range(pairs):
            put(bands, row, q, high(first + 2 * q) * g[0], (0,))
        low, high = analysis(columns(hi, row, step), source_start, left)
        for q in range(pairs):
            put(bands, row, q, low(first + 2 * q) * g[1], (1,))
            put(bands, row, q, high(first + 2 * q) * g[2], (2,))
        return carry

    lax.fori_loop(0, rows // step, body, 0)


def analysis_kernel(geo, lats, place, edge, gain, x, *refs):
    lat, parity = place[0], place[1] % 2
    ll4, out2, out3, out4, send_e, send_o, p2, m2, p3, m3 = refs[:10]
    ext, la, g1, gh, gl, lo2, g2, lo3, g3, lo4, hi2, hi3, hi4, d2, d3, d4, sems, out_sems = refs[10:]
    outs = {2: (d2, out2), 3: (d3, out3), 4: (d4, out4)}
    rows = geo.rows[0]
    start, count = geo.low[1]
    width = x.shape[1]
    begin = LEAD + HALO
    blocks = count // 112
    cuts = [0] + [min(rows, 224 * b + 256 - begin) for b in range(blocks - 1)] + [rows]
    copies = []
    for i in range(blocks):
        part = pl.ds(cuts[i], cuts[i + 1] - cuts[i])
        to = pl.ds(begin + cuts[i], cuts[i + 1] - cuts[i])
        copies.append(pltpu.make_async_copy(x.at[part, :], ext.at[to, :], sems.at[i]))
        copies[-1].start()
    top = slice(LEAD, begin)
    bottom = slice(begin + rows, begin + rows + HALO)
    ext[0:LEAD, :] = jnp.zeros((LEAD, width), BF16)
    tail = geo.extended - (LEAD + 2 * HALO + rows)
    if tail:
        ext[geo.extended - tail :, :] = jnp.zeros((tail, width), BF16)

    @pl.when(lat == 0)
    def _():
        ext[top, :] = jnp.zeros((HALO, width), BF16)
        ext[bottom, :] = edge[...]

    @pl.when(lat != 0)
    def _():
        ext[top, :] = edge[...]
        ext[bottom, :] = jnp.zeros((HALO, width), BF16)

    base = analysis_matrix(LOW, start, 112, 0 - LEAD - HALO, 256)
    for b in range(blocks):
        copies[b].wait()
        mh, ml = two_terms(masked_rows(base, start + 112 * b, geo.rows[1], lat, lats))
        data = ext[224 * b : 224 * b + 256, :]
        la[112 * b : 112 * b + 112, :] = mxu(mh, data) + mxu(ml, data)
    low_rows(geo, 1, la, 0, g1)
    gh[...], gl[...] = two_terms(g1[...])
    out_start, out_rows = geo.low[2]
    for b in range(out_rows // 88):
        at = min(176 * b, count - 192)
        window = slice(at, at + 192)
        matrix = analysis_matrix(LOW, out_start + 88 * b, 88, start + at, 192)
        matrix = masked_rows(matrix, out_start + 88 * b, geo.rows[2], lat, lats)
        lo2[88 * b : 88 * b + 88, :] = dot3(matrix, gh[window, :], gl[window, :])
    low_rows(geo, 2, lo2, geo.span[1][0], g2)
    for level, source, lo, target in ((3, g2, lo3, g3), (4, g3, lo4, ll4)):
        vh, vl = two_terms(source[...])
        matrix = analysis_matrix(LOW, *geo.low[level], *geo.low[level - 1])
        matrix = masked_rows(matrix, geo.low[level][0], geo.rows[level], lat, lats)
        lo[...] = dot3(matrix, vh, vl)
        low_rows(geo, level, lo, geo.span[level - 1][0], target)
    copies = []
    for level, lo, hi in ((2, lo2, hi2), (3, lo3, hi3), (4, lo4, hi4)):
        deep_bands(geo, lats, lat, level, {2: (gh, gl), 3: g2, 4: g3}[level], lo, hi, gain, outs[level][0])
        copies.append(pltpu.make_async_copy(*outs[level], out_sems.at[level - 2]))
        copies[-1].start()
    d = {2: d2, 3: d3, 4: d4}

    def fill(distance, to_left, to_right):
        for level, count, row in exchange_plan(geo)[distance]:
            n = geo.band[level][1]
            move = distance * geo.cells[level] // 2
            for b in range(3):
                lanes = slice(b * count * LANES, (b + 1) * count * LANES)
                to_left[row : row + n, lanes] = d[level][b, :, 0 : count * LANES].astype(BF16)
                to_right[row : row + n, lanes] = d[level][
                    b, :, move * LANES : (move + count) * LANES
                ].astype(BF16)

    @pl.when(parity == 0)
    def _():
        fill(1, send_o, send_e)

    @pl.when(parity != 0)
    def _():
        fill(1, send_e, send_o)

    fill(2, m2, p2)
    fill(3, m3, p3)
    for copy in copies:
        copy.wait()


def deep_bands(geo, lats, lat, level, source, lo, hi, gain, bands):
    start, count = geo.band[level]
    in_start = geo.low[level - 1][0]
    parts = 2 if level == 2 else 1
    half = count // parts
    for b in range(parts):
        if parts == 1:
            at, size = 0, source.shape[0]
            vh, vl = two_terms(source[...])
        else:
            at = (2 * (start + half * b) - 3 - in_start) // 16 * 16
            size = 2 * half + 16
            vh, vl = source[0][at : at + size, :], source[1][at : at + size, :]
        matrix = analysis_matrix(HIGH, start + half * b, half, in_start + at, size)
        matrix = masked_rows(matrix, start + half * b, geo.rows[level], lat, lats)
        hi[half * b : half * (b + 1), :] = dot3(matrix, vh, vl)
    skip = start - geo.low[level][0]
    band_rows(geo, level, lo, skip, hi, geo.span[level - 1][0], gain, bands)


def sides_kernel(place, x, side_e, side_o, sems):
    parity = place[1] % 2
    width, lanes = x.shape[1], side_e.shape[1]

    def both(low, high):
        copies = [
            pltpu.make_async_copy(x.at[:, pl.ds(0, lanes)], low, sems.at[0]),
            pltpu.make_async_copy(x.at[:, pl.ds(width - lanes, lanes)], high, sems.at[1]),
        ]
        for copy in copies:
            copy.start()
        for copy in copies:
            copy.wait()

    @pl.when(parity == 0)
    def _():
        both(side_o, side_e)

    @pl.when(parity != 0)
    def _():
        both(side_e, side_o)


def corners_kernel(place, side_e, side_o, out):
    lat, parity = place[0], place[1] % 2
    rows, lanes = side_e.shape
    at = jnp.where(lat == 0, rows - NEAR, 0)
    window = pl.ds(pl.multiple_of(at, NEAR), NEAR)

    @pl.when(parity == 0)
    def _():
        out[:, 0:lanes] = side_o[window, :]
        out[:, lanes:] = side_e[window, :]

    @pl.when(parity != 0)
    def _():
        out[:, 0:lanes] = side_e[window, :]
        out[:, lanes:] = side_o[window, :]


def ring_kernel(geo, flip, place, mine, other, ring, line):
    width, total = mine.shape[1], ring.shape[1]
    fold = line.shape[1] - total
    line[...] = jnp.zeros(line.shape, F32)
    lon = place[1]
    for part, where in ((mine, lon), (other, lon ^ flip)):
        at = pl.ds(pl.multiple_of(where * (geo.cells[4] * C), LANES), width)
        line[:, at] = line[:, at] + part[...]
    ring[:, 0:fold] = line[:, 0:fold] + line[:, total:]
    ring[:, fold:] = line[:, fold:total]


def add_kernel(geo, place, mine, other, ring, tokens):
    ring[...] = mine[...] + other[...]
    skip = -geo.low[4][0]
    tokens[...] = ring[skip : skip + geo.rows[4], :].astype(BF16)


def first_level_kernel(geo, lats, place, edge, side_e, side_o, corner, gain, x, held, ext, la, ha, d1, xh, xl, part, sem):
    lat, parity = place[0], place[1] % 2
    rows, width = x.shape
    lanes = SIDE * C
    copy = pltpu.make_async_copy(x, ext.at[pl.ds(NEAR, rows), pl.ds(lanes, width)], sem)
    copy.start()
    sides = (slice(0, lanes), slice(lanes + width, width + 2 * lanes))
    own = slice(lanes, lanes + width)
    inner = slice(NEAR, NEAR + rows)

    def rims(near, far, edges):
        ext[far, :] = jnp.zeros((NEAR, width + 2 * lanes), BF16)
        ext[near, own] = edges
        ext[near, sides[0]] = corner[:, 0:lanes]
        ext[near, sides[1]] = corner[:, lanes:]

    top, bottom = slice(0, NEAR), slice(NEAR + rows, 2 * NEAR + rows)

    @pl.when(lat == 0)
    def _():
        rims(bottom, top, edge[0:NEAR, :])

    @pl.when(lat != 0)
    def _():
        rims(top, bottom, edge[HALO - NEAR :, :])

    @pl.when(parity == 0)
    def _():
        ext[inner, sides[0]] = side_o[...]
        ext[inner, sides[1]] = side_e[...]

    @pl.when(parity != 0)
    def _():
        ext[inner, sides[0]] = side_e[...]
        ext[inner, sides[1]] = side_o[...]

    start, count = geo.band[1]
    low = analysis_matrix(LOW, start, 120, -NEAR, 256)
    high = analysis_matrix(HIGH, start, 120, -NEAR, 256)
    copy.wait()
    for b in range(count // 120):
        data = ext[240 * b : 240 * b + 256, :]
        for matrix, out in ((low, la), (high, ha)):
            mh, ml = two_terms(masked_rows(matrix, start + 120 * b, geo.rows[1], lat, lats))
            out[120 * b : 120 * b + 120, :] = mxu(mh, data) + mxu(ml, data)
    band_rows(geo, 1, la, 0, ha, -SIDE, gain, d1)
    half = rows // 2
    ylow, yhigh = la, ha
    used = slice(0, d1.shape[2])
    for block in range(2):
        w = 0 if block == 0 else count - LANES
        window = slice(w, w + LANES)
        target = slice(half * block, half * (block + 1))
        matrix = synthesis_matrix(half * block, half, start + w, LANES)
        sh, sl = two_terms(matrix)
        xh[0:LANES, :], xl[0:LANES, :] = two_terms(d1[0, window, :])
        xh[LANES:, :], xl[LANES:, :] = two_terms(d1[2, window, :])
        yhigh[target, used] = mxu(sh, xh[...]) + mxu(sh, xl[...]) + mxu(sl, xh[...])
        vh, vl = two_terms(d1[1, window, :])
        sh, sl = sh[:, LANES:], sl[:, LANES:]
        ylow[target, used] = mxu(sh, vh) + mxu(sh, vl) + mxu(sl, vh)

    begin, pairs = geo.span[1]
    most = 232

    def chunk(i, carry):
        row = pl.multiple_of(i * most, 8)
        pair = synthesis(
            columns(ylow, row, most, pairs), columns(yhigh, row, most, pairs), begin, first_half(most)
        )
        for q in range(geo.cells[0] // 2):
            put(part, row, q, pair(2 * q))
        copy = pltpu.make_async_copy(part.at[pl.ds(row, most), :], held.at[pl.ds(row, most), :], sem)
        copy.start()
        copy.wait()
        return carry

    lax.fori_loop(0, rows // most, chunk, 0)


def exchange_plan(geo):
    plan = {}
    for distance in (1, 2, 3):
        entries, row = [], 0
        for level in (2, 3, 4):
            count = geo.span[level][1] - distance * geo.cells[level] // 2
            if count > 0:
                entries.append((level, count, row))
                row += -(-geo.band[level][1] // 16) * 16
        plan[distance] = entries
    return plan


def plan_shape(geo, distance):
    entries = exchange_plan(geo)[distance]
    rows = sum(-(-geo.band[level][1] // 16) * 16 for level, _, _ in entries)
    return (rows, max(count for _, count, _ in entries) * 3 * LANES)


def attention_kernel(geo, lats, blocks, place, ring, own, others, we, wqkv, scale, wo, gain, wb, out, around, listed, keys):
    lat, lon = place[0], place[1]
    rows, width = out.shape
    cells = width // C
    total = ring.shape[1]
    around[:, 0:total] = ring[...]
    around[:, total:] = ring[:, 0 : around.shape[1] - total]
    field = around[:, pl.ds(pl.multiple_of(lon * (geo.cells[4] * C), LANES), width)]
    count = geo.rows[4]
    for source, shift in ((own, 0), (others, count)):
        for pair in range(total // LANES):
            value = source[:, pair * LANES : (pair + 1) * LANES].astype(F32)
            for side in range(2):
                at = 2 * count * (2 * pair + side) + shift
                listed[at : at + count, :] = value[:, side * C : (side + 1) * C]
    keys[...] = listed[...].astype(BF16)
    own = jnp.concatenate([field[:, C * c : C * (c + 1)] for c in range(cells)], 0)
    count = own.shape[0]
    embedded = mxu(own.astype(BF16), we[...])
    queries = mxu(embedded.astype(BF16), wqkv[:, 0:E]).astype(BF16)
    lane = lax.broadcasted_iota(jnp.int32, (1, E), 1)
    block = keys.shape[0] // blocks
    factor = [scale[h] * (1.0 / math.sqrt(HEAD_DIM)) for h in range(HEADS)]

    def keyvals(start):
        spread = mxu(keys[pl.ds(start, block), :], we[...]).astype(BF16)
        both = mxu(spread, wqkv[:, E : 3 * E]).astype(BF16)
        return both[:, 0:E], both[:, E : 2 * E]

    def scores_of(h, k):
        mine = (lane >= h * HEAD_DIM) & (lane < (h + 1) * HEAD_DIM)
        q = jnp.where(mine, queries, jnp.zeros_like(queries))
        s = lax.dot_general(q, k, (((1,), (1,)), ((), ())), preferred_element_type=F32)
        return s * factor[h]

    def masked(h, value):
        mine = (lane >= h * HEAD_DIM) & (lane < (h + 1) * HEAD_DIM)
        return jnp.where(mine, value, jnp.zeros_like(value))

    if blocks == 1:
        k, v = keyvals(0)
        attended = jnp.zeros((count, E), F32)
        for h in range(HEADS):
            s = scores_of(h, k)
            w = jnp.exp(s - jnp.max(s, -1, keepdims=True))
            total = jnp.sum(w, -1, keepdims=True)
            attended = attended + masked(h, mxu(w.astype(BF16), v) / total)
    else:

        def one_block(b, carry):
            peaks, totals, sums = carry
            k, v = keyvals(pl.multiple_of(b * block, 16))
            new_peaks, new_totals = [], []
            shrunk = jnp.zeros((count, E), F32)
            for h in range(HEADS):
                s = scores_of(h, k)
                peak = jnp.maximum(peaks[h], jnp.max(s, -1, keepdims=True))
                shrink = jnp.exp(peaks[h] - peak)
                w = jnp.exp(s - peak)
                new_peaks.append(peak)
                new_totals.append(totals[h] * shrink + jnp.sum(w, -1, keepdims=True))
                shrunk = shrunk + masked(h, sums * shrink + mxu(w.astype(BF16), v))
            return tuple(new_peaks), tuple(new_totals), shrunk

        start = (
            tuple(jnp.full((count, 1), -1e30, F32) for _ in range(HEADS)),
            tuple(jnp.zeros((count, 1), F32) for _ in range(HEADS)),
            jnp.zeros((count, E), F32),
        )
        _, totals, sums = lax.fori_loop(0, blocks, one_block, start)
        attended = jnp.zeros((count, E), F32)
        for h in range(HEADS):
            attended = attended + masked(h, sums / totals[h])
    hidden = embedded + mxu(attended.astype(BF16), wo[...])
    square = jnp.mean(hidden * hidden, -1, keepdims=True)
    normed = (hidden * lax.rsqrt(square + 1e-06) * gain[...]).astype(BF16)
    update = lax.dot_general(
        normed, wb[...], (((1,), (1,)), ((), ())), preferred_element_type=F32
    )
    back = [
        jnp.concatenate(
            [update[rows * c : rows * (c + 1), :], update[rows * (c + 1) : rows * (c + 2), :]], 1
        )
        for c in range(0, cells, 2)
    ]
    start = geo.band[4][0]
    for q, value in enumerate(back):
        at = slice(q * LANES, (q + 1) * LANES)
        out[:, at] = masked_rows(field[:, at] + value, start, geo.rows[4], lat, lats)


def synthesis_kernel(geo, lats, place, coarse, e2, o2, from_m2, from_p2, from_m3, from_p3, *refs):
    lat, parity = place[0], place[1] % 2
    held, (out, up3, up2, up1, ylow, yhigh, done), refs = refs[:4], refs[4:11], refs[11:]
    part, d2, d3, d4, sems, in_sems = refs
    arrive = [
        pltpu.make_async_copy(source, to, in_sems.at[i])
        for i, (source, to) in enumerate(zip(held, (part, d2, d3, d4)))
    ]
    for level in (4, 3, 2, 1):
        arrive[level - 1].start()
    bands = {2: d2, 3: d3, 4: d4}
    plan = exchange_plan(geo)

    def from_sides(level, b):
        n = geo.band[level][1]
        cols = [bands[level][b, :, LANES * p : LANES * (p + 1)] for p in range(geo.span[level][1])]
        for distance in (1, 2, 3):
            for which, count, row in plan[distance]:
                if which != level:
                    continue
                move = distance * geo.cells[level] // 2
                for p in range(count):
                    lanes = slice((b * count + p) * LANES, (b * count + p + 1) * LANES)
                    if distance == 1:
                        even = e2[row : row + n, lanes].astype(F32)
                        odd = o2[row : row + n, lanes].astype(F32)
                        low = jnp.where(parity == 0, odd, even)
                        high = jnp.where(parity == 0, even, odd)
                    else:
                        lows, highs = {2: (from_m2, from_p2), 3: (from_m3, from_p3)}[distance]
                        low = lows[row : row + n, lanes].astype(F32)
                        high = highs[row : row + n, lanes].astype(F32)
                    cols[p] = cols[p] + low
                    cols[p + move] = cols[p + move] + high
        return jnp.concatenate(cols, 1)

    uppers = {4: coarse, 3: up3, 2: up2, 1: up1}
    for level in (4, 3, 2):
        arrive[level - 1].wait()
        begin, pairs = geo.span[level]
        below = level - 1
        start, rows = geo.band[below]
        matrix = synthesis_matrix(start, rows, *geo.band[level])
        matrix = masked_rows(matrix, start, geo.rows[below], lat, lats)
        width = pairs * LANES
        for one, two, y in (
            (uppers[level][...], from_sides(level, 1), ylow),
            (from_sides(level, 0), from_sides(level, 2), yhigh),
        ):
            h, l = two_terms(jnp.concatenate([one, two], 0))
            y[0:rows, 0:width] = dot3(matrix, h, l)
        target = uppers[below]
        first, out_pairs = geo.span[below]

        step = best_step(rows)
        left = first_half(step)

        def joined(c, carry):
            row = pl.multiple_of(c * step, step)
            pair = synthesis(
                columns(ylow, row, step, pairs), columns(yhigh, row, step, pairs), begin, left
            )
            for q in range(out_pairs):
                put(target, row, q, pair(first + 2 * q))
            return carry

        lax.fori_loop(0, rows // step, joined, 0)

    n = geo.band[1][1]
    half = geo.rows[0] // 2
    for block in range(2):
        w = 0 if block == 0 else n - LANES
        matrix = synthesis_matrix(half * block, half, geo.band[1][0] + w, LANES)
        h, l = two_terms(up1[w : w + LANES, :])
        ylow[half * block : half * (block + 1), :] = dot3(matrix[:, 0:LANES], h, l)
    arrive[0].wait()
    begin, pairs = geo.span[1]
    most = 112

    def last(row, count):
        left = first_half(count)
        pair = synthesis(columns(ylow, row, count), None, begin, left)
        for q in range(geo.cells[0] // 2):
            more = part[pl.ds(row, count), pl.ds(LANES * q, LANES)]
            put(done, row, q, (pair(2 * q) + more).astype(BF16))

    def store(i, count):
        part = pl.ds(pl.multiple_of(i * most, 16), count)
        return pltpu.make_async_copy(done.at[part, :], out.at[part, :], sems.at[i])

    whole, rest = geo.rows[0] // most, geo.rows[0] % most

    def chunk(i, carry):
        last(pl.multiple_of(i * most, 16), most)
        store(i, most).start()
        return carry

    lax.fori_loop(0, whole, chunk, 0)
    if rest:
        last(whole * most, rest)
        store(whole, rest).start()
    for i in range(whole):
        store(i, most).wait()
    if rest:
        store(whole, rest).wait()


def call(kernel, out_shape, scratch, *args, cost=20_000_000, grant=24, raw=(), raw_out=()):
    vmem = pl.BlockSpec(memory_space=pltpu.VMEM)
    smem = pl.BlockSpec(memory_space=pltpu.SMEM)
    anywhere = pl.BlockSpec(memory_space=pl.ANY)
    specs = [smem if a.ndim == 1 and a.size < 16 else vmem for a in args]
    for at in raw:
        specs[at] = anywhere
    outs = [anywhere if i in raw_out else vmem for i in range(len(out_shape))]
    return pl.pallas_call(
        kernel,
        out_shape=tuple(out_shape),
        in_specs=specs,
        out_specs=tuple(outs),
        scratch_shapes=scratch,
        compiler_params=pltpu.CompilerParams(vmem_limit_bytes=grant << 20),
        cost_estimate=pl.CostEstimate(flops=cost, bytes_accessed=1 << 20, transcendentals=0),
    )(*args)


def shape(dims, dtype=F32):
    return jax.ShapeDtypeStruct(dims, dtype)


def per_device(mesh_shape, state_field, skip_gain, embed_weight, qkv_weight, head_scale, out_weight, norm_gain, back_weight):
    return program(
        mesh_shape, state_field, skip_gain, embed_weight, qkv_weight, head_scale, out_weight, norm_gain, back_weight
    )


def program(mesh_shape, state_field, skip_gain, embed_weight, qkv_weight, head_scale, out_weight, norm_gain, back_weight):
    lons, lats = mesh_shape["lon"], mesh_shape["lat"]
    rows, width = state_field.shape
    geo = Geometry(rows, width // C)
    lat, lon = lax.axis_index("lat"), lax.axis_index("lon")
    place = jnp.stack([lat, lon]).astype(jnp.int32)

    even_pairs = [(i, i ^ 1) for i in range(lons)]
    odd_pairs = [(i, (i + 1 if i % 2 else i - 1) % lons) for i in range(lons)]
    swap = [(i, lats - 1 - i) for i in range(lats)]

    def shifted(value, by):
        return lax.ppermute(value, "lon", [(i, (i + by) % lons) for i in range(lons)])

    edge = lax.dynamic_slice(
        state_field, (jnp.where(lat == 0, rows - HALO, 0), 0), (HALO, width)
    )
    edge = lax.ppermute(edge, "lat", swap)

    wide = SIDE * C
    extended = NEAR + rows + NEAR
    side_e, side_o = call(
        sides_kernel,
        [shape((rows, wide), BF16)] * 2,
        [pltpu.SemaphoreType.DMA((2,))],
        place,
        state_field,
        raw=(1,),
        cost=1_000_000,
    )
    side_e = lax.ppermute(side_e, "lon", even_pairs)
    side_o = lax.ppermute(side_o, "lon", odd_pairs)

    w = [None] + [geo.span[level][1] * LANES for level in (1, 2, 3, 4)]
    low = lambda level, lanes: pltpu.VMEM((geo.low[level][1], w[lanes]), F32)
    bands = [(3, geo.band[level][1], w[level]) for level in (1, 2, 3, 4)]
    ll4, d2, d3, d4, deep_e, deep_o, p2, m2, p3, m3 = call(
        functools.partial(analysis_kernel, geo, lats),
        [shape((geo.low[4][1], w[4]))]
        + [shape(dims) for dims in bands[1:]]
        + [shape(plan_shape(geo, d), BF16) for d in (1, 1, 2, 2, 3, 3)],
        [
            pltpu.VMEM((geo.extended, width), BF16),
            pltpu.VMEM((geo.low[1][1], width), F32),
            low(1, 1),
            pltpu.VMEM((geo.low[1][1], w[1]), BF16),
            pltpu.VMEM((geo.low[1][1], w[1]), BF16),
            low(2, 1),
            low(2, 2),
            low(3, 2),
            low(3, 3),
            low(4, 3),
        ]
        + [pltpu.VMEM((geo.band[level][1], w[level - 1]), F32) for level in (2, 3, 4)]
        + [pltpu.VMEM(dims, F32) for dims in bands[1:]]
        + [
            pltpu.SemaphoreType.DMA((geo.low[1][1] // 112,)),
            pltpu.SemaphoreType.DMA((3,)),
        ],
        place,
        edge,
        skip_gain,
        state_field,
        raw=(3,),
        raw_out=(1, 2, 3),
    )
    (corner,) = call(
        corners_kernel, [shape((NEAR, 2 * wide), BF16)], [], place, side_e, side_o, cost=100_000
    )
    corner = lax.ppermute(corner, "lat", swap)
    (part,) = call(
        functools.partial(first_level_kernel, geo, lats),
        [shape((rows, width))],
        [
            pltpu.VMEM((extended, width + 2 * wide), BF16),
            pltpu.VMEM((rows, width + 2 * wide), F32),
            pltpu.VMEM((rows, width + 2 * wide), F32),
            pltpu.VMEM(bands[0], F32),
            pltpu.VMEM((2 * LANES, w[1]), BF16),
            pltpu.VMEM((2 * LANES, w[1]), BF16),
            pltpu.VMEM((rows, width), F32),
            pltpu.SemaphoreType.DMA,
        ],
        place,
        edge,
        side_e,
        side_o,
        corner,
        skip_gain,
        state_field,
        raw=(6,),
        raw_out=(0,),
        grant=40,
    )

    total = geo.cells[4] * lons * C
    flip = lons // 2
    other = lax.ppermute(ll4, "lon", [(i, i ^ flip) for i in range(lons)])
    (ring,) = call(
        functools.partial(ring_kernel, geo, flip),
        [shape((ll4.shape[0], total))],
        [pltpu.VMEM((ll4.shape[0], total + 6 * C), F32)],
        place,
        ll4,
        other,
        cost=100_000,
    )
    while flip > 1:
        flip = flip // 2
        other = lax.ppermute(ring, "lon", [(i, i ^ flip) for i in range(lons)])
        ring, tokens = call(
            functools.partial(add_kernel, geo),
            [shape(ring.shape), shape((geo.rows[4], total), BF16)],
            [],
            place,
            ring,
            other,
            cost=100_000,
        )
    others = lax.ppermute(tokens, "lat", swap)

    deep_e = lax.ppermute(deep_e, "lon", even_pairs)
    deep_o = lax.ppermute(deep_o, "lon", odd_pairs)
    from_m2, from_p2 = shifted(p2, 2), shifted(m2, -2)
    from_m3, from_p3 = shifted(p3, 3), shifted(m3, -3)

    key_count = 2 * geo.rows[4] * geo.cells[4] * lons
    blocks = key_count // 928 if key_count % 928 == 0 else 1
    (coarse,) = call(
        functools.partial(attention_kernel, geo, lats, blocks),
        [shape((geo.low[4][1], w[4]))],
        [
            pltpu.VMEM((geo.low[4][1], total + 6 * C), F32),
            pltpu.VMEM((key_count, C), F32),
            pltpu.VMEM((key_count, C), BF16),
        ],
        place,
        ring,
        tokens,
        others,
        embed_weight,
        qkv_weight,
        head_scale,
        out_weight,
        norm_gain[None],
        back_weight.T,
        cost=200_000_000,
        grant=40,
    )

    (out,) = call(
        functools.partial(synthesis_kernel, geo, lats),
        [shape((rows, width), BF16)],
        [pltpu.VMEM((geo.band[level][1], w[level]), F32) for level in (3, 2, 1)]
        + [
            pltpu.VMEM((rows, w[1]), F32),
            pltpu.VMEM((geo.band[1][1], w[2]), F32),
            pltpu.VMEM((rows, width), BF16),
            pltpu.VMEM((rows, width), F32),
        ]
        + [pltpu.VMEM(dims, F32) for dims in bands[1:]]
        + [
            pltpu.SemaphoreType.DMA((rows // 112 + 1,)),
            pltpu.SemaphoreType.DMA((4,)),
        ],
        place,
        coarse,
        deep_e,
        deep_o,
        from_m2,
        from_p2,
        from_m3,
        from_p3,
        part,
        d2,
        d3,
        d4,
        raw=(8, 9, 10, 11),
        raw_out=(0,),
        grant=40,
    )
    return out


def solution(mesh):
    in_specs = (P("lat", ("member", "lon")), P(), P(), P(), P(), P(), P(), P())
    out_specs = P("lat", ("member", "lon"))
    return jax.shard_map(
        functools.partial(per_device, dict(mesh.shape)),
        mesh=mesh,
        in_specs=in_specs,
        out_specs=out_specs,
        check_vma=False,
    )
```

```python
import functools
import math

import jax
import jax.numpy as jnp
import numpy as np
from jax import lax
from jax.experimental import pallas as pl
from jax.experimental.pallas import tpu as pltpu
from jax.sharding import PartitionSpec as P


C = 64
HEADS = 8
HEAD_DIM = 32
E = 256
LANES = 128
HALO = 96
LEAD = 16

LOW = np.array(
    [
        -0.010597401784997278,
        0.032883011666982945,
        0.030841381835986965,
        -0.18703481171888114,
        -0.02798376941698385,
        0.6308807679295904,
        0.7148465705525415,
        0.23037781330885523,
    ]
)
HIGH = np.array([(-1.0) ** j * LOW[7 - j] for j in range(8)])


F32 = jnp.float32
BF16 = jnp.bfloat16


def two_terms(value):
    top = value.astype(BF16)
    return top, (value - top.astype(F32)).astype(BF16)


def masked_rows(matrix, start, count, lat, lats):
    row = lax.broadcasted_iota(jnp.int32, matrix.shape, 0) + (start + lat * count)
    return jnp.where((row >= 0) & (row < count * lats), matrix, 0.0)


def banded(shape, low, high, row_factor, column_factor, offset):
    row = lax.broadcasted_iota(jnp.int32, shape, 0)
    column = lax.broadcasted_iota(jnp.int32, shape, 1)
    tap = row_factor * row + column_factor * column + offset
    if high is not None:
        second = column >= shape[1] // 2
        tap = jnp.where(second, tap - column_factor * (shape[1] // 2), tap)
    matrix = jnp.zeros(shape, F32)
    for t in range(8):
        value = F32(low[t]) if high is None else jnp.where(second, F32(high[t]), F32(low[t]))
        matrix = jnp.where(tap == t, value, matrix)
    return matrix


def analysis_matrix(taps, out_start, out_rows, in_start, in_rows):
    return banded((out_rows, in_rows), taps, None, -2, 1, in_start + 3 - 2 * out_start)


def synthesis_matrix(out_start, out_rows, in_start, in_rows):
    shape = (out_rows, 2 * in_rows)
    return banded(shape, LOW, HIGH, 1, -2, out_start - 2 * in_start + 3)


def mxu(a, b):
    return jnp.dot(a, b, preferred_element_type=F32)


def dot3(matrix, vh, vl):
    mh, ml = two_terms(matrix)
    return mxu(mh, vh) + mxu(mh, vl) + mxu(ml, vh)


def first_half(rows):
    return lax.broadcasted_iota(jnp.int32, (rows, LANES), 1) < C


def half_turn(value):
    return None if value is None else pltpu.roll(value, C, 1)


def pick(left, a, b):
    if a is None and b is None:
        return None
    return jnp.where(left, 0.0 if a is None else a, 0.0 if b is None else b)


def plus(a, b, factor):
    if b is None:
        return a
    if a is None:
        return b * factor
    return a + b * factor


class Memo:
    def __init__(self, make):
        self.make, self.known = make, {}

    def __call__(self, n):
        if n not in self.known:
            self.known[n] = self.make(n)
        return self.known[n]


def analysis(cols, start, left):
    turned = Memo(lambda i: half_turn(cols[i]) if 0 <= i < len(cols) else None)
    plain = lambda i: cols[i] if 0 <= i < len(cols) else None
    if start % 2 == 0:
        at = lambda n: n - 1 - start // 2
        u = Memo(lambda n: pick(left, turned(at(n) - 1), plain(at(n))))
        w = Memo(lambda n: pick(left, plain(at(n)), turned(at(n) + 1)))
    else:
        at = lambda n: n - (start + 3) // 2
        u = Memo(lambda n: pick(left, plain(at(n)), turned(at(n) + 1)))
        w = Memo(lambda n: pick(left, turned(at(n)), plain(at(n) + 1)))

    def band(taps):
        def make(k):
            total = None
            for step in range(4):
                total = plus(total, u(k + step), float(taps[2 * step]))
                total = plus(total, w(k + step), float(taps[2 * step + 1]))
            return total

        return make

    return band(LOW), band(HIGH)


def synthesis(lows, highs, start, left):
    parity = start % 2

    def cells(cols):
        col = lambda k: cols[(k - start) // 2] if 0 <= k - start < 2 * len(cols) else None
        turned = Memo(lambda k: half_turn(col(k)))

        def at(k):
            if k % 2 == parity:
                return col(k)
            return pick(left, turned(k - 1), turned(k + 1))

        return Memo(at)

    sources = ((cells(lows), LOW), (cells(highs), HIGH))

    def output(first):
        def make(n):
            total = None
            for step in range(4):
                for source, taps in sources:
                    total = plus(total, source(n - step), float(taps[2 * step + first]))
            return total

        return Memo(make)

    u, w = output(0), output(1)
    u_turned, w_turned = Memo(lambda n: half_turn(u(n))), Memo(lambda n: half_turn(w(n)))

    def pair(m):
        if m % 2:
            n = (m + 3) // 2
            if n % 2 == parity:
                return pick(left, u(n), w_turned(n))
            return pick(left, u_turned(n - 1), w(n - 1))
        n = m // 2 + 1
        if n % 2 == parity:
            return pick(left, w(n), u(n))
        return pick(left, w_turned(n - 1), u_turned(n + 1))

    return pair


def synthesis_of_lows(lows, start, left):
    def dup(k):
        i = (k - start) // 2
        if not 0 <= i < len(lows):
            return None
        turned = rolled(i)
        return jnp.where(left, lows[i], turned) if (k - start) % 2 == 0 else jnp.where(left, turned, lows[i])

    rolled = Memo(lambda i: half_turn(lows[i]))
    both = Memo(dup)

    def tap(t):
        return F32(LOW[t]) if 0 <= t < 8 else F32(0.0)

    weights = [jnp.where(left[0:8], tap(7 - 2 * i), tap(8 - 2 * i)) for i in range(5)]
    weights = [jnp.concatenate([v] * (left.shape[0] // 8), 0) for v in weights]

    def pair(m):
        total = None
        for i in range(5):
            cell = both(m // 2 - 2 + i)
            if cell is not None:
                total = cell * weights[i] if total is None else total + cell * weights[i]
        return total

    return pair


def columns(ref, row, rows, count=None):
    count = ref.shape[-1] // LANES if count is None else count
    return [ref[pl.ds(row, rows), pl.ds(LANES * p, LANES)] for p in range(count)]


def put(ref, row, p, value, lead=()):
    ref[lead + (pl.ds(row, value.shape[0]), pl.ds(LANES * p, LANES))] = value


class Geometry:
    def __init__(self, rows, cells):
        self.rows = [rows >> level for level in range(5)]
        self.cells = [cells >> level for level in range(5)]
        up = lambda value, step: -(-value // step) * step
        self.band = [
            None,
            (-4, up(self.rows[1] + 4, 120)),
            (-8, up(self.rows[2] + 11, 16)),
            (-3, up(self.rows[3] + 6, 8)),
            (-3, up(self.rows[4] + 6, 8)),
        ]
        self.low = [
            None,
            (-52, up(self.rows[1] + 97, 112)),
            (-24, up(self.rows[2] + 45, 88)),
            (-11, up(self.rows[3] + 20, 8)),
            (-3, up(self.rows[4] + 6, 8)),
        ]
        self.span = [None, (-2, self.cells[1] // 2 + 2)]
        for level in (2, 3, 4):
            self.span.append((-3, self.cells[level] // 2 + 3))
        self.extended = max(
            LEAD + 2 * HALO + rows, 2 * (self.low[1][1] - 112) + 256
        )


STEP = 240
SIDE = 8
NEAR = 16


def best_step(rows, most=None):
    return max(s for s in range(8, (most or STEP) + 1, 8) if rows % s == 0)


def low_rows(geo, level, source, source_start, target):
    first, pairs = geo.span[level]
    rows = geo.low[level][1]
    step = best_step(rows, 168)
    left = first_half(step)

    def body(c, carry):
        row = pl.multiple_of(c * step, step)
        low, _ = analysis(columns(source, row, step), source_start, left)
        for q in range(pairs):
            put(target, row, q, low(first + 2 * q))
        return carry

    lax.fori_loop(0, rows // step, body, 0)


def band_rows(geo, level, lo, skip, hi, source_start, gain, bands):
    first, pairs = geo.span[level]
    rows = geo.band[level][1]
    step = best_step(rows)
    left = first_half(step)

    def body(c, carry):
        row = pl.multiple_of(c * step, step)
        g = []
        for b in range(3):
            one = gain[level - 1, b : b + 1, :]
            g.append(jnp.broadcast_to(jnp.concatenate([one, one], 1), (step, LANES)))
        _, high = analysis(columns(lo, row + skip, step), source_start, left)
        for q in range(pairs):
            put(bands, row, q, high(first + 2 * q) * g[0], (0,))
        low, high = analysis(columns(hi, row, step), source_start, left)
        for q in range(pairs):
            put(bands, row, q, low(first + 2 * q) * g[1], (1,))
            put(bands, row, q, high(first + 2 * q) * g[2], (2,))
        return carry

    lax.fori_loop(0, rows // step, body, 0)


def analysis_kernel(geo, lats, place, edge, gain, x, *refs):
    lat, parity = place[0], place[1] % 2
    ll4, out2, out3, out4, send_e, send_o, p2, m2, p3, m3 = refs[:10]
    ext, la, g1, gh, gl, lo2, g2, lo3, g3, lo4, hi2, hi3, hi4, d2, d3, d4, sems, out_sems = refs[10:]
    outs = {2: (d2, out2), 3: (d3, out3), 4: (d4, out4)}
    rows = geo.rows[0]
    start, count = geo.low[1]
    width = x.shape[1]
    begin = LEAD + HALO
    blocks = count // 112
    cuts = [0] + [min(rows, 224 * b + 256 - begin) for b in range(blocks - 1)] + [rows]
    copies = []
    for i in range(blocks):
        part = pl.ds(cuts[i], cuts[i + 1] - cuts[i])
        to = pl.ds(begin + cuts[i], cuts[i + 1] - cuts[i])
        copies.append(pltpu.make_async_copy(x.at[part, :], ext.at[to, :], sems.at[i]))
        copies[-1].start()
    top = slice(LEAD, begin)
    bottom = slice(begin + rows, begin + rows + HALO)
    ext[0:LEAD, :] = jnp.zeros((LEAD, width), BF16)
    tail = geo.extended - (LEAD + 2 * HALO + rows)
    if tail:
        ext[geo.extended - tail :, :] = jnp.zeros((tail, width), BF16)

    @pl.when(lat == 0)
    def _():
        ext[top, :] = jnp.zeros((HALO, width), BF16)
        ext[bottom, :] = edge[...]

    @pl.when(lat != 0)
    def _():
        ext[top, :] = edge[...]
        ext[bottom, :] = jnp.zeros((HALO, width), BF16)

    base = analysis_matrix(LOW, start, 112, 0 - LEAD - HALO, 256)
    for b in range(blocks):
        copies[b].wait()
        mh, ml = two_terms(masked_rows(base, start + 112 * b, geo.rows[1], lat, lats))
        data = ext[224 * b : 224 * b + 256, :]
        la[112 * b : 112 * b + 112, :] = mxu(mh, data) + mxu(ml, data)
    low_rows(geo, 1, la, 0, g1)
    gh[...], gl[...] = two_terms(g1[...])
    out_start, out_rows = geo.low[2]
    for b in range(out_rows // 88):
        at = min(176 * b, count - 192)
        window = slice(at, at + 192)
        matrix = analysis_matrix(LOW, out_start + 88 * b, 88, start + at, 192)
        matrix = masked_rows(matrix, out_start + 88 * b, geo.rows[2], lat, lats)
        lo2[88 * b : 88 * b + 88, :] = dot3(matrix, gh[window, :], gl[window, :])
    low_rows(geo, 2, lo2, geo.span[1][0], g2)
    for level, source, lo, target in ((3, g2, lo3, g3), (4, g3, lo4, ll4)):
        vh, vl = two_terms(source[...])
        matrix = analysis_matrix(LOW, *geo.low[level], *geo.low[level - 1])
        matrix = masked_rows(matrix, geo.low[level][0], geo.rows[level], lat, lats)
        lo[...] = dot3(matrix, vh, vl)
        low_rows(geo, level, lo, geo.span[level - 1][0], target)
    copies = []
    for level, lo, hi in ((2, lo2, hi2), (3, lo3, hi3), (4, lo4, hi4)):
        deep_bands(geo, lats, lat, level, {2: (gh, gl), 3: g2, 4: g3}[level], lo, hi, gain, outs[level][0])
        copies.append(pltpu.make_async_copy(*outs[level], out_sems.at[level - 2]))
        copies[-1].start()
    d = {2: d2, 3: d3, 4: d4}

    def fill(distance, to_left, to_right):
        for level, count, row in exchange_plan(geo)[distance]:
            n = geo.band[level][1]
            move = distance * geo.cells[level] // 2
            for b in range(3):
                lanes = slice(b * count * LANES, (b + 1) * count * LANES)
                to_left[row : row + n, lanes] = d[level][b, :, 0 : count * LANES].astype(BF16)
                to_right[row : row + n, lanes] = d[level][
                    b, :, move * LANES : (move + count) * LANES
                ].astype(BF16)

    @pl.when(parity == 0)
    def _():
        fill(1, send_o, send_e)

    @pl.when(parity != 0)
    def _():
        fill(1, send_e, send_o)

    fill(2, m2, p2)
    fill(3, m3, p3)
    for copy in copies:
        copy.wait()


def deep_bands(geo, lats, lat, level, source, lo, hi, gain, bands):
    start, count = geo.band[level]
    in_start = geo.low[level - 1][0]
    parts = 2 if level == 2 else 1
    half = count // parts
    for b in range(parts):
        if parts == 1:
            at, size = 0, source.shape[0]
            vh, vl = two_terms(source[...])
        else:
            at = (2 * (start + half * b) - 3 - in_start) // 16 * 16
            size = 2 * half + 16
            vh, vl = source[0][at : at + size, :], source[1][at : at + size, :]
        matrix = analysis_matrix(HIGH, start + half * b, half, in_start + at, size)
        matrix = masked_rows(matrix, start + half * b, geo.rows[level], lat, lats)
        hi[half * b : half * (b + 1), :] = dot3(matrix, vh, vl)
    skip = start - geo.low[level][0]
    band_rows(geo, level, lo, skip, hi, geo.span[level - 1][0], gain, bands)


def sides_kernel(place, x, side_e, side_o, sems):
    parity = place[1] % 2
    width, lanes = x.shape[1], side_e.shape[1]

    def both(low, high):
        copies = [
            pltpu.make_async_copy(x.at[:, pl.ds(0, lanes)], low, sems.at[0]),
            pltpu.make_async_copy(x.at[:, pl.ds(width - lanes, lanes)], high, sems.at[1]),
        ]
        for copy in copies:
            copy.start()
        for copy in copies:
            copy.wait()

    @pl.when(parity == 0)
    def _():
        both(side_o, side_e)

    @pl.when(parity != 0)
    def _():
        both(side_e, side_o)


def corners_kernel(place, side_e, side_o, out):
    lat, parity = place[0], place[1] % 2
    rows, lanes = side_e.shape
    at = jnp.where(lat == 0, rows - NEAR, 0)
    window = pl.ds(pl.multiple_of(at, NEAR), NEAR)

    @pl.when(parity == 0)
    def _():
        out[:, 0:lanes] = side_o[window, :]
        out[:, lanes:] = side_e[window, :]

    @pl.when(parity != 0)
    def _():
        out[:, 0:lanes] = side_e[window, :]
        out[:, lanes:] = side_o[window, :]


def merge_kernel(size, more, place, mine, other, out):
    width = mine.shape[1]

    def add(lower, upper):
        out[:, 0:more] = lower[:, 0:more]
        out[:, more:width] = lower[:, more:] + upper[:, 0 : width - more]
        out[:, width:] = upper[:, width - more :]

    lower_half = (place[1] // size) % 2 == 0

    @pl.when(lower_half)
    def _():
        add(mine, other)

    @pl.when(jnp.logical_not(lower_half))
    def _():
        add(other, mine)


def last_merge_kernel(geo, size, more, place, mine, other, ring, tokens, merged):
    merge_kernel(size, more, place, mine, other, merged)
    around = ring.shape[1]
    fold = merged.shape[1] - around
    ring[:, 0:fold] = merged[:, 0:fold] + merged[:, around:]
    ring[:, fold:] = merged[:, fold:around]
    skip = -geo.low[4][0]
    tokens[...] = ring[skip : skip + geo.rows[4], :].astype(BF16)


def first_level_kernel(geo, lats, place, edge, side_e, side_o, corner, gain, x, held, ext, la, ha, d1, xh, xl, part, sem):
    lat, parity = place[0], place[1] % 2
    rows, width = x.shape
    lanes = SIDE * C
    copy = pltpu.make_async_copy(x, ext.at[pl.ds(NEAR, rows), pl.ds(lanes, width)], sem)
    copy.start()
    sides = (slice(0, lanes), slice(lanes + width, width + 2 * lanes))
    own = slice(lanes, lanes + width)
    inner = slice(NEAR, NEAR + rows)

    def rims(near, far, edges):
        ext[far, :] = jnp.zeros((NEAR, width + 2 * lanes), BF16)
        ext[near, own] = edges
        ext[near, sides[0]] = corner[:, 0:lanes]
        ext[near, sides[1]] = corner[:, lanes:]

    top, bottom = slice(0, NEAR), slice(NEAR + rows, 2 * NEAR + rows)

    @pl.when(lat == 0)
    def _():
        rims(bottom, top, edge[0:NEAR, :])

    @pl.when(lat != 0)
    def _():
        rims(top, bottom, edge[HALO - NEAR :, :])

    @pl.when(parity == 0)
    def _():
        ext[inner, sides[0]] = side_o[...]
        ext[inner, sides[1]] = side_e[...]

    @pl.when(parity != 0)
    def _():
        ext[inner, sides[0]] = side_e[...]
        ext[inner, sides[1]] = side_o[...]

    start, count = geo.band[1]
    low = analysis_matrix(LOW, start, 120, -NEAR, 256)
    high = analysis_matrix(HIGH, start, 120, -NEAR, 256)
    copy.wait()
    for b in range(count // 120):
        data = ext[240 * b : 240 * b + 256, :]
        for matrix, out in ((low, la), (high, ha)):
            mh, ml = two_terms(masked_rows(matrix, start + 120 * b, geo.rows[1], lat, lats))
            out[120 * b : 120 * b + 120, :] = mxu(mh, data) + mxu(ml, data)
    band_rows(geo, 1, la, 0, ha, -SIDE, gain, d1)
    half = rows // 2
    ylow, yhigh = la, ha
    used = slice(0, d1.shape[2])
    for block in range(2):
        w = 0 if block == 0 else count - LANES
        window = slice(w, w + LANES)
        target = slice(half * block, half * (block + 1))
        matrix = synthesis_matrix(half * block, half, start + w, LANES)
        sh, sl = two_terms(matrix)
        xh[0:LANES, :], xl[0:LANES, :] = two_terms(d1[0, window, :])
        xh[LANES:, :], xl[LANES:, :] = two_terms(d1[2, window, :])
        yhigh[target, used] = mxu(sh, xh[...]) + mxu(sh, xl[...]) + mxu(sl, xh[...])
        vh, vl = two_terms(d1[1, window, :])
        sh, sl = sh[:, LANES:], sl[:, LANES:]
        ylow[target, used] = mxu(sh, vh) + mxu(sh, vl) + mxu(sl, vh)

    begin, pairs = geo.span[1]
    most = 232

    def chunk(i, carry):
        row = pl.multiple_of(i * most, 8)
        pair = synthesis(
            columns(ylow, row, most, pairs), columns(yhigh, row, most, pairs), begin, first_half(most)
        )
        for q in range(geo.cells[0] // 2):
            put(part, row, q, pair(2 * q))
        copy = pltpu.make_async_copy(part.at[pl.ds(row, most), :], held.at[pl.ds(row, most), :], sem)
        copy.start()
        copy.wait()
        return carry

    lax.fori_loop(0, rows // most, chunk, 0)


def exchange_plan(geo):
    plan = {}
    for distance in (1, 2, 3):
        entries, row = [], 0
        for level in (2, 3, 4):
            count = geo.span[level][1] - distance * geo.cells[level] // 2
            if count > 0:
                entries.append((level, count, row))
                row += -(-geo.band[level][1] // 16) * 16
        plan[distance] = entries
    return plan


def plan_shape(geo, distance):
    entries = exchange_plan(geo)[distance]
    rows = sum(-(-geo.band[level][1] // 16) * 16 for level, _, _ in entries)
    return (rows, max(count for _, count, _ in entries) * 3 * LANES)


def attention_kernel(geo, lats, blocks, place, ring, own, others, we, wqkv, scale, wo, gain, wb, out, around, listed, keys):
    lat, lon = place[0], place[1]
    rows, width = out.shape
    cells = width // C
    total = ring.shape[1]
    around[:, 0:total] = ring[...]
    around[:, total:] = ring[:, 0 : around.shape[1] - total]
    field = around[:, pl.ds(pl.multiple_of(lon * (geo.cells[4] * C), LANES), width)]
    count = geo.rows[4]
    for source, shift in ((own, 0), (others, count)):
        for pair in range(total // LANES):
            value = source[:, pair * LANES : (pair + 1) * LANES].astype(F32)
            for side in range(2):
                at = 2 * count * (2 * pair + side) + shift
                listed[at : at + count, :] = value[:, side * C : (side + 1) * C]
    keys[...] = listed[...].astype(BF16)
    own = jnp.concatenate([field[:, C * c : C * (c + 1)] for c in range(cells)], 0)
    count = own.shape[0]
    embedded = mxu(own.astype(BF16), we[...])
    queries = mxu(embedded.astype(BF16), wqkv[:, 0:E]).astype(BF16)
    lane = lax.broadcasted_iota(jnp.int32, (1, E), 1)
    block = keys.shape[0] // blocks
    factor = [scale[h] * (1.0 / math.sqrt(HEAD_DIM)) for h in range(HEADS)]

    def keyvals(start):
        spread = mxu(keys[pl.ds(start, block), :], we[...]).astype(BF16)
        both = mxu(spread, wqkv[:, E : 3 * E]).astype(BF16)
        return both[:, 0:E], both[:, E : 2 * E]

    def scores_of(h, k):
        mine = (lane >= h * HEAD_DIM) & (lane < (h + 1) * HEAD_DIM)
        q = jnp.where(mine, queries, jnp.zeros_like(queries))
        s = lax.dot_general(q, k, (((1,), (1,)), ((), ())), preferred_element_type=F32)
        return s * factor[h]

    def masked(h, value):
        mine = (lane >= h * HEAD_DIM) & (lane < (h + 1) * HEAD_DIM)
        return jnp.where(mine, value, jnp.zeros_like(value))

    if blocks == 1:
        k, v = keyvals(0)
        attended = jnp.zeros((count, E), F32)
        for h in range(HEADS):
            s = scores_of(h, k)
            w = jnp.exp(s - jnp.max(s, -1, keepdims=True))
            total = jnp.sum(w, -1, keepdims=True)
            attended = attended + masked(h, mxu(w.astype(BF16), v) / total)
    else:

        def one_block(b, carry):
            peaks, totals, sums = carry
            k, v = keyvals(pl.multiple_of(b * block, 16))
            new_peaks, new_totals = [], []
            shrunk = jnp.zeros((count, E), F32)
            for h in range(HEADS):
                s = scores_of(h, k)
                peak = jnp.maximum(peaks[h], jnp.max(s, -1, keepdims=True))
                shrink = jnp.exp(peaks[h] - peak)
                w = jnp.exp(s - peak)
                new_peaks.append(peak)
                new_totals.append(totals[h] * shrink + jnp.sum(w, -1, keepdims=True))
                shrunk = shrunk + masked(h, sums * shrink + mxu(w.astype(BF16), v))
            return tuple(new_peaks), tuple(new_totals), shrunk

        start = (
            tuple(jnp.full((count, 1), -1e30, F32) for _ in range(HEADS)),
            tuple(jnp.zeros((count, 1), F32) for _ in range(HEADS)),
            jnp.zeros((count, E), F32),
        )
        _, totals, sums = lax.fori_loop(0, blocks, one_block, start)
        attended = jnp.zeros((count, E), F32)
        for h in range(HEADS):
            attended = attended + masked(h, sums / totals[h])
    hidden = embedded + mxu(attended.astype(BF16), wo[...])
    square = jnp.mean(hidden * hidden, -1, keepdims=True)
    normed = (hidden * lax.rsqrt(square + 1e-06) * gain[...]).astype(BF16)
    update = lax.dot_general(
        normed, wb[...], (((1,), (1,)), ((), ())), preferred_element_type=F32
    )
    back = [
        jnp.concatenate(
            [update[rows * c : rows * (c + 1), :], update[rows * (c + 1) : rows * (c + 2), :]], 1
        )
        for c in range(0, cells, 2)
    ]
    start = geo.band[4][0]
    for q, value in enumerate(back):
        at = slice(q * LANES, (q + 1) * LANES)
        out[:, at] = masked_rows(field[:, at] + value, start, geo.rows[4], lat, lats)


def synthesis_kernel(geo, lats, place, coarse, e2, o2, from_m2, from_p2, from_m3, from_p3, *refs):
    lat, parity = place[0], place[1] % 2
    held, (out, up3, up2, up1, ylow, yhigh, done), refs = refs[:4], refs[4:11], refs[11:]
    part, d2, d3, d4, sems, in_sems = refs
    arrive = [
        pltpu.make_async_copy(source, to, in_sems.at[i])
        for i, (source, to) in enumerate(zip(held, (part, d2, d3, d4)))
    ]
    for level in (4, 3, 2, 1):
        arrive[level - 1].start()
    bands = {2: d2, 3: d3, 4: d4}
    plan = exchange_plan(geo)

    def from_sides(level, b):
        n = geo.band[level][1]
        cols = [bands[level][b, :, LANES * p : LANES * (p + 1)] for p in range(geo.span[level][1])]
        for distance in (1, 2, 3):
            for which, count, row in plan[distance]:
                if which != level:
                    continue
                move = distance * geo.cells[level] // 2
                for p in range(count):
                    lanes = slice((b * count + p) * LANES, (b * count + p + 1) * LANES)
                    if distance == 1:
                        even = e2[row : row + n, lanes].astype(F32)
                        odd = o2[row : row + n, lanes].astype(F32)
                        low = jnp.where(parity == 0, odd, even)
                        high = jnp.where(parity == 0, even, odd)
                    else:
                        lows, highs = {2: (from_m2, from_p2), 3: (from_m3, from_p3)}[distance]
                        low = lows[row : row + n, lanes].astype(F32)
                        high = highs[row : row + n, lanes].astype(F32)
                    cols[p] = cols[p] + low
                    cols[p + move] = cols[p + move] + high
        return jnp.concatenate(cols, 1)

    uppers = {4: coarse, 3: up3, 2: up2, 1: up1}
    for level in (4, 3, 2):
        arrive[level - 1].wait()
        begin, pairs = geo.span[level]
        below = level - 1
        start, rows = geo.band[below]
        matrix = synthesis_matrix(start, rows, *geo.band[level])
        matrix = masked_rows(matrix, start, geo.rows[below], lat, lats)
        width = pairs * LANES
        for one, two, y in (
            (uppers[level][...], from_sides(level, 1), ylow),
            (from_sides(level, 0), from_sides(level, 2), yhigh),
        ):
            h, l = two_terms(jnp.concatenate([one, two], 0))
            y[0:rows, 0:width] = dot3(matrix, h, l)
        target = uppers[below]
        first, out_pairs = geo.span[below]

        step = best_step(rows)
        left = first_half(step)

        def joined(c, carry):
            row = pl.multiple_of(c * step, step)
            pair = synthesis(
                columns(ylow, row, step, pairs), columns(yhigh, row, step, pairs), begin, left
            )
            for q in range(out_pairs):
                put(target, row, q, pair(first + 2 * q))
            return carry

        lax.fori_loop(0, rows // step, joined, 0)

    n = geo.band[1][1]
    half = geo.rows[0] // 2
    for block in range(2):
        w = 0 if block == 0 else n - LANES
        matrix = synthesis_matrix(half * block, half, geo.band[1][0] + w, LANES)
        h, l = two_terms(up1[w : w + LANES, :])
        ylow[half * block : half * (block + 1), :] = dot3(matrix[:, 0:LANES], h, l)
    arrive[0].wait()
    begin, pairs = geo.span[1]
    most = 112

    def last(row, count):
        left = first_half(count)
        pair = synthesis_of_lows(columns(ylow, row, count), begin, left)
        for q in range(geo.cells[0] // 2):
            more = part[pl.ds(row, count), pl.ds(LANES * q, LANES)]
            put(done, row, q, (pair(2 * q) + more).astype(BF16))

    def store(i, count):
        part = pl.ds(pl.multiple_of(i * most, 16), count)
        return pltpu.make_async_copy(done.at[part, :], out.at[part, :], sems.at[i])

    whole, rest = geo.rows[0] // most, geo.rows[0] % most

    def chunk(i, carry):
        last(pl.multiple_of(i * most, 16), most)
        store(i, most).start()
        return carry

    lax.fori_loop(0, whole, chunk, 0)
    if rest:
        last(whole * most, rest)
        store(whole, rest).start()
    for i in range(whole):
        store(i, most).wait()
    if rest:
        store(whole, rest).wait()


def call(kernel, out_shape, scratch, *args, cost=20_000_000, grant=24, raw=(), raw_out=()):
    vmem = pl.BlockSpec(memory_space=pltpu.VMEM)
    smem = pl.BlockSpec(memory_space=pltpu.SMEM)
    anywhere = pl.BlockSpec(memory_space=pl.ANY)
    specs = [smem if a.ndim == 1 and a.size < 16 else vmem for a in args]
    for at in raw:
        specs[at] = anywhere
    outs = [anywhere if i in raw_out else vmem for i in range(len(out_shape))]
    return pl.pallas_call(
        kernel,
        out_shape=tuple(out_shape),
        in_specs=specs,
        out_specs=tuple(outs),
        scratch_shapes=scratch,
        compiler_params=pltpu.CompilerParams(vmem_limit_bytes=grant << 20),
        cost_estimate=pl.CostEstimate(flops=cost, bytes_accessed=1 << 20, transcendentals=0),
    )(*args)


def shape(dims, dtype=F32):
    return jax.ShapeDtypeStruct(dims, dtype)


def per_device(mesh_shape, state_field, skip_gain, embed_weight, qkv_weight, head_scale, out_weight, norm_gain, back_weight):
    return program(
        mesh_shape, state_field, skip_gain, embed_weight, qkv_weight, head_scale, out_weight, norm_gain, back_weight
    )


def program(mesh_shape, state_field, skip_gain, embed_weight, qkv_weight, head_scale, out_weight, norm_gain, back_weight):
    lons, lats = mesh_shape["lon"], mesh_shape["lat"]
    rows, width = state_field.shape
    geo = Geometry(rows, width // C)
    lat, lon = lax.axis_index("lat"), lax.axis_index("lon")
    place = jnp.stack([lat, lon]).astype(jnp.int32)

    even_pairs = [(i, i ^ 1) for i in range(lons)]
    odd_pairs = [(i, (i + 1 if i % 2 else i - 1) % lons) for i in range(lons)]
    swap = [(i, lats - 1 - i) for i in range(lats)]

    def shifted(value, by):
        return lax.ppermute(value, "lon", [(i, (i + by) % lons) for i in range(lons)])

    edge = lax.dynamic_slice(
        state_field, (jnp.where(lat == 0, rows - HALO, 0), 0), (HALO, width)
    )
    edge = lax.ppermute(edge, "lat", swap)

    wide = SIDE * C
    extended = NEAR + rows + NEAR
    side_e, side_o = call(
        sides_kernel,
        [shape((rows, wide), BF16)] * 2,
        [pltpu.SemaphoreType.DMA((2,))],
        place,
        state_field,
        raw=(1,),
        cost=1_000_000,
    )
    side_e = lax.ppermute(side_e, "lon", even_pairs)
    side_o = lax.ppermute(side_o, "lon", odd_pairs)

    w = [None] + [geo.span[level][1] * LANES for level in (1, 2, 3, 4)]
    low = lambda level, lanes: pltpu.VMEM((geo.low[level][1], w[lanes]), F32)
    bands = [(3, geo.band[level][1], w[level]) for level in (1, 2, 3, 4)]
    ll4, d2, d3, d4, deep_e, deep_o, p2, m2, p3, m3 = call(
        functools.partial(analysis_kernel, geo, lats),
        [shape((geo.low[4][1], w[4]))]
        + [shape(dims) for dims in bands[1:]]
        + [shape(plan_shape(geo, d), BF16) for d in (1, 1, 2, 2, 3, 3)],
        [
            pltpu.VMEM((geo.extended, width), BF16),
            pltpu.VMEM((geo.low[1][1], width), F32),
            low(1, 1),
            pltpu.VMEM((geo.low[1][1], w[1]), BF16),
            pltpu.VMEM((geo.low[1][1], w[1]), BF16),
            low(2, 1),
            low(2, 2),
            low(3, 2),
            low(3, 3),
            low(4, 3),
        ]
        + [pltpu.VMEM((geo.band[level][1], w[level - 1]), F32) for level in (2, 3, 4)]
        + [pltpu.VMEM(dims, F32) for dims in bands[1:]]
        + [
            pltpu.SemaphoreType.DMA((geo.low[1][1] // 112,)),
            pltpu.SemaphoreType.DMA((3,)),
        ],
        place,
        edge,
        skip_gain,
        state_field,
        raw=(3,),
        raw_out=(1, 2, 3),
    )
    (corner,) = call(
        corners_kernel, [shape((NEAR, 2 * wide), BF16)], [], place, side_e, side_o, cost=100_000
    )
    corner = lax.ppermute(corner, "lat", swap)
    (part,) = call(
        functools.partial(first_level_kernel, geo, lats),
        [shape((rows, width))],
        [
            pltpu.VMEM((extended, width + 2 * wide), BF16),
            pltpu.VMEM((rows, width + 2 * wide), F32),
            pltpu.VMEM((rows, width + 2 * wide), F32),
            pltpu.VMEM(bands[0], F32),
            pltpu.VMEM((2 * LANES, w[1]), BF16),
            pltpu.VMEM((2 * LANES, w[1]), BF16),
            pltpu.VMEM((rows, width), F32),
            pltpu.SemaphoreType.DMA,
        ],
        place,
        edge,
        side_e,
        side_o,
        corner,
        skip_gain,
        state_field,
        raw=(6,),
        raw_out=(0,),
        grant=40,
    )

    merged, size = ll4, 1
    total = geo.cells[4] * lons * C
    while size < lons:
        other = lax.ppermute(merged, "lon", [(i, i ^ size) for i in range(lons)])
        more = geo.cells[4] * C * size
        dims = (merged.shape[0], merged.shape[1] + more)
        if 2 * size < lons:
            (merged,) = call(
                functools.partial(merge_kernel, size, more), [shape(dims)], [], place, merged, other, cost=100_000
            )
        else:
            ring, tokens = call(
                functools.partial(last_merge_kernel, geo, size, more),
                [shape((dims[0], total)), shape((geo.rows[4], total), BF16)],
                [pltpu.VMEM(dims, F32)],
                place,
                merged,
                other,
                cost=100_000,
            )
        size = 2 * size
    others = lax.ppermute(tokens, "lat", swap)

    deep_e = lax.ppermute(deep_e, "lon", even_pairs)
    deep_o = lax.ppermute(deep_o, "lon", odd_pairs)
    from_m2, from_p2 = shifted(p2, 2), shifted(m2, -2)
    from_m3, from_p3 = shifted(p3, 3), shifted(m3, -3)

    key_count = 2 * geo.rows[4] * geo.cells[4] * lons
    blocks = key_count // 928 if key_count % 928 == 0 else 1
    (coarse,) = call(
        functools.partial(attention_kernel, geo, lats, blocks),
        [shape((geo.low[4][1], w[4]))],
        [
            pltpu.VMEM((geo.low[4][1], total + 6 * C), F32),
            pltpu.VMEM((key_count, C), F32),
            pltpu.VMEM((key_count, C), BF16),
        ],
        place,
        ring,
        tokens,
        others,
        embed_weight,
        qkv_weight,
        head_scale,
        out_weight,
        norm_gain[None],
        back_weight.T,
        cost=200_000_000,
        grant=40,
    )

    (out,) = call(
        functools.partial(synthesis_kernel, geo, lats),
        [shape((rows, width), BF16)],
        [pltpu.VMEM((geo.band[level][1], w[level]), F32) for level in (3, 2, 1)]
        + [
            pltpu.VMEM((rows, w[1]), F32),
            pltpu.VMEM((geo.band[1][1], w[2]), F32),
            pltpu.VMEM((rows, width), BF16),
            pltpu.VMEM((rows, width), F32),
        ]
        + [pltpu.VMEM(dims, F32) for dims in bands[1:]]
        + [
            pltpu.SemaphoreType.DMA((rows // 112 + 1,)),
            pltpu.SemaphoreType.DMA((4,)),
        ],
        place,
        coarse,
        deep_e,
        deep_o,
        from_m2,
        from_p2,
        from_m3,
        from_p3,
        part,
        d2,
        d3,
        d4,
        raw=(8, 9, 10, 11),
        raw_out=(0,),
        grant=40,
    )
    return out


def solution(mesh):
    in_specs = (P("lat", ("member", "lon")), P(), P(), P(), P(), P(), P(), P())
    out_specs = P("lat", ("member", "lon"))
    return jax.shard_map(
        functools.partial(per_device, dict(mesh.shape)),
        mesh=mesh,
        in_specs=in_specs,
        out_specs=out_specs,
        check_vma=False,
    )
```

```python
import functools
import math

import jax
import jax.numpy as jnp
import numpy as np
from jax import lax
from jax.experimental import pallas as pl
from jax.experimental.pallas import tpu as pltpu
from jax.sharding import PartitionSpec as P


C = 64
HEADS = 8
HEAD_DIM = 32
E = 256
LANES = 128
HALO = 96
LEAD = 16

LOW = np.array(
    [
        -0.010597401784997278,
        0.032883011666982945,
        0.030841381835986965,
        -0.18703481171888114,
        -0.02798376941698385,
        0.6308807679295904,
        0.7148465705525415,
        0.23037781330885523,
    ]
)
HIGH = np.array([(-1.0) ** j * LOW[7 - j] for j in range(8)])


F32 = jnp.float32
BF16 = jnp.bfloat16


def two_terms(value):
    top = value.astype(BF16)
    return top, (value - top.astype(F32)).astype(BF16)


def masked_rows(matrix, start, count, lat, lats):
    row = lax.broadcasted_iota(jnp.int32, matrix.shape, 0) + (start + lat * count)
    return jnp.where((row >= 0) & (row < count * lats), matrix, 0.0)


def banded(shape, low, high, row_factor, column_factor, offset):
    row = lax.broadcasted_iota(jnp.int32, shape, 0)
    column = lax.broadcasted_iota(jnp.int32, shape, 1)
    tap = row_factor * row + column_factor * column + offset
    if high is not None:
        second = column >= shape[1] // 2
        tap = jnp.where(second, tap - column_factor * (shape[1] // 2), tap)
    matrix = jnp.zeros(shape, F32)
    for t in range(8):
        value = F32(low[t]) if high is None else jnp.where(second, F32(high[t]), F32(low[t]))
        matrix = jnp.where(tap == t, value, matrix)
    return matrix


def analysis_matrix(taps, out_start, out_rows, in_start, in_rows):
    return banded((out_rows, in_rows), taps, None, -2, 1, in_start + 3 - 2 * out_start)


def synthesis_matrix(out_start, out_rows, in_start, in_rows):
    shape = (out_rows, 2 * in_rows)
    return banded(shape, LOW, HIGH, 1, -2, out_start - 2 * in_start + 3)


def mxu(a, b):
    return jnp.dot(a, b, preferred_element_type=F32)


def dot3(matrix, vh, vl):
    mh, ml = two_terms(matrix)
    return mxu(mh, vh) + mxu(mh, vl) + mxu(ml, vh)


def first_half(rows):
    return lax.broadcasted_iota(jnp.int32, (rows, LANES), 1) < C


def half_turn(value):
    return None if value is None else pltpu.roll(value, C, 1)


def pick(left, a, b):
    if a is None and b is None:
        return None
    return jnp.where(left, 0.0 if a is None else a, 0.0 if b is None else b)


def plus(a, b, factor):
    if b is None:
        return a
    if a is None:
        return b * factor
    return a + b * factor


class Memo:
    def __init__(self, make):
        self.make, self.known = make, {}

    def __call__(self, n):
        if n not in self.known:
            self.known[n] = self.make(n)
        return self.known[n]


def analysis(cols, start, left):
    turned = Memo(lambda i: half_turn(cols[i]) if 0 <= i < len(cols) else None)
    plain = lambda i: cols[i] if 0 <= i < len(cols) else None
    if start % 2 == 0:
        at = lambda n: n - 1 - start // 2
        u = Memo(lambda n: pick(left, turned(at(n) - 1), plain(at(n))))
        w = Memo(lambda n: pick(left, plain(at(n)), turned(at(n) + 1)))
    else:
        at = lambda n: n - (start + 3) // 2
        u = Memo(lambda n: pick(left, plain(at(n)), turned(at(n) + 1)))
        w = Memo(lambda n: pick(left, turned(at(n)), plain(at(n) + 1)))

    def band(taps):
        def make(k):
            total = None
            for step in range(4):
                total = plus(total, u(k + step), float(taps[2 * step]))
                total = plus(total, w(k + step), float(taps[2 * step + 1]))
            return total

        return make

    return band(LOW), band(HIGH)


def synthesis(lows, highs, start, left):
    parity = start % 2

    def cells(cols):
        col = lambda k: cols[(k - start) // 2] if 0 <= k - start < 2 * len(cols) else None
        turned = Memo(lambda k: half_turn(col(k)))

        def at(k):
            if k % 2 == parity:
                return col(k)
            return pick(left, turned(k - 1), turned(k + 1))

        return Memo(at)

    sources = ((cells(lows), LOW), (cells(highs), HIGH))

    def output(first):
        def make(n):
            total = None
            for step in range(4):
                for source, taps in sources:
                    total = plus(total, source(n - step), float(taps[2 * step + first]))
            return total

        return Memo(make)

    u, w = output(0), output(1)
    u_turned, w_turned = Memo(lambda n: half_turn(u(n))), Memo(lambda n: half_turn(w(n)))

    def pair(m):
        if m % 2:
            n = (m + 3) // 2
            if n % 2 == parity:
                return pick(left, u(n), w_turned(n))
            return pick(left, u_turned(n - 1), w(n - 1))
        n = m // 2 + 1
        if n % 2 == parity:
            return pick(left, w(n), u(n))
        return pick(left, w_turned(n - 1), u_turned(n + 1))

    return pair


def synthesis_of_lows(lows, start, left):
    def dup(k):
        i = (k - start) // 2
        if not 0 <= i < len(lows):
            return None
        turned = rolled(i)
        return jnp.where(left, lows[i], turned) if (k - start) % 2 == 0 else jnp.where(left, turned, lows[i])

    rolled = Memo(lambda i: half_turn(lows[i]))
    both = Memo(dup)

    def tap(t):
        return F32(LOW[t]) if 0 <= t < 8 else F32(0.0)

    weights = [jnp.where(left[0:8], tap(7 - 2 * i), tap(8 - 2 * i)) for i in range(5)]
    weights = [jnp.concatenate([v] * (left.shape[0] // 8), 0) for v in weights]

    def pair(m):
        total = None
        for i in range(5):
            cell = both(m // 2 - 2 + i)
            if cell is not None:
                total = cell * weights[i] if total is None else total + cell * weights[i]
        return total

    return pair


def columns(ref, row, rows, count=None):
    count = ref.shape[-1] // LANES if count is None else count
    return [ref[pl.ds(row, rows), pl.ds(LANES * p, LANES)] for p in range(count)]


def put(ref, row, p, value, lead=()):
    ref[lead + (pl.ds(row, value.shape[0]), pl.ds(LANES * p, LANES))] = value


class Geometry:
    def __init__(self, rows, cells):
        self.rows = [rows >> level for level in range(5)]
        self.cells = [cells >> level for level in range(5)]
        up = lambda value, step: -(-value // step) * step
        self.band = [
            None,
            (-4, up(self.rows[1] + 4, 120)),
            (-8, up(self.rows[2] + 11, 16)),
            (-3, up(self.rows[3] + 6, 8)),
            (-3, up(self.rows[4] + 6, 8)),
        ]
        self.low = [
            None,
            (-52, up(self.rows[1] + 97, 112)),
            (-24, up(self.rows[2] + 45, 88)),
            (-11, up(self.rows[3] + 20, 8)),
            (-3, up(self.rows[4] + 6, 8)),
        ]
        self.span = [None, (-2, self.cells[1] // 2 + 2)]
        for level in (2, 3, 4):
            self.span.append((-3, self.cells[level] // 2 + 3))
        self.extended = max(
            LEAD + 2 * HALO + rows, 2 * (self.low[1][1] - 112) + 256
        )


STEP = 240
SIDE = 8
NEAR = 16


def best_step(rows, most=None):
    return max(s for s in range(8, (most or STEP) + 1, 8) if rows % s == 0)


def low_rows(geo, level, source, source_start, target):
    first, pairs = geo.span[level]
    rows = geo.low[level][1]
    step = best_step(rows, 168)
    left = first_half(step)

    def body(c, carry):
        row = pl.multiple_of(c * step, step)
        low, _ = analysis(columns(source, row, step), source_start, left)
        for q in range(pairs):
            put(target, row, q, low(first + 2 * q))
        return carry

    lax.fori_loop(0, rows // step, body, 0)


def band_rows(geo, level, lo, skip, hi, source_start, gain, bands):
    first, pairs = geo.span[level]
    rows = geo.band[level][1]
    step = best_step(rows)
    left = first_half(step)

    def body(c, carry):
        row = pl.multiple_of(c * step, step)
        g = []
        for b in range(3):
            one = gain[level - 1, b : b + 1, :]
            g.append(jnp.broadcast_to(jnp.concatenate([one, one], 1), (step, LANES)))
        _, high = analysis(columns(lo, row + skip, step), source_start, left)
        for q in range(pairs):
            put(bands, row, q, high(first + 2 * q) * g[0], (0,))
        low, high = analysis(columns(hi, row, step), source_start, left)
        for q in range(pairs):
            put(bands, row, q, low(first + 2 * q) * g[1], (1,))
            put(bands, row, q, high(first + 2 * q) * g[2], (2,))
        return carry

    lax.fori_loop(0, rows // step, body, 0)


def analysis_kernel(geo, lats, place, edge, gain, x, *refs):
    lat, parity = place[0], place[1] % 2
    ll4, d2, d3, d4, send_e, send_o, p2, m2, p3, m3 = refs[:10]
    ext, la, g1, gh, gl, lo2, g2, lo3, g3, lo4, hi2, hi3, hi4, sems = refs[10:]
    rows = geo.rows[0]
    start, count = geo.low[1]
    width = x.shape[1]
    begin = LEAD + HALO
    blocks = count // 112
    cuts = [0] + [min(rows, 224 * b + 256 - begin) for b in range(blocks - 1)] + [rows]
    copies = []
    for i in range(blocks):
        part = pl.ds(cuts[i], cuts[i + 1] - cuts[i])
        to = pl.ds(begin + cuts[i], cuts[i + 1] - cuts[i])
        copies.append(pltpu.make_async_copy(x.at[part, :], ext.at[to, :], sems.at[i]))
        copies[-1].start()
    top = slice(LEAD, begin)
    bottom = slice(begin + rows, begin + rows + HALO)
    ext[0:LEAD, :] = jnp.zeros((LEAD, width), BF16)
    tail = geo.extended - (LEAD + 2 * HALO + rows)
    if tail:
        ext[geo.extended - tail :, :] = jnp.zeros((tail, width), BF16)

    @pl.when(lat == 0)
    def _():
        ext[top, :] = jnp.zeros((HALO, width), BF16)
        ext[bottom, :] = edge[...]

    @pl.when(lat != 0)
    def _():
        ext[top, :] = edge[...]
        ext[bottom, :] = jnp.zeros((HALO, width), BF16)

    base = analysis_matrix(LOW, start, 112, 0 - LEAD - HALO, 256)
    for b in range(blocks):
        copies[b].wait()
        mh, ml = two_terms(masked_rows(base, start + 112 * b, geo.rows[1], lat, lats))
        data = ext[224 * b : 224 * b + 256, :]
        la[112 * b : 112 * b + 112, :] = mxu(mh, data) + mxu(ml, data)
    low_rows(geo, 1, la, 0, g1)
    gh[...], gl[...] = two_terms(g1[...])
    out_start, out_rows = geo.low[2]
    for b in range(out_rows // 88):
        at = min(176 * b, count - 192)
        window = slice(at, at + 192)
        matrix = analysis_matrix(LOW, out_start + 88 * b, 88, start + at, 192)
        matrix = masked_rows(matrix, out_start + 88 * b, geo.rows[2], lat, lats)
        lo2[88 * b : 88 * b + 88, :] = dot3(matrix, gh[window, :], gl[window, :])
    low_rows(geo, 2, lo2, geo.span[1][0], g2)
    for level, source, lo, target in ((3, g2, lo3, g3), (4, g3, lo4, ll4)):
        vh, vl = two_terms(source[...])
        matrix = analysis_matrix(LOW, *geo.low[level], *geo.low[level - 1])
        matrix = masked_rows(matrix, geo.low[level][0], geo.rows[level], lat, lats)
        lo[...] = dot3(matrix, vh, vl)
        low_rows(geo, level, lo, geo.span[level - 1][0], target)
    d = {2: d2, 3: d3, 4: d4}
    for level, lo, hi in ((2, lo2, hi2), (3, lo3, hi3), (4, lo4, hi4)):
        deep_bands(geo, lats, lat, level, {2: (gh, gl), 3: g2, 4: g3}[level], lo, hi, gain, d[level])

    def fill(distance, to_left, to_right):
        for level, count, row in exchange_plan(geo)[distance]:
            n = geo.band[level][1]
            move = distance * geo.cells[level] // 2
            for b in range(3):
                lanes = slice(b * count * LANES, (b + 1) * count * LANES)
                to_left[row : row + n, lanes] = d[level][b, :, 0 : count * LANES].astype(BF16)
                to_right[row : row + n, lanes] = d[level][
                    b, :, move * LANES : (move + count) * LANES
                ].astype(BF16)

    @pl.when(parity == 0)
    def _():
        fill(1, send_o, send_e)

    @pl.when(parity != 0)
    def _():
        fill(1, send_e, send_o)

    fill(2, m2, p2)
    fill(3, m3, p3)


def deep_bands(geo, lats, lat, level, source, lo, hi, gain, bands):
    start, count = geo.band[level]
    in_start = geo.low[level - 1][0]
    parts = 2 if level == 2 else 1
    half = count // parts
    for b in range(parts):
        if parts == 1:
            at, size = 0, source.shape[0]
            vh, vl = two_terms(source[...])
        else:
            at = (2 * (start + half * b) - 3 - in_start) // 16 * 16
            size = 2 * half + 16
            vh, vl = source[0][at : at + size, :], source[1][at : at + size, :]
        matrix = analysis_matrix(HIGH, start + half * b, half, in_start + at, size)
        matrix = masked_rows(matrix, start + half * b, geo.rows[level], lat, lats)
        hi[half * b : half * (b + 1), :] = dot3(matrix, vh, vl)
    skip = start - geo.low[level][0]
    band_rows(geo, level, lo, skip, hi, geo.span[level - 1][0], gain, bands)


def sides_kernel(place, x, side_e, side_o, sems):
    parity = place[1] % 2
    width, lanes = x.shape[1], side_e.shape[1]

    def both(low, high):
        copies = [
            pltpu.make_async_copy(x.at[:, pl.ds(0, lanes)], low, sems.at[0]),
            pltpu.make_async_copy(x.at[:, pl.ds(width - lanes, lanes)], high, sems.at[1]),
        ]
        for copy in copies:
            copy.start()
        for copy in copies:
            copy.wait()

    @pl.when(parity == 0)
    def _():
        both(side_o, side_e)

    @pl.when(parity != 0)
    def _():
        both(side_e, side_o)


def corners_kernel(place, side_e, side_o, out):
    lat, parity = place[0], place[1] % 2
    rows, lanes = side_e.shape
    at = jnp.where(lat == 0, rows - NEAR, 0)
    window = pl.ds(pl.multiple_of(at, NEAR), NEAR)

    @pl.when(parity == 0)
    def _():
        out[:, 0:lanes] = side_o[window, :]
        out[:, lanes:] = side_e[window, :]

    @pl.when(parity != 0)
    def _():
        out[:, 0:lanes] = side_e[window, :]
        out[:, lanes:] = side_o[window, :]


def merge_kernel(size, more, place, mine, other, out):
    width = mine.shape[1]

    def add(lower, upper):
        out[:, 0:more] = lower[:, 0:more]
        out[:, more:width] = lower[:, more:] + upper[:, 0 : width - more]
        out[:, width:] = upper[:, width - more :]

    lower_half = (place[1] // size) % 2 == 0

    @pl.when(lower_half)
    def _():
        add(mine, other)

    @pl.when(jnp.logical_not(lower_half))
    def _():
        add(other, mine)


def last_merge_kernel(geo, size, more, place, mine, other, ring, tokens, merged):
    merge_kernel(size, more, place, mine, other, merged)
    around = ring.shape[1]
    fold = merged.shape[1] - around
    ring[:, 0:fold] = merged[:, 0:fold] + merged[:, around:]
    ring[:, fold:] = merged[:, fold:around]
    skip = -geo.low[4][0]
    tokens[...] = ring[skip : skip + geo.rows[4], :].astype(BF16)


def first_level_kernel(geo, lats, place, edge, side_e, side_o, corner, gain, x, part, ext, la, ha, d1, xh, xl, sem):
    lat, parity = place[0], place[1] % 2
    rows, width = x.shape
    lanes = SIDE * C
    copy = pltpu.make_async_copy(x, ext.at[pl.ds(NEAR, rows), pl.ds(lanes, width)], sem)
    copy.start()
    sides = (slice(0, lanes), slice(lanes + width, width + 2 * lanes))
    own = slice(lanes, lanes + width)
    inner = slice(NEAR, NEAR + rows)

    def rims(near, far, edges):
        ext[far, :] = jnp.zeros((NEAR, width + 2 * lanes), BF16)
        ext[near, own] = edges
        ext[near, sides[0]] = corner[:, 0:lanes]
        ext[near, sides[1]] = corner[:, lanes:]

    top, bottom = slice(0, NEAR), slice(NEAR + rows, 2 * NEAR + rows)

    @pl.when(lat == 0)
    def _():
        rims(bottom, top, edge[0:NEAR, :])

    @pl.when(lat != 0)
    def _():
        rims(top, bottom, edge[HALO - NEAR :, :])

    @pl.when(parity == 0)
    def _():
        ext[inner, sides[0]] = side_o[...]
        ext[inner, sides[1]] = side_e[...]

    @pl.when(parity != 0)
    def _():
        ext[inner, sides[0]] = side_e[...]
        ext[inner, sides[1]] = side_o[...]

    start, count = geo.band[1]
    low = analysis_matrix(LOW, start, 120, -NEAR, 256)
    high = analysis_matrix(HIGH, start, 120, -NEAR, 256)
    copy.wait()
    for b in range(count // 120):
        data = ext[240 * b : 240 * b + 256, :]
        for matrix, out in ((low, la), (high, ha)):
            mh, ml = two_terms(masked_rows(matrix, start + 120 * b, geo.rows[1], lat, lats))
            out[120 * b : 120 * b + 120, :] = mxu(mh, data) + mxu(ml, data)
    band_rows(geo, 1, la, 0, ha, -SIDE, gain, d1)
    half = rows // 2
    ylow, yhigh = la, ha
    used = slice(0, d1.shape[2])
    for block in range(2):
        w = 0 if block == 0 else count - LANES
        window = slice(w, w + LANES)
        target = slice(half * block, half * (block + 1))
        matrix = synthesis_matrix(half * block, half, start + w, LANES)
        sh, sl = two_terms(matrix)
        xh[0:LANES, :], xl[0:LANES, :] = two_terms(d1[0, window, :])
        xh[LANES:, :], xl[LANES:, :] = two_terms(d1[2, window, :])
        yhigh[target, used] = mxu(sh, xh[...]) + mxu(sh, xl[...]) + mxu(sl, xh[...])
        vh, vl = two_terms(d1[1, window, :])
        sh, sl = sh[:, LANES:], sl[:, LANES:]
        ylow[target, used] = mxu(sh, vh) + mxu(sh, vl) + mxu(sl, vh)

    begin, pairs = geo.span[1]
    most = 232

    def chunk(i, carry):
        row = pl.multiple_of(i * most, 8)
        pair = synthesis(
            columns(ylow, row, most, pairs), columns(yhigh, row, most, pairs), begin, first_half(most)
        )
        for q in range(geo.cells[0] // 2):
            put(part, row, q, pair(2 * q))
        return carry

    lax.fori_loop(0, rows // most, chunk, 0)


def exchange_plan(geo):
    plan = {}
    for distance in (1, 2, 3):
        entries, row = [], 0
        for level in (2, 3, 4):
            count = geo.span[level][1] - distance * geo.cells[level] // 2
            if count > 0:
                entries.append((level, count, row))
                row += -(-geo.band[level][1] // 16) * 16
        plan[distance] = entries
    return plan


def plan_shape(geo, distance):
    entries = exchange_plan(geo)[distance]
    rows = sum(-(-geo.band[level][1] // 16) * 16 for level, _, _ in entries)
    return (rows, max(count for _, count, _ in entries) * 3 * LANES)


def attention_kernel(geo, lats, blocks, place, ring, own, others, we, wqkv, scale, wo, gain, wb, out, around, listed, keys):
    lat, lon = place[0], place[1]
    rows, width = out.shape
    cells = width // C
    total = ring.shape[1]
    around[:, 0:total] = ring[...]
    around[:, total:] = ring[:, 0 : around.shape[1] - total]
    field = around[:, pl.ds(pl.multiple_of(lon * (geo.cells[4] * C), LANES), width)]
    count = geo.rows[4]
    for source, shift in ((own, 0), (others, count)):
        for pair in range(total // LANES):
            value = source[:, pair * LANES : (pair + 1) * LANES].astype(F32)
            for side in range(2):
                at = 2 * count * (2 * pair + side) + shift
                listed[at : at + count, :] = value[:, side * C : (side + 1) * C]
    keys[...] = listed[...].astype(BF16)
    own = jnp.concatenate([field[:, C * c : C * (c + 1)] for c in range(cells)], 0)
    count = own.shape[0]
    embedded = mxu(own.astype(BF16), we[...])
    queries = mxu(embedded.astype(BF16), wqkv[:, 0:E]).astype(BF16)
    lane = lax.broadcasted_iota(jnp.int32, (1, E), 1)
    block = keys.shape[0] // blocks
    factor = [scale[h] * (1.0 / math.sqrt(HEAD_DIM)) for h in range(HEADS)]

    def keyvals(start):
        spread = mxu(keys[pl.ds(start, block), :], we[...]).astype(BF16)
        both = mxu(spread, wqkv[:, E : 3 * E]).astype(BF16)
        return both[:, 0:E], both[:, E : 2 * E]

    def scores_of(h, k):
        mine = (lane >= h * HEAD_DIM) & (lane < (h + 1) * HEAD_DIM)
        q = jnp.where(mine, queries, jnp.zeros_like(queries))
        s = lax.dot_general(q, k, (((1,), (1,)), ((), ())), preferred_element_type=F32)
        return s * factor[h]

    def masked(h, value):
        mine = (lane >= h * HEAD_DIM) & (lane < (h + 1) * HEAD_DIM)
        return jnp.where(mine, value, jnp.zeros_like(value))

    if blocks == 1:
        k, v = keyvals(0)
        attended = jnp.zeros((count, E), F32)
        for h in range(HEADS):
            s = scores_of(h, k)
            w = jnp.exp(s - jnp.max(s, -1, keepdims=True))
            total = jnp.sum(w, -1, keepdims=True)
            attended = attended + masked(h, mxu(w.astype(BF16), v) / total)
    else:

        def one_block(b, carry):
            peaks, totals, sums = carry
            k, v = keyvals(pl.multiple_of(b * block, 16))
            new_peaks, new_totals = [], []
            shrunk = jnp.zeros((count, E), F32)
            for h in range(HEADS):
                s = scores_of(h, k)
                peak = jnp.maximum(peaks[h], jnp.max(s, -1, keepdims=True))
                shrink = jnp.exp(peaks[h] - peak)
                w = jnp.exp(s - peak)
                new_peaks.append(peak)
                new_totals.append(totals[h] * shrink + jnp.sum(w, -1, keepdims=True))
                shrunk = shrunk + masked(h, sums * shrink + mxu(w.astype(BF16), v))
            return tuple(new_peaks), tuple(new_totals), shrunk

        start = (
            tuple(jnp.full((count, 1), -1e30, F32) for _ in range(HEADS)),
            tuple(jnp.zeros((count, 1), F32) for _ in range(HEADS)),
            jnp.zeros((count, E), F32),
        )
        _, totals, sums = lax.fori_loop(0, blocks, one_block, start)
        attended = jnp.zeros((count, E), F32)
        for h in range(HEADS):
            attended = attended + masked(h, sums / totals[h])
    hidden = embedded + mxu(attended.astype(BF16), wo[...])
    square = jnp.mean(hidden * hidden, -1, keepdims=True)
    normed = (hidden * lax.rsqrt(square + 1e-06) * gain[...]).astype(BF16)
    update = lax.dot_general(
        normed, wb[...], (((1,), (1,)), ((), ())), preferred_element_type=F32
    )
    back = [
        jnp.concatenate(
            [update[rows * c : rows * (c + 1), :], update[rows * (c + 1) : rows * (c + 2), :]], 1
        )
        for c in range(0, cells, 2)
    ]
    start = geo.band[4][0]
    for q, value in enumerate(back):
        at = slice(q * LANES, (q + 1) * LANES)
        out[:, at] = masked_rows(field[:, at] + value, start, geo.rows[4], lat, lats)


def synthesis_kernel(geo, lats, place, coarse, e2, o2, from_m2, from_p2, from_m3, from_p3, *refs):
    lat, parity = place[0], place[1] % 2
    part, d2, d3, d4, out, up3, up2, up1, ylow, yhigh, done, sems = refs
    bands = {2: d2, 3: d3, 4: d4}
    plan = exchange_plan(geo)

    def from_sides(level, b):
        n = geo.band[level][1]
        cols = [bands[level][b, :, LANES * p : LANES * (p + 1)] for p in range(geo.span[level][1])]
        for distance in (1, 2, 3):
            for which, count, row in plan[distance]:
                if which != level:
                    continue
                move = distance * geo.cells[level] // 2
                for p in range(count):
                    lanes = slice((b * count + p) * LANES, (b * count + p + 1) * LANES)
                    if distance == 1:
                        even = e2[row : row + n, lanes].astype(F32)
                        odd = o2[row : row + n, lanes].astype(F32)
                        low = jnp.where(parity == 0, odd, even)
                        high = jnp.where(parity == 0, even, odd)
                    else:
                        lows, highs = {2: (from_m2, from_p2), 3: (from_m3, from_p3)}[distance]
                        low = lows[row : row + n, lanes].astype(F32)
                        high = highs[row : row + n, lanes].astype(F32)
                    cols[p] = cols[p] + low
                    cols[p + move] = cols[p + move] + high
        return jnp.concatenate(cols, 1)

    uppers = {4: coarse, 3: up3, 2: up2, 1: up1}
    for level in (4, 3, 2):
        begin, pairs = geo.span[level]
        below = level - 1
        start, rows = geo.band[below]
        matrix = synthesis_matrix(start, rows, *geo.band[level])
        matrix = masked_rows(matrix, start, geo.rows[below], lat, lats)
        width = pairs * LANES
        for one, two, y in (
            (uppers[level][...], from_sides(level, 1), ylow),
            (from_sides(level, 0), from_sides(level, 2), yhigh),
        ):
            h, l = two_terms(jnp.concatenate([one, two], 0))
            y[0:rows, 0:width] = dot3(matrix, h, l)
        target = uppers[below]
        first, out_pairs = geo.span[below]

        step = best_step(rows)
        left = first_half(step)

        def joined(c, carry):
            row = pl.multiple_of(c * step, step)
            pair = synthesis(
                columns(ylow, row, step, pairs), columns(yhigh, row, step, pairs), begin, left
            )
            for q in range(out_pairs):
                put(target, row, q, pair(first + 2 * q))
            return carry

        lax.fori_loop(0, rows // step, joined, 0)

    n = geo.band[1][1]
    half = geo.rows[0] // 2
    for block in range(2):
        w = 0 if block == 0 else n - LANES
        matrix = synthesis_matrix(half * block, half, geo.band[1][0] + w, LANES)
        h, l = two_terms(up1[w : w + LANES, :])
        ylow[half * block : half * (block + 1), :] = dot3(matrix[:, 0:LANES], h, l)
    begin, pairs = geo.span[1]
    most = 112

    def last(row, count):
        left = first_half(count)
        pair = synthesis_of_lows(columns(ylow, row, count), begin, left)
        for q in range(geo.cells[0] // 2):
            more = part[pl.ds(row, count), pl.ds(LANES * q, LANES)]
            put(done, row, q, (pair(2 * q) + more).astype(BF16))

    def store(i, count):
        part = pl.ds(pl.multiple_of(i * most, 16), count)
        return pltpu.make_async_copy(done.at[part, :], out.at[part, :], sems.at[i])

    whole, rest = geo.rows[0] // most, geo.rows[0] % most

    def chunk(i, carry):
        last(pl.multiple_of(i * most, 16), most)
        store(i, most).start()
        return carry

    lax.fori_loop(0, whole, chunk, 0)
    if rest:
        last(whole * most, rest)
        store(whole, rest).start()
    for i in range(whole):
        store(i, most).wait()
    if rest:
        store(whole, rest).wait()


def call(kernel, out_shape, scratch, *args, cost=20_000_000, grant=24, raw=(), raw_out=(), stay=()):
    vmem = pl.BlockSpec(memory_space=pltpu.VMEM)
    smem = pl.BlockSpec(memory_space=pltpu.SMEM)
    anywhere = pl.BlockSpec(memory_space=pl.ANY)
    specs = [smem if a.ndim == 1 and a.size < 16 else vmem for a in args]
    for at in raw:
        specs[at] = anywhere
    held = lambda a: pltpu.with_memory_space_constraint(a, pltpu.HBM)
    args = [held(a) if i in stay else a for i, a in enumerate(args)]
    outs = [anywhere if i in raw_out else vmem for i in range(len(out_shape))]
    return pl.pallas_call(
        kernel,
        out_shape=tuple(out_shape),
        in_specs=specs,
        out_specs=tuple(outs),
        scratch_shapes=scratch,
        compiler_params=pltpu.CompilerParams(vmem_limit_bytes=grant << 20),
        cost_estimate=pl.CostEstimate(flops=cost, bytes_accessed=1 << 20, transcendentals=0),
    )(*args)


def shape(dims, dtype=F32):
    return jax.ShapeDtypeStruct(dims, dtype)


def per_device(mesh_shape, state_field, skip_gain, embed_weight, qkv_weight, head_scale, out_weight, norm_gain, back_weight):
    return program(
        mesh_shape, state_field, skip_gain, embed_weight, qkv_weight, head_scale, out_weight, norm_gain, back_weight
    )


def program(mesh_shape, state_field, skip_gain, embed_weight, qkv_weight, head_scale, out_weight, norm_gain, back_weight):
    lons, lats = mesh_shape["lon"], mesh_shape["lat"]
    rows, width = state_field.shape
    geo = Geometry(rows, width // C)
    lat, lon = lax.axis_index("lat"), lax.axis_index("lon")
    place = jnp.stack([lat, lon]).astype(jnp.int32)

    even_pairs = [(i, i ^ 1) for i in range(lons)]
    odd_pairs = [(i, (i + 1 if i % 2 else i - 1) % lons) for i in range(lons)]
    swap = [(i, lats - 1 - i) for i in range(lats)]

    def shifted(value, by):
        return lax.ppermute(value, "lon", [(i, (i + by) % lons) for i in range(lons)])

    edge = lax.dynamic_slice(
        state_field, (jnp.where(lat == 0, rows - HALO, 0), 0), (HALO, width)
    )
    edge = lax.ppermute(edge, "lat", swap)

    wide = SIDE * C
    extended = NEAR + rows + NEAR
    side_e, side_o = call(
        sides_kernel,
        [shape((rows, wide), BF16)] * 2,
        [pltpu.SemaphoreType.DMA((2,))],
        place,
        state_field,
        raw=(1,),
        stay=(1,),
        cost=1_000_000,
    )
    side_e = lax.ppermute(side_e, "lon", even_pairs)
    side_o = lax.ppermute(side_o, "lon", odd_pairs)

    w = [None] + [geo.span[level][1] * LANES for level in (1, 2, 3, 4)]
    low = lambda level, lanes: pltpu.VMEM((geo.low[level][1], w[lanes]), F32)
    bands = [(3, geo.band[level][1], w[level]) for level in (1, 2, 3, 4)]
    ll4, d2, d3, d4, deep_e, deep_o, p2, m2, p3, m3 = call(
        functools.partial(analysis_kernel, geo, lats),
        [shape((geo.low[4][1], w[4]))]
        + [shape(dims) for dims in bands[1:]]
        + [shape(plan_shape(geo, d), BF16) for d in (1, 1, 2, 2, 3, 3)],
        [
            pltpu.VMEM((geo.extended, width), BF16),
            pltpu.VMEM((geo.low[1][1], width), F32),
            low(1, 1),
            pltpu.VMEM((geo.low[1][1], w[1]), BF16),
            pltpu.VMEM((geo.low[1][1], w[1]), BF16),
            low(2, 1),
            low(2, 2),
            low(3, 2),
            low(3, 3),
            low(4, 3),
        ]
        + [pltpu.VMEM((geo.band[level][1], w[level - 1]), F32) for level in (2, 3, 4)]
        + [pltpu.SemaphoreType.DMA((geo.low[1][1] // 112,))],
        place,
        edge,
        skip_gain,
        state_field,
        raw=(3,),
        stay=(3,),
    )
    (corner,) = call(
        corners_kernel, [shape((NEAR, 2 * wide), BF16)], [], place, side_e, side_o, cost=100_000
    )
    corner = lax.ppermute(corner, "lat", swap)
    (part,) = call(
        functools.partial(first_level_kernel, geo, lats),
        [shape((rows, width))],
        [
            pltpu.VMEM((extended, width + 2 * wide), BF16),
            pltpu.VMEM((rows, width + 2 * wide), F32),
            pltpu.VMEM((rows, width + 2 * wide), F32),
            pltpu.VMEM(bands[0], F32),
            pltpu.VMEM((2 * LANES, w[1]), BF16),
            pltpu.VMEM((2 * LANES, w[1]), BF16),
            pltpu.SemaphoreType.DMA,
        ],
        place,
        edge,
        side_e,
        side_o,
        corner,
        skip_gain,
        state_field,
        raw=(6,),
        stay=(6,),
        grant=30,
    )

    merged, size = ll4, 1
    total = geo.cells[4] * lons * C
    while size < lons:
        other = lax.ppermute(merged, "lon", [(i, i ^ size) for i in range(lons)])
        more = geo.cells[4] * C * size
        dims = (merged.shape[0], merged.shape[1] + more)
        if 2 * size < lons:
            (merged,) = call(
                functools.partial(merge_kernel, size, more), [shape(dims)], [], place, merged, other, cost=100_000
            )
        else:
            ring, tokens = call(
                functools.partial(last_merge_kernel, geo, size, more),
                [shape((dims[0], total)), shape((geo.rows[4], total), BF16)],
                [pltpu.VMEM(dims, F32)],
                place,
                merged,
                other,
                cost=100_000,
            )
        size = 2 * size
    others = lax.ppermute(tokens, "lat", swap)

    deep_e = lax.ppermute(deep_e, "lon", even_pairs)
    deep_o = lax.ppermute(deep_o, "lon", odd_pairs)
    from_m2, from_p2 = shifted(p2, 2), shifted(m2, -2)
    from_m3, from_p3 = shifted(p3, 3), shifted(m3, -3)

    key_count = 2 * geo.rows[4] * geo.cells[4] * lons
    blocks = key_count // 928 if key_count % 928 == 0 else 1
    (coarse,) = call(
        functools.partial(attention_kernel, geo, lats, blocks),
        [shape((geo.low[4][1], w[4]))],
        [
            pltpu.VMEM((geo.low[4][1], total + 6 * C), F32),
            pltpu.VMEM((key_count, C), F32),
            pltpu.VMEM((key_count, C), BF16),
        ],
        place,
        ring,
        tokens,
        others,
        embed_weight,
        qkv_weight,
        head_scale,
        out_weight,
        norm_gain[None],
        back_weight.T,
        cost=200_000_000,
        grant=40,
    )

    (out,) = call(
        functools.partial(synthesis_kernel, geo, lats),
        [shape((rows, width), BF16)],
        [pltpu.VMEM((geo.band[level][1], w[level]), F32) for level in (3, 2, 1)]
        + [
            pltpu.VMEM((rows, w[1]), F32),
            pltpu.VMEM((geo.band[1][1], w[2]), F32),
            pltpu.VMEM((rows, width), BF16),
            pltpu.SemaphoreType.DMA((rows // 112 + 1,)),
        ],
        place,
        coarse,
        deep_e,
        deep_o,
        from_m2,
        from_p2,
        from_m3,
        from_p3,
        part,
        d2,
        d3,
        d4,
        raw_out=(0,),
        grant=30,
    )
    return out


def solution(mesh):
    in_specs = (P("lat", ("member", "lon")), P(), P(), P(), P(), P(), P(), P())
    out_specs = P("lat", ("member", "lon"))
    return jax.shard_map(
        functools.partial(per_device, dict(mesh.shape)),
        mesh=mesh,
        in_specs=in_specs,
        out_specs=out_specs,
        check_vma=False,
    )
```

```python
import functools
import math

import jax
import jax.numpy as jnp
import numpy as np
from jax import lax
from jax.experimental import pallas as pl
from jax.experimental.pallas import tpu as pltpu
from jax.sharding import PartitionSpec as P


C = 64
HEADS = 8
HEAD_DIM = 32
E = 256
LANES = 128
HALO = 96
LEAD = 16

LOW = np.array(
    [
        -0.010597401784997278,
        0.032883011666982945,
        0.030841381835986965,
        -0.18703481171888114,
        -0.02798376941698385,
        0.6308807679295904,
        0.7148465705525415,
        0.23037781330885523,
    ]
)
HIGH = np.array([(-1.0) ** j * LOW[7 - j] for j in range(8)])


F32 = jnp.float32
BF16 = jnp.bfloat16


def two_terms(value):
    top = value.astype(BF16)
    return top, (value - top.astype(F32)).astype(BF16)


def masked_rows(matrix, start, count, lat, lats):
    row = lax.broadcasted_iota(jnp.int32, matrix.shape, 0) + (start + lat * count)
    return jnp.where((row >= 0) & (row < count * lats), matrix, 0.0)


def banded(shape, low, high, row_factor, column_factor, offset):
    row = lax.broadcasted_iota(jnp.int32, shape, 0)
    column = lax.broadcasted_iota(jnp.int32, shape, 1)
    tap = row_factor * row + column_factor * column + offset
    if high is not None:
        second = column >= shape[1] // 2
        tap = jnp.where(second, tap - column_factor * (shape[1] // 2), tap)
    matrix = jnp.zeros(shape, F32)
    for t in range(8):
        value = F32(low[t]) if high is None else jnp.where(second, F32(high[t]), F32(low[t]))
        matrix = jnp.where(tap == t, value, matrix)
    return matrix


def analysis_matrix(taps, out_start, out_rows, in_start, in_rows):
    return banded((out_rows, in_rows), taps, None, -2, 1, in_start + 3 - 2 * out_start)


def synthesis_matrix(out_start, out_rows, in_start, in_rows):
    shape = (out_rows, 2 * in_rows)
    return banded(shape, LOW, HIGH, 1, -2, out_start - 2 * in_start + 3)


def mxu(a, b):
    return jnp.dot(a, b, preferred_element_type=F32)


def dot3(matrix, vh, vl):
    mh, ml = two_terms(matrix)
    return mxu(mh, vh) + mxu(mh, vl) + mxu(ml, vh)


def first_half(rows):
    return lax.broadcasted_iota(jnp.int32, (rows, LANES), 1) < C


def half_turn(value):
    return None if value is None else pltpu.roll(value, C, 1)


def pick(left, a, b):
    if a is None and b is None:
        return None
    return jnp.where(left, 0.0 if a is None else a, 0.0 if b is None else b)


def plus(a, b, factor):
    if b is None:
        return a
    if a is None:
        return b * factor
    return a + b * factor


class Memo:
    def __init__(self, make):
        self.make, self.known = make, {}

    def __call__(self, n):
        if n not in self.known:
            self.known[n] = self.make(n)
        return self.known[n]


def analysis(cols, start, left):
    turned = Memo(lambda i: half_turn(cols[i]) if 0 <= i < len(cols) else None)
    plain = lambda i: cols[i] if 0 <= i < len(cols) else None
    if start % 2 == 0:
        at = lambda n: n - 1 - start // 2
        u = Memo(lambda n: pick(left, turned(at(n) - 1), plain(at(n))))
        w = Memo(lambda n: pick(left, plain(at(n)), turned(at(n) + 1)))
    else:
        at = lambda n: n - (start + 3) // 2
        u = Memo(lambda n: pick(left, plain(at(n)), turned(at(n) + 1)))
        w = Memo(lambda n: pick(left, turned(at(n)), plain(at(n) + 1)))

    def band(taps):
        def make(k):
            total = None
            for step in range(4):
                total = plus(total, u(k + step), float(taps[2 * step]))
                total = plus(total, w(k + step), float(taps[2 * step + 1]))
            return total

        return make

    return band(LOW), band(HIGH)


def synthesis(lows, highs, start, left):
    parity = start % 2

    def cells(cols):
        col = lambda k: cols[(k - start) // 2] if 0 <= k - start < 2 * len(cols) else None
        turned = Memo(lambda k: half_turn(col(k)))

        def at(k):
            if k % 2 == parity:
                return col(k)
            return pick(left, turned(k - 1), turned(k + 1))

        return Memo(at)

    sources = ((cells(lows), LOW), (cells(highs), HIGH))

    def output(first):
        def make(n):
            total = None
            for step in range(4):
                for source, taps in sources:
                    total = plus(total, source(n - step), float(taps[2 * step + first]))
            return total

        return Memo(make)

    u, w = output(0), output(1)
    u_turned, w_turned = Memo(lambda n: half_turn(u(n))), Memo(lambda n: half_turn(w(n)))

    def pair(m):
        if m % 2:
            n = (m + 3) // 2
            if n % 2 == parity:
                return pick(left, u(n), w_turned(n))
            return pick(left, u_turned(n - 1), w(n - 1))
        n = m // 2 + 1
        if n % 2 == parity:
            return pick(left, w(n), u(n))
        return pick(left, w_turned(n - 1), u_turned(n + 1))

    return pair


def synthesis_of_lows(lows, start, left):
    def dup(k):
        i = (k - start) // 2
        if not 0 <= i < len(lows):
            return None
        turned = rolled(i)
        return jnp.where(left, lows[i], turned) if (k - start) % 2 == 0 else jnp.where(left, turned, lows[i])

    rolled = Memo(lambda i: half_turn(lows[i]))
    both = Memo(dup)

    def tap(t):
        return F32(LOW[t]) if 0 <= t < 8 else F32(0.0)

    weights = [jnp.where(left[0:8], tap(7 - 2 * i), tap(8 - 2 * i)) for i in range(5)]
    weights = [jnp.concatenate([v] * (left.shape[0] // 8), 0) for v in weights]

    def pair(m):
        total = None
        for i in range(5):
            cell = both(m // 2 - 2 + i)
            if cell is not None:
                total = cell * weights[i] if total is None else total + cell * weights[i]
        return total

    return pair


def columns(ref, row, rows, count=None):
    count = ref.shape[-1] // LANES if count is None else count
    return [ref[pl.ds(row, rows), pl.ds(LANES * p, LANES)] for p in range(count)]


def put(ref, row, p, value, lead=()):
    ref[lead + (pl.ds(row, value.shape[0]), pl.ds(LANES * p, LANES))] = value


class Geometry:
    def __init__(self, rows, cells):
        self.rows = [rows >> level for level in range(5)]
        self.cells = [cells >> level for level in range(5)]
        up = lambda value, step: -(-value // step) * step
        self.band = [
            None,
            (-4, up(self.rows[1] + 4, 120)),
            (-8, up(self.rows[2] + 11, 16)),
            (-3, up(self.rows[3] + 6, 8)),
            (-3, up(self.rows[4] + 6, 8)),
        ]
        self.low = [
            None,
            (-52, up(self.rows[1] + 97, 112)),
            (-24, up(self.rows[2] + 45, 88)),
            (-11, up(self.rows[3] + 20, 8)),
            (-3, up(self.rows[4] + 6, 8)),
        ]
        self.span = [None, (-2, self.cells[1] // 2 + 2)]
        for level in (2, 3, 4):
            self.span.append((-3, self.cells[level] // 2 + 3))
        self.extended = max(
            LEAD + 2 * HALO + rows, 2 * (self.low[1][1] - 112) + 256
        )


STEP = 240
SIDE = 8
NEAR = 16


def best_step(rows, most=None):
    return max(s for s in range(8, (most or STEP) + 1, 8) if rows % s == 0)


def low_rows(geo, level, source, source_start, target):
    first, pairs = geo.span[level]
    rows = geo.low[level][1]
    step = best_step(rows, 168)
    left = first_half(step)

    def body(c, carry):
        row = pl.multiple_of(c * step, step)
        low, _ = analysis(columns(source, row, step), source_start, left)
        for q in range(pairs):
            put(target, row, q, low(first + 2 * q))
        return carry

    lax.fori_loop(0, rows // step, body, 0)


def band_rows(geo, level, lo, skip, hi, source_start, gain, bands):
    first, pairs = geo.span[level]
    rows = geo.band[level][1]
    step = best_step(rows)
    left = first_half(step)

    def body(c, carry):
        row = pl.multiple_of(c * step, step)
        g = []
        for b in range(3):
            one = gain[level - 1, b : b + 1, :]
            g.append(jnp.broadcast_to(jnp.concatenate([one, one], 1), (step, LANES)))
        _, high = analysis(columns(lo, row + skip, step), source_start, left)
        for q in range(pairs):
            put(bands, row, q, high(first + 2 * q) * g[0], (0,))
        low, high = analysis(columns(hi, row, step), source_start, left)
        for q in range(pairs):
            put(bands, row, q, low(first + 2 * q) * g[1], (1,))
            put(bands, row, q, high(first + 2 * q) * g[2], (2,))
        return carry

    lax.fori_loop(0, rows // step, body, 0)


def analysis_kernel(geo, lats, place, edge, gain, x, *refs):
    lat, parity = place[0], place[1] % 2
    ll4, d2, d3, d4, send_e, send_o, p2, m2, p3, m3 = refs[:10]
    ext, la, g1, gh, gl, lo2, g2, lo3, g3, lo4, hi2, hi3, hi4, sems = refs[10:]
    rows = geo.rows[0]
    start, count = geo.low[1]
    width = x.shape[1]
    begin = LEAD + HALO
    blocks = count // 112
    cuts = [0] + [min(rows, 224 * b + 256 - begin) for b in range(blocks - 1)] + [rows]
    copies = []
    for i in range(blocks):
        part = pl.ds(cuts[i], cuts[i + 1] - cuts[i])
        to = pl.ds(begin + cuts[i], cuts[i + 1] - cuts[i])
        copies.append(pltpu.make_async_copy(x.at[part, :], ext.at[to, :], sems.at[i]))
        copies[-1].start()
    top = slice(LEAD, begin)
    bottom = slice(begin + rows, begin + rows + HALO)
    ext[0:LEAD, :] = jnp.zeros((LEAD, width), BF16)
    tail = geo.extended - (LEAD + 2 * HALO + rows)
    if tail:
        ext[geo.extended - tail :, :] = jnp.zeros((tail, width), BF16)

    @pl.when(lat == 0)
    def _():
        ext[top, :] = jnp.zeros((HALO, width), BF16)
        ext[bottom, :] = edge[...]

    @pl.when(lat != 0)
    def _():
        ext[top, :] = edge[...]
        ext[bottom, :] = jnp.zeros((HALO, width), BF16)

    base = analysis_matrix(LOW, start, 112, 0 - LEAD - HALO, 256)
    for b in range(blocks):
        copies[b].wait()
        mh, ml = two_terms(masked_rows(base, start + 112 * b, geo.rows[1], lat, lats))
        data = ext[224 * b : 224 * b + 256, :]
        la[112 * b : 112 * b + 112, :] = mxu(mh, data) + mxu(ml, data)
    low_rows(geo, 1, la, 0, g1)
    gh[...], gl[...] = two_terms(g1[...])
    out_start, out_rows = geo.low[2]
    for b in range(out_rows // 88):
        at = min(176 * b, count - 192)
        window = slice(at, at + 192)
        matrix = analysis_matrix(LOW, out_start + 88 * b, 88, start + at, 192)
        matrix = masked_rows(matrix, out_start + 88 * b, geo.rows[2], lat, lats)
        lo2[88 * b : 88 * b + 88, :] = dot3(matrix, gh[window, :], gl[window, :])
    low_rows(geo, 2, lo2, geo.span[1][0], g2)
    for level, source, lo, target in ((3, g2, lo3, g3), (4, g3, lo4, ll4)):
        vh, vl = two_terms(source[...])
        matrix = analysis_matrix(LOW, *geo.low[level], *geo.low[level - 1])
        matrix = masked_rows(matrix, geo.low[level][0], geo.rows[level], lat, lats)
        lo[...] = dot3(matrix, vh, vl)
        low_rows(geo, level, lo, geo.span[level - 1][0], target)
    d = {2: d2, 3: d3, 4: d4}
    for level, lo, hi in ((2, lo2, hi2), (3, lo3, hi3), (4, lo4, hi4)):
        deep_bands(geo, lats, lat, level, {2: (gh, gl), 3: g2, 4: g3}[level], lo, hi, gain, d[level])

    def fill(distance, to_left, to_right):
        for level, count, row in exchange_plan(geo)[distance]:
            n = geo.band[level][1]
            move = distance * geo.cells[level] // 2
            for b in range(3):
                lanes = slice(b * count * LANES, (b + 1) * count * LANES)
                to_left[row : row + n, lanes] = d[level][b, :, 0 : count * LANES].astype(BF16)
                to_right[row : row + n, lanes] = d[level][
                    b, :, move * LANES : (move + count) * LANES
                ].astype(BF16)

    @pl.when(parity == 0)
    def _():
        fill(1, send_o, send_e)

    @pl.when(parity != 0)
    def _():
        fill(1, send_e, send_o)

    fill(2, m2, p2)
    fill(3, m3, p3)


def deep_bands(geo, lats, lat, level, source, lo, hi, gain, bands):
    start, count = geo.band[level]
    in_start = geo.low[level - 1][0]
    parts = 2 if level == 2 else 1
    half = count // parts
    for b in range(parts):
        if parts == 1:
            at, size = 0, source.shape[0]
            vh, vl = two_terms(source[...])
        else:
            at = (2 * (start + half * b) - 3 - in_start) // 16 * 16
            size = 2 * half + 16
            vh, vl = source[0][at : at + size, :], source[1][at : at + size, :]
        matrix = analysis_matrix(HIGH, start + half * b, half, in_start + at, size)
        matrix = masked_rows(matrix, start + half * b, geo.rows[level], lat, lats)
        hi[half * b : half * (b + 1), :] = dot3(matrix, vh, vl)
    skip = start - geo.low[level][0]
    band_rows(geo, level, lo, skip, hi, geo.span[level - 1][0], gain, bands)


def sides_kernel(place, x, side_e, side_o, sems):
    parity = place[1] % 2
    width, lanes = x.shape[1], side_e.shape[1]

    def both(low, high):
        copies = [
            pltpu.make_async_copy(x.at[:, pl.ds(0, lanes)], low, sems.at[0]),
            pltpu.make_async_copy(x.at[:, pl.ds(width - lanes, lanes)], high, sems.at[1]),
        ]
        for copy in copies:
            copy.start()
        for copy in copies:
            copy.wait()

    @pl.when(parity == 0)
    def _():
        both(side_o, side_e)

    @pl.when(parity != 0)
    def _():
        both(side_e, side_o)


def corners_kernel(place, side_e, side_o, out):
    lat, parity = place[0], place[1] % 2
    rows, lanes = side_e.shape
    at = jnp.where(lat == 0, rows - NEAR, 0)
    window = pl.ds(pl.multiple_of(at, NEAR), NEAR)

    @pl.when(parity == 0)
    def _():
        out[:, 0:lanes] = side_o[window, :]
        out[:, lanes:] = side_e[window, :]

    @pl.when(parity != 0)
    def _():
        out[:, 0:lanes] = side_e[window, :]
        out[:, lanes:] = side_o[window, :]


def merge_kernel(size, more, place, mine, other, out):
    width = mine.shape[1]

    def add(lower, upper):
        out[:, 0:more] = lower[:, 0:more]
        out[:, more:width] = lower[:, more:] + upper[:, 0 : width - more]
        out[:, width:] = upper[:, width - more :]

    lower_half = (place[1] // size) % 2 == 0

    @pl.when(lower_half)
    def _():
        add(mine, other)

    @pl.when(jnp.logical_not(lower_half))
    def _():
        add(other, mine)


def last_merge_kernel(geo, size, more, place, mine, other, ring, tokens, merged):
    merge_kernel(size, more, place, mine, other, merged)
    around = ring.shape[1]
    fold = merged.shape[1] - around
    ring[:, 0:fold] = merged[:, 0:fold] + merged[:, around:]
    ring[:, fold:] = merged[:, fold:around]
    skip = -geo.low[4][0]
    tokens[...] = ring[skip : skip + geo.rows[4], :].astype(BF16)


def latitude_bands(geo, lats, lat, ext, la, ha):
    start, count = geo.band[1]
    low = analysis_matrix(LOW, start, 120, -NEAR, 256)
    high = analysis_matrix(HIGH, start, 120, -NEAR, 256)
    for b in range(count // 120):
        data = ext[240 * b : 240 * b + 256, :]
        for matrix, out in ((low, la), (high, ha)):
            mh, ml = two_terms(masked_rows(matrix, start + 120 * b, geo.rows[1], lat, lats))
            out[120 * b : 120 * b + 120, :] = mxu(mh, data) + mxu(ml, data)


def first_bands(row, los, his, start, groups, gain, bands):
    step = los[0].shape[0]
    left = first_half(step)
    g = []
    for b in range(3):
        one = gain[0, b : b + 1, :]
        g.append(jnp.broadcast_to(jnp.concatenate([one, one], 1), (step, LANES)))
    _, high = analysis(los, start, left)
    for q, k in groups:
        put(bands, row, q, high(k) * g[0], (0,))
    low, high = analysis(his, start, left)
    for q, k in groups:
        put(bands, row, q, low(k) * g[1], (1,))
        put(bands, row, q, high(k) * g[2], (2,))


def edge_pairs():
    return 2


def inner_kernel(geo, lats, place, edge, gain, x, d1, lo_rim, hi_rim, ext, la, ha, sem):
    lat = place[0]
    rows, width = x.shape
    copy = pltpu.make_async_copy(x, ext.at[pl.ds(NEAR, rows), :], sem)
    copy.start()

    @pl.when(lat == 0)
    def _():
        ext[0:NEAR, :] = jnp.zeros((NEAR, width), BF16)
        ext[NEAR + rows :, :] = edge[0:NEAR, :]

    @pl.when(lat != 0)
    def _():
        ext[0:NEAR, :] = edge[HALO - NEAR :, :]
        ext[NEAR + rows :, :] = jnp.zeros((NEAR, width), BF16)

    copy.wait()
    latitude_bands(geo, lats, lat, ext, la, ha)
    rim = SIDE * C
    for out, source in ((lo_rim, la), (hi_rim, ha)):
        out[:, 0:rim] = source[:, 0:rim]
        out[:, rim:] = source[:, width - rim :]
    first, pairs = geo.span[1]
    ends = edge_pairs()
    groups = [(q, first + 2 * q) for q in range(ends, pairs - ends)]
    step = best_step(geo.band[1][1])

    def body(c, carry):
        row = pl.multiple_of(c * step, step)
        first_bands(row, columns(la, row, step), columns(ha, row, step), 0, groups, gain, d1)
        return carry

    lax.fori_loop(0, geo.band[1][1] // step, body, 0)


def first_level_kernel(geo, lats, place, side_e, side_o, corner, gain, inner, lo_rim, hi_rim, part, ext, lo_side, hi_side, d1, la, ha, xh, xl):
    lat, parity = place[0], place[1] % 2
    rows, _ = part.shape
    lanes = SIDE * C
    sides = (slice(0, lanes), slice(lanes, 2 * lanes))
    own = slice(NEAR, NEAR + rows)
    top, bottom = slice(0, NEAR), slice(NEAR + rows, 2 * NEAR + rows)

    def rims(near, far):
        ext[far, :] = jnp.zeros((NEAR, 2 * lanes), BF16)
        ext[near, :] = corner[...]

    @pl.when(lat == 0)
    def _():
        rims(bottom, top)

    @pl.when(lat != 0)
    def _():
        rims(top, bottom)

    @pl.when(parity == 0)
    def _():
        ext[own, sides[0]] = side_o[...]
        ext[own, sides[1]] = side_e[...]

    @pl.when(parity != 0)
    def _():
        ext[own, sides[0]] = side_e[...]
        ext[own, sides[1]] = side_o[...]

    start, count = geo.band[1]
    latitude_bands(geo, lats, lat, ext, lo_side, hi_side)
    first, pairs = geo.span[1]
    ends = edge_pairs()
    step = best_step(count)
    beside = SIDE // 2

    def body(c, carry):
        row = pl.multiple_of(c * step, step)
        sources = [columns(ref, row, step) for ref in (lo_side, hi_side, lo_rim, hi_rim)]
        lo_s, hi_s, lo_r, hi_r = sources
        groups = [(q, first + 2 * q) for q in range(ends)]
        first_bands(
            row, lo_s[:beside] + lo_r[:beside], hi_s[:beside] + hi_r[:beside], -SIDE, groups, gain, d1
        )
        groups = [(ends + q, first + 2 * (pairs - ends + q)) for q in range(ends)]
        begin = geo.cells[0] - SIDE
        first_bands(
            row, lo_r[beside:] + lo_s[beside:], hi_r[beside:] + hi_s[beside:], begin, groups, gain, d1
        )
        return carry

    lax.fori_loop(0, count // step, body, 0)
    rim, whole = ends * LANES, pairs * LANES

    def terms(b, window, to):
        for lanes_to, source, lanes_from in (
            (slice(0, rim), d1, slice(0, rim)),
            (slice(rim, whole - rim), inner, slice(rim, whole - rim)),
            (slice(whole - rim, whole), d1, slice(rim, 2 * rim)),
        ):
            h, l = two_terms(source[b, window, lanes_from])
            xh[to, lanes_to], xl[to, lanes_to] = h, l

    half = rows // 2
    ylow, yhigh = la, ha
    used = slice(0, whole)
    upper, lower = slice(0, LANES), slice(LANES, 2 * LANES)
    for block in range(2):
        w = 0 if block == 0 else count - LANES
        window = slice(w, w + LANES)
        target = slice(half * block, half * (block + 1))
        matrix = synthesis_matrix(half * block, half, start + w, LANES)
        sh, sl = two_terms(matrix)
        terms(0, window, upper)
        terms(2, window, lower)
        yhigh[target, used] = mxu(sh, xh[...]) + mxu(sh, xl[...]) + mxu(sl, xh[...])
        terms(1, window, lower)
        sh, sl = sh[:, LANES:], sl[:, LANES:]
        vh, vl = xh[lower, :], xl[lower, :]
        ylow[target, used] = mxu(sh, vh) + mxu(sh, vl) + mxu(sl, vh)

    begin, pairs = geo.span[1]
    most = 232

    def chunk(i, carry):
        row = pl.multiple_of(i * most, 8)
        pair = synthesis(
            columns(ylow, row, most, pairs), columns(yhigh, row, most, pairs), begin, first_half(most)
        )
        for q in range(geo.cells[0] // 2):
            put(part, row, q, pair(2 * q))
        return carry

    lax.fori_loop(0, rows // most, chunk, 0)


def exchange_plan(geo):
    plan = {}
    for distance in (1, 2, 3):
        entries, row = [], 0
        for level in (2, 3, 4):
            count = geo.span[level][1] - distance * geo.cells[level] // 2
            if count > 0:
                entries.append((level, count, row))
                row += -(-geo.band[level][1] // 16) * 16
        plan[distance] = entries
    return plan


def plan_shape(geo, distance):
    entries = exchange_plan(geo)[distance]
    rows = sum(-(-geo.band[level][1] // 16) * 16 for level, _, _ in entries)
    return (rows, max(count for _, count, _ in entries) * 3 * LANES)


def attention_kernel(geo, lats, blocks, place, ring, own, others, we, wqkv, scale, wo, gain, wb, out, around, listed, keys):
    lat, lon = place[0], place[1]
    rows, width = out.shape
    cells = width // C
    total = ring.shape[1]
    around[:, 0:total] = ring[...]
    around[:, total:] = ring[:, 0 : around.shape[1] - total]
    field = around[:, pl.ds(pl.multiple_of(lon * (geo.cells[4] * C), LANES), width)]
    count = geo.rows[4]
    for source, shift in ((own, 0), (others, count)):
        for pair in range(total // LANES):
            value = source[:, pair * LANES : (pair + 1) * LANES].astype(F32)
            for side in range(2):
                at = 2 * count * (2 * pair + side) + shift
                listed[at : at + count, :] = value[:, side * C : (side + 1) * C]
    keys[...] = listed[...].astype(BF16)
    own = jnp.concatenate([field[:, C * c : C * (c + 1)] for c in range(cells)], 0)
    count = own.shape[0]
    embedded = mxu(own.astype(BF16), we[...])
    queries = mxu(embedded.astype(BF16), wqkv[:, 0:E]).astype(BF16)
    lane = lax.broadcasted_iota(jnp.int32, (1, E), 1)
    block = keys.shape[0] // blocks
    factor = [scale[h] * (math.log2(math.e) / math.sqrt(HEAD_DIM)) for h in range(HEADS)]

    def keyvals(start):
        spread = mxu(keys[pl.ds(start, block), :], we[...]).astype(BF16)
        both = mxu(spread, wqkv[:, E : 3 * E]).astype(BF16)
        return both[:, 0:E], both[:, E : 2 * E]

    def scores_of(h, k):
        mine = (lane >= h * HEAD_DIM) & (lane < (h + 1) * HEAD_DIM)
        q = jnp.where(mine, queries, jnp.zeros_like(queries))
        return lax.dot_general(q, k, (((1,), (1,)), ((), ())), preferred_element_type=F32)

    def masked(h, value):
        mine = (lane >= h * HEAD_DIM) & (lane < (h + 1) * HEAD_DIM)
        return jnp.where(mine, value, jnp.zeros_like(value))

    if blocks == 1:
        k, v = keyvals(0)
        attended = jnp.zeros((count, E), F32)
        for h in range(HEADS):
            s = scores_of(h, k)
            w = jnp.exp2((s - jnp.max(s, -1, keepdims=True)) * factor[h])
            total = jnp.sum(w, -1, keepdims=True)
            attended = attended + masked(h, mxu(w.astype(BF16), v) / total)
    else:

        def one_block(b, carry):
            peaks, totals, sums = carry
            k, v = keyvals(pl.multiple_of(b * block, 16))
            new_peaks, new_totals = [], []
            shrunk = jnp.zeros((count, E), F32)
            for h in range(HEADS):
                s = scores_of(h, k)
                peak = jnp.maximum(peaks[h], jnp.max(s, -1, keepdims=True))
                shrink = jnp.exp2((peaks[h] - peak) * factor[h])
                w = jnp.exp2((s - peak) * factor[h])
                new_peaks.append(peak)
                new_totals.append(totals[h] * shrink + jnp.sum(w, -1, keepdims=True))
                shrunk = shrunk + masked(h, sums * shrink + mxu(w.astype(BF16), v))
            return tuple(new_peaks), tuple(new_totals), shrunk

        start = (
            tuple(jnp.full((count, 1), -1e30, F32) for _ in range(HEADS)),
            tuple(jnp.zeros((count, 1), F32) for _ in range(HEADS)),
            jnp.zeros((count, E), F32),
        )
        _, totals, sums = lax.fori_loop(0, blocks, one_block, start)
        attended = jnp.zeros((count, E), F32)
        for h in range(HEADS):
            attended = attended + masked(h, sums / totals[h])
    hidden = embedded + mxu(attended.astype(BF16), wo[...])
    square = jnp.mean(hidden * hidden, -1, keepdims=True)
    normed = (hidden * lax.rsqrt(square + 1e-06) * gain[...]).astype(BF16)
    update = lax.dot_general(
        normed, wb[...], (((1,), (1,)), ((), ())), preferred_element_type=F32
    )
    back = [
        jnp.concatenate(
            [update[rows * c : rows * (c + 1), :], update[rows * (c + 1) : rows * (c + 2), :]], 1
        )
        for c in range(0, cells, 2)
    ]
    start = geo.band[4][0]
    for q, value in enumerate(back):
        at = slice(q * LANES, (q + 1) * LANES)
        out[:, at] = masked_rows(field[:, at] + value, start, geo.rows[4], lat, lats)


def synthesis_kernel(geo, lats, place, coarse, e2, o2, from_m2, from_p2, from_m3, from_p3, *refs):
    lat, parity = place[0], place[1] % 2
    part, d2, d3, d4, out, up3, up2, up1, ylow, yhigh, done, sems = refs
    bands = {2: d2, 3: d3, 4: d4}
    plan = exchange_plan(geo)

    def from_sides(level, b):
        n = geo.band[level][1]
        cols = [bands[level][b, :, LANES * p : LANES * (p + 1)] for p in range(geo.span[level][1])]
        for distance in (1, 2, 3):
            for which, count, row in plan[distance]:
                if which != level:
                    continue
                move = distance * geo.cells[level] // 2
                for p in range(count):
                    lanes = slice((b * count + p) * LANES, (b * count + p + 1) * LANES)
                    if distance == 1:
                        even = e2[row : row + n, lanes].astype(F32)
                        odd = o2[row : row + n, lanes].astype(F32)
                        low = jnp.where(parity == 0, odd, even)
                        high = jnp.where(parity == 0, even, odd)
                    else:
                        lows, highs = {2: (from_m2, from_p2), 3: (from_m3, from_p3)}[distance]
                        low = lows[row : row + n, lanes].astype(F32)
                        high = highs[row : row + n, lanes].astype(F32)
                    cols[p] = cols[p] + low
                    cols[p + move] = cols[p + move] + high
        return jnp.concatenate(cols, 1)

    uppers = {4: coarse, 3: up3, 2: up2, 1: up1}
    for level in (4, 3, 2):
        begin, pairs = geo.span[level]
        below = level - 1
        start, rows = geo.band[below]
        matrix = synthesis_matrix(start, rows, *geo.band[level])
        matrix = masked_rows(matrix, start, geo.rows[below], lat, lats)
        width = pairs * LANES
        for one, two, y in (
            (uppers[level][...], from_sides(level, 1), ylow),
            (from_sides(level, 0), from_sides(level, 2), yhigh),
        ):
            h, l = two_terms(jnp.concatenate([one, two], 0))
            y[0:rows, 0:width] = dot3(matrix, h, l)
        target = uppers[below]
        first, out_pairs = geo.span[below]

        step = best_step(rows)
        left = first_half(step)

        def joined(c, carry):
            row = pl.multiple_of(c * step, step)
            pair = synthesis(
                columns(ylow, row, step, pairs), columns(yhigh, row, step, pairs), begin, left
            )
            for q in range(out_pairs):
                put(target, row, q, pair(first + 2 * q))
            return carry

        lax.fori_loop(0, rows // step, joined, 0)

    n = geo.band[1][1]
    half = geo.rows[0] // 2
    for block in range(2):
        w = 0 if block == 0 else n - LANES
        matrix = synthesis_matrix(half * block, half, geo.band[1][0] + w, LANES)
        h, l = two_terms(up1[w : w + LANES, :])
        ylow[half * block : half * (block + 1), :] = dot3(matrix[:, 0:LANES], h, l)
    begin, pairs = geo.span[1]
    most = 112

    def last(row, count):
        left = first_half(count)
        pair = synthesis_of_lows(columns(ylow, row, count), begin, left)
        for q in range(geo.cells[0] // 2):
            more = part[pl.ds(row, count), pl.ds(LANES * q, LANES)]
            put(done, row, q, (pair(2 * q) + more).astype(BF16))

    def store(i, count):
        part = pl.ds(pl.multiple_of(i * most, 16), count)
        return pltpu.make_async_copy(done.at[part, :], out.at[part, :], sems.at[i])

    whole, rest = geo.rows[0] // most, geo.rows[0] % most

    def chunk(i, carry):
        last(pl.multiple_of(i * most, 16), most)
        store(i, most).start()
        return carry

    lax.fori_loop(0, whole, chunk, 0)
    if rest:
        last(whole * most, rest)
        store(whole, rest).start()
    for i in range(whole):
        store(i, most).wait()
    if rest:
        store(whole, rest).wait()


def call(kernel, out_shape, scratch, *args, cost=20_000_000, grant=24, raw=(), raw_out=(), stay=()):
    vmem = pl.BlockSpec(memory_space=pltpu.VMEM)
    smem = pl.BlockSpec(memory_space=pltpu.SMEM)
    anywhere = pl.BlockSpec(memory_space=pl.ANY)
    specs = [smem if a.ndim == 1 and a.size < 16 else vmem for a in args]
    for at in raw:
        specs[at] = anywhere
    held = lambda a: pltpu.with_memory_space_constraint(a, pltpu.HBM)
    args = [held(a) if i in stay else a for i, a in enumerate(args)]
    outs = [anywhere if i in raw_out else vmem for i in range(len(out_shape))]
    return pl.pallas_call(
        kernel,
        out_shape=tuple(out_shape),
        in_specs=specs,
        out_specs=tuple(outs),
        scratch_shapes=scratch,
        compiler_params=pltpu.CompilerParams(vmem_limit_bytes=grant << 20),
        cost_estimate=pl.CostEstimate(flops=cost, bytes_accessed=1 << 20, transcendentals=0),
    )(*args)


def shape(dims, dtype=F32):
    return jax.ShapeDtypeStruct(dims, dtype)


def per_device(mesh_shape, state_field, skip_gain, embed_weight, qkv_weight, head_scale, out_weight, norm_gain, back_weight):
    return program(
        mesh_shape, state_field, skip_gain, embed_weight, qkv_weight, head_scale, out_weight, norm_gain, back_weight
    )


def program(mesh_shape, state_field, skip_gain, embed_weight, qkv_weight, head_scale, out_weight, norm_gain, back_weight):
    lons, lats = mesh_shape["lon"], mesh_shape["lat"]
    rows, width = state_field.shape
    geo = Geometry(rows, width // C)
    lat, lon = lax.axis_index("lat"), lax.axis_index("lon")
    place = jnp.stack([lat, lon]).astype(jnp.int32)

    even_pairs = [(i, i ^ 1) for i in range(lons)]
    odd_pairs = [(i, (i + 1 if i % 2 else i - 1) % lons) for i in range(lons)]
    swap = [(i, lats - 1 - i) for i in range(lats)]

    def shifted(value, by):
        return lax.ppermute(value, "lon", [(i, (i + by) % lons) for i in range(lons)])

    edge = lax.dynamic_slice(
        state_field, (jnp.where(lat == 0, rows - HALO, 0), 0), (HALO, width)
    )
    edge = lax.ppermute(edge, "lat", swap)

    wide = SIDE * C
    extended = NEAR + rows + NEAR
    side_e, side_o = call(
        sides_kernel,
        [shape((rows, wide), BF16)] * 2,
        [pltpu.SemaphoreType.DMA((2,))],
        place,
        state_field,
        raw=(1,),
        stay=(1,),
        cost=1_000_000,
    )
    side_e = lax.ppermute(side_e, "lon", even_pairs)
    side_o = lax.ppermute(side_o, "lon", odd_pairs)

    w = [None] + [geo.span[level][1] * LANES for level in (1, 2, 3, 4)]
    low = lambda level, lanes: pltpu.VMEM((geo.low[level][1], w[lanes]), F32)
    bands = [(3, geo.band[level][1], w[level]) for level in (1, 2, 3, 4)]
    ll4, d2, d3, d4, deep_e, deep_o, p2, m2, p3, m3 = call(
        functools.partial(analysis_kernel, geo, lats),
        [shape((geo.low[4][1], w[4]))]
        + [shape(dims) for dims in bands[1:]]
        + [shape(plan_shape(geo, d), BF16) for d in (1, 1, 2, 2, 3, 3)],
        [
            pltpu.VMEM((geo.extended, width), BF16),
            pltpu.VMEM((geo.low[1][1], width), F32),
            low(1, 1),
            pltpu.VMEM((geo.low[1][1], w[1]), BF16),
            pltpu.VMEM((geo.low[1][1], w[1]), BF16),
            low(2, 1),
            low(2, 2),
            low(3, 2),
            low(3, 3),
            low(4, 3),
        ]
        + [pltpu.VMEM((geo.band[level][1], w[level - 1]), F32) for level in (2, 3, 4)]
        + [pltpu.SemaphoreType.DMA((geo.low[1][1] // 112,))],
        place,
        edge,
        skip_gain,
        state_field,
        raw=(3,),
        stay=(3,),
    )
    (corner,) = call(
        corners_kernel, [shape((NEAR, 2 * wide), BF16)], [], place, side_e, side_o, cost=100_000
    )
    corner = lax.ppermute(corner, "lat", swap)
    count = geo.band[1][1]
    inner, lo_rim, hi_rim = call(
        functools.partial(inner_kernel, geo, lats),
        [shape(bands[0]), shape((count, 2 * wide)), shape((count, 2 * wide))],
        [
            pltpu.VMEM((extended, width), BF16),
            pltpu.VMEM((count, width), F32),
            pltpu.VMEM((count, width), F32),
            pltpu.SemaphoreType.DMA,
        ],
        place,
        edge,
        skip_gain,
        state_field,
        raw=(3,),
        stay=(3,),
    )
    ends = 2 * edge_pairs() * LANES
    (part,) = call(
        functools.partial(first_level_kernel, geo, lats),
        [shape((rows, width))],
        [
            pltpu.VMEM((extended, 2 * wide), BF16),
            pltpu.VMEM((count, 2 * wide), F32),
            pltpu.VMEM((count, 2 * wide), F32),
            pltpu.VMEM((3, count, ends), F32),
            pltpu.VMEM((rows, w[1]), F32),
            pltpu.VMEM((rows, w[1]), F32),
            pltpu.VMEM((2 * LANES, w[1]), BF16),
            pltpu.VMEM((2 * LANES, w[1]), BF16),
        ],
        place,
        side_e,
        side_o,
        corner,
        skip_gain,
        inner,
        lo_rim,
        hi_rim,
        grant=30,
    )

    merged, size = ll4, 1
    total = geo.cells[4] * lons * C
    while size < lons:
        other = lax.ppermute(merged, "lon", [(i, i ^ size) for i in range(lons)])
        more = geo.cells[4] * C * size
        dims = (merged.shape[0], merged.shape[1] + more)
        if 2 * size < lons:
            (merged,) = call(
                functools.partial(merge_kernel, size, more), [shape(dims)], [], place, merged, other, cost=100_000
            )
        else:
            ring, tokens = call(
                functools.partial(last_merge_kernel, geo, size, more),
                [shape((dims[0], total)), shape((geo.rows[4], total), BF16)],
                [pltpu.VMEM(dims, F32)],
                place,
                merged,
                other,
                cost=100_000,
            )
        size = 2 * size
    others = lax.ppermute(tokens, "lat", swap)

    deep_e = lax.ppermute(deep_e, "lon", even_pairs)
    deep_o = lax.ppermute(deep_o, "lon", odd_pairs)
    from_m2, from_p2 = shifted(p2, 2), shifted(m2, -2)
    from_m3, from_p3 = shifted(p3, 3), shifted(m3, -3)

    key_count = 2 * geo.rows[4] * geo.cells[4] * lons
    blocks = key_count // 928 if key_count % 928 == 0 else 1
    (coarse,) = call(
        functools.partial(attention_kernel, geo, lats, blocks),
        [shape((geo.low[4][1], w[4]))],
        [
            pltpu.VMEM((geo.low[4][1], total + 6 * C), F32),
            pltpu.VMEM((key_count, C), F32),
            pltpu.VMEM((key_count, C), BF16),
        ],
        place,
        ring,
        tokens,
        others,
        embed_weight,
        qkv_weight,
        head_scale,
        out_weight,
        norm_gain[None],
        back_weight.T,
        cost=200_000_000,
        grant=40,
    )

    (out,) = call(
        functools.partial(synthesis_kernel, geo, lats),
        [shape((rows, width), BF16)],
        [pltpu.VMEM((geo.band[level][1], w[level]), F32) for level in (3, 2, 1)]
        + [
            pltpu.VMEM((rows, w[1]), F32),
            pltpu.VMEM((geo.band[1][1], w[2]), F32),
            pltpu.VMEM((rows, width), BF16),
            pltpu.SemaphoreType.DMA((rows // 112 + 1,)),
        ],
        place,
        coarse,
        deep_e,
        deep_o,
        from_m2,
        from_p2,
        from_m3,
        from_p3,
        part,
        d2,
        d3,
        d4,
        raw_out=(0,),
        grant=30,
    )
    return out


def solution(mesh):
    in_specs = (P("lat", ("member", "lon")), P(), P(), P(), P(), P(), P(), P())
    out_specs = P("lat", ("member", "lon"))
    return jax.shard_map(
        functools.partial(per_device, dict(mesh.shape)),
        mesh=mesh,
        in_specs=in_specs,
        out_specs=out_specs,
        check_vma=False,
    )
```

```python
import functools
import math

import jax
import jax.numpy as jnp
import numpy as np
from jax import lax
from jax.experimental import pallas as pl
from jax.experimental.pallas import tpu as pltpu
from jax.sharding import PartitionSpec as P


C = 64
HEADS = 8
HEAD_DIM = 32
E = 256
LANES = 128
HALO = 96
LEAD = 16

LOW = np.array(
    [
        -0.010597401784997278,
        0.032883011666982945,
        0.030841381835986965,
        -0.18703481171888114,
        -0.02798376941698385,
        0.6308807679295904,
        0.7148465705525415,
        0.23037781330885523,
    ]
)
HIGH = np.array([(-1.0) ** j * LOW[7 - j] for j in range(8)])


F32 = jnp.float32
BF16 = jnp.bfloat16


def two_terms(value):
    top = value.astype(BF16)
    return top, (value - top.astype(F32)).astype(BF16)


def masked_rows(matrix, start, count, lat, lats):
    row = lax.broadcasted_iota(jnp.int32, matrix.shape, 0) + (start + lat * count)
    return jnp.where((row >= 0) & (row < count * lats), matrix, 0.0)


def banded(shape, low, high, row_factor, column_factor, offset):
    row = lax.broadcasted_iota(jnp.int32, shape, 0)
    column = lax.broadcasted_iota(jnp.int32, shape, 1)
    tap = row_factor * row + column_factor * column + offset
    if high is not None:
        second = column >= shape[1] // 2
        tap = jnp.where(second, tap - column_factor * (shape[1] // 2), tap)
    matrix = jnp.zeros(shape, F32)
    for t in range(8):
        value = F32(low[t]) if high is None else jnp.where(second, F32(high[t]), F32(low[t]))
        matrix = jnp.where(tap == t, value, matrix)
    return matrix


def analysis_matrix(taps, out_start, out_rows, in_start, in_rows):
    return banded((out_rows, in_rows), taps, None, -2, 1, in_start + 3 - 2 * out_start)


def synthesis_matrix(out_start, out_rows, in_start, in_rows):
    shape = (out_rows, 2 * in_rows)
    return banded(shape, LOW, HIGH, 1, -2, out_start - 2 * in_start + 3)


def mxu(a, b):
    return jnp.dot(a, b, preferred_element_type=F32)


def dot3(matrix, vh, vl):
    mh, ml = two_terms(matrix)
    return mxu(mh, vh) + mxu(mh, vl) + mxu(ml, vh)


def first_half(rows):
    return lax.broadcasted_iota(jnp.int32, (rows, LANES), 1) < C


def half_turn(value):
    return None if value is None else pltpu.roll(value, C, 1)


def pick(left, a, b):
    if a is None and b is None:
        return None
    return jnp.where(left, 0.0 if a is None else a, 0.0 if b is None else b)


def plus(a, b, factor):
    if b is None:
        return a
    if a is None:
        return b * factor
    return a + b * factor


class Memo:
    def __init__(self, make):
        self.make, self.known = make, {}

    def __call__(self, n):
        if n not in self.known:
            self.known[n] = self.make(n)
        return self.known[n]


def analysis(cols, start, left):
    turned = Memo(lambda i: half_turn(cols[i]) if 0 <= i < len(cols) else None)
    plain = lambda i: cols[i] if 0 <= i < len(cols) else None
    if start % 2 == 0:
        at = lambda n: n - 1 - start // 2
        u = Memo(lambda n: pick(left, turned(at(n) - 1), plain(at(n))))
        w = Memo(lambda n: pick(left, plain(at(n)), turned(at(n) + 1)))
    else:
        at = lambda n: n - (start + 3) // 2
        u = Memo(lambda n: pick(left, plain(at(n)), turned(at(n) + 1)))
        w = Memo(lambda n: pick(left, turned(at(n)), plain(at(n) + 1)))

    def band(taps):
        def make(k):
            total = None
            for step in range(4):
                total = plus(total, u(k + step), float(taps[2 * step]))
                total = plus(total, w(k + step), float(taps[2 * step + 1]))
            return total

        return make

    return band(LOW), band(HIGH)


def synthesis(lows, highs, start, left):
    parity = start % 2

    def cells(cols):
        col = lambda k: cols[(k - start) // 2] if 0 <= k - start < 2 * len(cols) else None
        turned = Memo(lambda k: half_turn(col(k)))

        def at(k):
            if k % 2 == parity:
                return col(k)
            return pick(left, turned(k - 1), turned(k + 1))

        return Memo(at)

    sources = ((cells(lows), LOW), (cells(highs), HIGH))

    def output(first):
        def make(n):
            total = None
            for step in range(4):
                for source, taps in sources:
                    total = plus(total, source(n - step), float(taps[2 * step + first]))
            return total

        return Memo(make)

    u, w = output(0), output(1)
    u_turned, w_turned = Memo(lambda n: half_turn(u(n))), Memo(lambda n: half_turn(w(n)))

    def pair(m):
        if m % 2:
            n = (m + 3) // 2
            if n % 2 == parity:
                return pick(left, u(n), w_turned(n))
            return pick(left, u_turned(n - 1), w(n - 1))
        n = m // 2 + 1
        if n % 2 == parity:
            return pick(left, w(n), u(n))
        return pick(left, w_turned(n - 1), u_turned(n + 1))

    return pair


def synthesis_of_lows(lows, start, left):
    def dup(k):
        i = (k - start) // 2
        if not 0 <= i < len(lows):
            return None
        turned = rolled(i)
        return jnp.where(left, lows[i], turned) if (k - start) % 2 == 0 else jnp.where(left, turned, lows[i])

    rolled = Memo(lambda i: half_turn(lows[i]))
    both = Memo(dup)

    def tap(t):
        return F32(LOW[t]) if 0 <= t < 8 else F32(0.0)

    weights = [jnp.where(left[0:8], tap(7 - 2 * i), tap(8 - 2 * i)) for i in range(5)]
    weights = [jnp.concatenate([v] * (left.shape[0] // 8), 0) for v in weights]

    def pair(m):
        total = None
        for i in range(5):
            cell = both(m // 2 - 2 + i)
            if cell is not None:
                total = cell * weights[i] if total is None else total + cell * weights[i]
        return total

    return pair


def columns(ref, row, rows, count=None):
    count = ref.shape[-1] // LANES if count is None else count
    return [ref[pl.ds(row, rows), pl.ds(LANES * p, LANES)] for p in range(count)]


def put(ref, row, p, value, lead=()):
    ref[lead + (pl.ds(row, value.shape[0]), pl.ds(LANES * p, LANES))] = value


class Geometry:
    def __init__(self, rows, cells):
        self.rows = [rows >> level for level in range(5)]
        self.cells = [cells >> level for level in range(5)]
        up = lambda value, step: -(-value // step) * step
        self.band = [
            None,
            (-4, up(self.rows[1] + 4, 120)),
            (-8, up(self.rows[2] + 11, 16)),
            (-3, up(self.rows[3] + 6, 8)),
            (-3, up(self.rows[4] + 6, 8)),
        ]
        self.low = [
            None,
            (-52, up(self.rows[1] + 97, 112)),
            (-24, up(self.rows[2] + 45, 88)),
            (-11, up(self.rows[3] + 20, 8)),
            (-3, up(self.rows[4] + 6, 8)),
        ]
        self.span = [None, (-2, self.cells[1] // 2 + 2)]
        for level in (2, 3, 4):
            self.span.append((-3, self.cells[level] // 2 + 3))
        self.extended = max(
            LEAD + 2 * HALO + rows, 2 * (self.low[1][1] - 112) + 256
        )


STEP = 240
SIDE = 8
NEAR = 16


def best_step(rows, most=None):
    return max(s for s in range(8, (most or STEP) + 1, 8) if rows % s == 0)


def low_rows(geo, level, source, source_start, target):
    first, pairs = geo.span[level]
    rows = geo.low[level][1]
    step = best_step(rows, 168)
    left = first_half(step)

    def body(c, carry):
        row = pl.multiple_of(c * step, step)
        low, _ = analysis(columns(source, row, step), source_start, left)
        for q in range(pairs):
            put(target, row, q, low(first + 2 * q))
        return carry

    lax.fori_loop(0, rows // step, body, 0)


def band_rows(geo, level, lo, skip, hi, source_start, gain, bands):
    first, pairs = geo.span[level]
    rows = geo.band[level][1]
    step = best_step(rows)
    left = first_half(step)

    def body(c, carry):
        row = pl.multiple_of(c * step, step)
        g = []
        for b in range(3):
            one = gain[level - 1, b : b + 1, :]
            g.append(jnp.broadcast_to(jnp.concatenate([one, one], 1), (step, LANES)))
        _, high = analysis(columns(lo, row + skip, step), source_start, left)
        for q in range(pairs):
            put(bands, row, q, high(first + 2 * q) * g[0], (0,))
        low, high = analysis(columns(hi, row, step), source_start, left)
        for q in range(pairs):
            put(bands, row, q, low(first + 2 * q) * g[1], (1,))
            put(bands, row, q, high(first + 2 * q) * g[2], (2,))
        return carry

    lax.fori_loop(0, rows // step, body, 0)


def analysis_kernel(geo, lats, place, edge, gain, x, *refs):
    lat, parity = place[0], place[1] % 2
    ll4, d2, d3, d4, send_e, send_o, p2, m2, p3, m3 = refs[:10]
    ext, la, g1, gh, gl, lo2, g2, lo3, g3, lo4, hi2, hi3, hi4, sems = refs[10:]
    rows = geo.rows[0]
    start, count = geo.low[1]
    width = x.shape[1]
    begin = LEAD + HALO
    blocks = count // 112
    cuts = [0] + [min(rows, 224 * b + 256 - begin) for b in range(blocks - 1)] + [rows]
    copies = []
    for i in range(blocks):
        part = pl.ds(cuts[i], cuts[i + 1] - cuts[i])
        to = pl.ds(begin + cuts[i], cuts[i + 1] - cuts[i])
        copies.append(pltpu.make_async_copy(x.at[part, :], ext.at[to, :], sems.at[i]))
        copies[-1].start()
    top = slice(LEAD, begin)
    bottom = slice(begin + rows, begin + rows + HALO)
    ext[0:LEAD, :] = jnp.zeros((LEAD, width), BF16)
    tail = geo.extended - (LEAD + 2 * HALO + rows)
    if tail:
        ext[geo.extended - tail :, :] = jnp.zeros((tail, width), BF16)

    @pl.when(lat == 0)
    def _():
        ext[top, :] = jnp.zeros((HALO, width), BF16)
        ext[bottom, :] = edge[...]

    @pl.when(lat != 0)
    def _():
        ext[top, :] = edge[...]
        ext[bottom, :] = jnp.zeros((HALO, width), BF16)

    base = analysis_matrix(LOW, start, 112, 0 - LEAD - HALO, 256)
    for b in range(blocks):
        copies[b].wait()
        mh, ml = two_terms(masked_rows(base, start + 112 * b, geo.rows[1], lat, lats))
        data = ext[224 * b : 224 * b + 256, :]
        la[112 * b : 112 * b + 112, :] = mxu(mh, data) + mxu(ml, data)
    low_rows(geo, 1, la, 0, g1)
    gh[...], gl[...] = two_terms(g1[...])
    out_start, out_rows = geo.low[2]
    for b in range(out_rows // 88):
        at = min(176 * b, count - 192)
        window = slice(at, at + 192)
        matrix = analysis_matrix(LOW, out_start + 88 * b, 88, start + at, 192)
        matrix = masked_rows(matrix, out_start + 88 * b, geo.rows[2], lat, lats)
        lo2[88 * b : 88 * b + 88, :] = dot3(matrix, gh[window, :], gl[window, :])
    low_rows(geo, 2, lo2, geo.span[1][0], g2)
    for level, source, lo, target in ((3, g2, lo3, g3), (4, g3, lo4, ll4)):
        vh, vl = two_terms(source[...])
        matrix = analysis_matrix(LOW, *geo.low[level], *geo.low[level - 1])
        matrix = masked_rows(matrix, geo.low[level][0], geo.rows[level], lat, lats)
        lo[...] = dot3(matrix, vh, vl)
        low_rows(geo, level, lo, geo.span[level - 1][0], target)
    d = {2: d2, 3: d3, 4: d4}
    for level, lo, hi in ((2, lo2, hi2), (3, lo3, hi3), (4, lo4, hi4)):
        deep_bands(geo, lats, lat, level, {2: (gh, gl), 3: g2, 4: g3}[level], lo, hi, gain, d[level])

    def fill(distance, to_left, to_right):
        for level, count, row in exchange_plan(geo)[distance]:
            n = geo.band[level][1]
            move = distance * geo.cells[level] // 2
            for b in range(3):
                lanes = slice(b * count * LANES, (b + 1) * count * LANES)
                to_left[row : row + n, lanes] = d[level][b, :, 0 : count * LANES].astype(BF16)
                to_right[row : row + n, lanes] = d[level][
                    b, :, move * LANES : (move + count) * LANES
                ].astype(BF16)

    @pl.when(parity == 0)
    def _():
        fill(1, send_o, send_e)

    @pl.when(parity != 0)
    def _():
        fill(1, send_e, send_o)

    fill(2, m2, p2)
    fill(3, m3, p3)


def deep_bands(geo, lats, lat, level, source, lo, hi, gain, bands):
    start, count = geo.band[level]
    in_start = geo.low[level - 1][0]
    parts = 2 if level == 2 else 1
    half = count // parts
    for b in range(parts):
        if parts == 1:
            at, size = 0, source.shape[0]
            vh, vl = two_terms(source[...])
        else:
            at = (2 * (start + half * b) - 3 - in_start) // 16 * 16
            size = 2 * half + 16
            vh, vl = source[0][at : at + size, :], source[1][at : at + size, :]
        matrix = analysis_matrix(HIGH, start + half * b, half, in_start + at, size)
        matrix = masked_rows(matrix, start + half * b, geo.rows[level], lat, lats)
        hi[half * b : half * (b + 1), :] = dot3(matrix, vh, vl)
    skip = start - geo.low[level][0]
    band_rows(geo, level, lo, skip, hi, geo.span[level - 1][0], gain, bands)


def side_shape(rows):
    tall = side_split(rows)
    return (rows + tall // 3, 3 * LANES)


def side_split(rows):
    return -(-(-(-rows // 2)) // 48) * 48


def sides_kernel(place, x, side_e, side_o, edge, ends, sems):
    lat, parity = place[0], place[1] % 2
    rows, width = x.shape
    lanes = 3 * LANES
    tall = side_split(rows)
    third = tall // 3
    at = pl.multiple_of(jnp.where(lat == 0, rows - HALO, 0), NEAR)
    strip = pltpu.make_async_copy(x.at[pl.ds(at, HALO), :], edge, sems.at[4])
    strip.start()

    def both(low, high):
        body = pl.ds(0, rows)
        copies = [
            pltpu.make_async_copy(x.at[:, pl.ds(lanes, LANES)], ends.at[0], sems.at[0]),
            pltpu.make_async_copy(x.at[:, pl.ds(width - lanes - LANES, LANES)], ends.at[1], sems.at[1]),
            pltpu.make_async_copy(x.at[:, pl.ds(0, lanes)], low.at[body, :], sems.at[2]),
            pltpu.make_async_copy(x.at[:, pl.ds(width - lanes, lanes)], high.at[body, :], sems.at[3]),
        ]
        for copy in copies:
            copy.start()
        for side, out in ((0, low), (1, high)):
            copies[side].wait()
            one = ends[side, 0:tall, :].astype(F32)
            two = ends[side, tall:rows, :].astype(F32)
            if side:
                one = half_turn(one)
            else:
                two = half_turn(two)
            two = jnp.concatenate([two, jnp.zeros((2 * tall - rows, LANES), F32)], 0)
            mixed = jnp.where(lax.broadcasted_iota(jnp.int32, (tall, LANES), 1) < C, one, two)
            for b in range(3):
                block = mixed[third * b : third * (b + 1), :].astype(BF16)
                out[rows : rows + third, b * LANES : (b + 1) * LANES] = block
        copies[2].wait()
        copies[3].wait()

    @pl.when(parity == 0)
    def _():
        both(side_o, side_e)

    @pl.when(parity != 0)
    def _():
        both(side_e, side_o)

    strip.wait()


def unpack_side(side, rows, out, row, at_left):
    lanes = 3 * LANES
    tall = side_split(rows)
    third = tall // 3
    half = jnp.concatenate(
        [side[rows : rows + third, b * LANES : (b + 1) * LANES].astype(F32) for b in range(3)], 0
    )
    is_left = lax.broadcasted_iota(jnp.int32, (tall, LANES), 1) < C
    turned = half_turn(half)
    if at_left:
        one, two = jnp.where(is_left, 0.0, turned), jnp.where(is_left, 0.0, half)
        pairs, end = slice(LANES, LANES + lanes), slice(0, LANES)
    else:
        one, two = jnp.where(is_left, half, 0.0), jnp.where(is_left, turned, 0.0)
        pairs, end = slice(0, lanes), slice(lanes, lanes + LANES)
    base = 0 if at_left else SIDE * C
    out[row : row + rows, base + pairs.start : base + pairs.stop] = side[0:rows, :]
    out[row : row + tall, base + end.start : base + end.stop] = one.astype(BF16)
    out[row + tall : row + rows, base + end.start : base + end.stop] = two[0 : rows - tall].astype(BF16)


def corners_kernel(geo, place, side_e, side_o, out, ext):
    lat, parity = place[0], place[1] % 2
    rows = geo.rows[0]

    @pl.when(parity == 0)
    def _():
        unpack_side(side_o, rows, ext, 0, True)
        unpack_side(side_e, rows, ext, 0, False)

    @pl.when(parity != 0)
    def _():
        unpack_side(side_e, rows, ext, 0, True)
        unpack_side(side_o, rows, ext, 0, False)

    at = jnp.where(lat == 0, rows - NEAR, 0)
    out[...] = ext[pl.ds(pl.multiple_of(at, NEAR), NEAR), :]


def merge_kernel(size, more, place, mine, other, out):
    width = mine.shape[1]

    def add(lower, upper):
        out[:, 0:more] = lower[:, 0:more]
        out[:, more:width] = lower[:, more:] + upper[:, 0 : width - more]
        out[:, width:] = upper[:, width - more :]

    lower_half = (place[1] // size) % 2 == 0

    @pl.when(lower_half)
    def _():
        add(mine, other)

    @pl.when(jnp.logical_not(lower_half))
    def _():
        add(other, mine)


def last_merge_kernel(geo, size, more, place, mine, other, ring, tokens, merged):
    merge_kernel(size, more, place, mine, other, merged)
    around = ring.shape[1]
    fold = merged.shape[1] - around
    ring[:, 0:fold] = merged[:, 0:fold] + merged[:, around:]
    ring[:, fold:] = merged[:, fold:around]
    skip = -geo.low[4][0]
    tokens[...] = ring[skip : skip + geo.rows[4], :].astype(BF16)


def latitude_bands(geo, lats, lat, ext, la, ha):
    start, count = geo.band[1]
    low = analysis_matrix(LOW, start, 120, -NEAR, 256)
    high = analysis_matrix(HIGH, start, 120, -NEAR, 256)
    for b in range(count // 120):
        data = ext[240 * b : 240 * b + 256, :]
        for matrix, out in ((low, la), (high, ha)):
            mh, ml = two_terms(masked_rows(matrix, start + 120 * b, geo.rows[1], lat, lats))
            out[120 * b : 120 * b + 120, :] = mxu(mh, data) + mxu(ml, data)


def first_bands(row, los, his, start, groups, gain, bands):
    step = los[0].shape[0]
    left = first_half(step)
    g = []
    for b in range(3):
        one = gain[0, b : b + 1, :]
        g.append(jnp.broadcast_to(jnp.concatenate([one, one], 1), (step, LANES)))
    _, high = analysis(los, start, left)
    for q, k in groups:
        put(bands, row, q, high(k) * g[0], (0,))
    low, high = analysis(his, start, left)
    for q, k in groups:
        put(bands, row, q, low(k) * g[1], (1,))
        put(bands, row, q, high(k) * g[2], (2,))


def edge_pairs():
    return 2


def inner_kernel(geo, lats, place, edge, gain, x, d1, lo_rim, hi_rim, ext, la, ha, sem):
    lat = place[0]
    rows, width = x.shape
    copy = pltpu.make_async_copy(x, ext.at[pl.ds(NEAR, rows), :], sem)
    copy.start()

    @pl.when(lat == 0)
    def _():
        ext[0:NEAR, :] = jnp.zeros((NEAR, width), BF16)
        ext[NEAR + rows :, :] = edge[0:NEAR, :]

    @pl.when(lat != 0)
    def _():
        ext[0:NEAR, :] = edge[HALO - NEAR :, :]
        ext[NEAR + rows :, :] = jnp.zeros((NEAR, width), BF16)

    copy.wait()
    latitude_bands(geo, lats, lat, ext, la, ha)
    rim = SIDE * C
    for out, source in ((lo_rim, la), (hi_rim, ha)):
        out[:, 0:rim] = source[:, 0:rim]
        out[:, rim:] = source[:, width - rim :]
    first, pairs = geo.span[1]
    ends = edge_pairs()
    groups = [(q, first + 2 * q) for q in range(ends, pairs - ends)]
    step = best_step(geo.band[1][1])

    def body(c, carry):
        row = pl.multiple_of(c * step, step)
        first_bands(row, columns(la, row, step), columns(ha, row, step), 0, groups, gain, d1)
        return carry

    lax.fori_loop(0, geo.band[1][1] // step, body, 0)


def first_level_kernel(geo, lats, place, beside, corner, gain, inner, lo_rim, hi_rim, part, ext, lo_side, hi_side, d1, la, ha, xh, xl):
    lat = place[0]
    rows, _ = part.shape
    lanes = SIDE * C
    top, bottom = slice(0, NEAR), slice(NEAR + rows, 2 * NEAR + rows)

    def rims(near, far):
        ext[far, :] = jnp.zeros((NEAR, 2 * lanes), BF16)
        ext[near, :] = corner[...]

    @pl.when(lat == 0)
    def _():
        rims(bottom, top)

    @pl.when(lat != 0)
    def _():
        rims(top, bottom)

    ext[NEAR : NEAR + rows, :] = beside[...]
    start, count = geo.band[1]
    latitude_bands(geo, lats, lat, ext, lo_side, hi_side)
    first, pairs = geo.span[1]
    ends = edge_pairs()
    step = best_step(count)
    near = SIDE // 2

    def body(c, carry):
        row = pl.multiple_of(c * step, step)
        sources = [columns(ref, row, step) for ref in (lo_side, hi_side, lo_rim, hi_rim)]
        lo_s, hi_s, lo_r, hi_r = sources
        groups = [(q, first + 2 * q) for q in range(ends)]
        first_bands(
            row, lo_s[:near] + lo_r[:near], hi_s[:near] + hi_r[:near], -SIDE, groups, gain, d1
        )
        groups = [(ends + q, first + 2 * (pairs - ends + q)) for q in range(ends)]
        begin = geo.cells[0] - SIDE
        first_bands(
            row, lo_r[near:] + lo_s[near:], hi_r[near:] + hi_s[near:], begin, groups, gain, d1
        )
        return carry

    lax.fori_loop(0, count // step, body, 0)
    rim, whole = ends * LANES, pairs * LANES

    def terms(b, window, to):
        for lanes_to, source, lanes_from in (
            (slice(0, rim), d1, slice(0, rim)),
            (slice(rim, whole - rim), inner, slice(rim, whole - rim)),
            (slice(whole - rim, whole), d1, slice(rim, 2 * rim)),
        ):
            h, l = two_terms(source[b, window, lanes_from])
            xh[to, lanes_to], xl[to, lanes_to] = h, l

    half = rows // 2
    ylow, yhigh = la, ha
    used = slice(0, whole)
    upper, lower = slice(0, LANES), slice(LANES, 2 * LANES)
    for block in range(2):
        w = 0 if block == 0 else count - LANES
        window = slice(w, w + LANES)
        target = slice(half * block, half * (block + 1))
        matrix = synthesis_matrix(half * block, half, start + w, LANES)
        sh, sl = two_terms(matrix)
        terms(0, window, upper)
        terms(2, window, lower)
        yhigh[target, used] = mxu(sh, xh[...]) + mxu(sh, xl[...]) + mxu(sl, xh[...])
        terms(1, window, lower)
        sh, sl = sh[:, LANES:], sl[:, LANES:]
        vh, vl = xh[lower, :], xl[lower, :]
        ylow[target, used] = mxu(sh, vh) + mxu(sh, vl) + mxu(sl, vh)

    begin, pairs = geo.span[1]
    most = 232

    def chunk(i, carry):
        row = pl.multiple_of(i * most, 8)
        pair = synthesis(
            columns(ylow, row, most, pairs), columns(yhigh, row, most, pairs), begin, first_half(most)
        )
        for q in range(geo.cells[0] // 2):
            put(part, row, q, pair(2 * q))
        return carry

    lax.fori_loop(0, rows // most, chunk, 0)


def exchange_plan(geo):
    plan = {}
    for distance in (1, 2, 3):
        entries, row = [], 0
        for level in (2, 3, 4):
            count = geo.span[level][1] - distance * geo.cells[level] // 2
            if count > 0:
                entries.append((level, count, row))
                row += -(-geo.band[level][1] // 16) * 16
        plan[distance] = entries
    return plan


def plan_shape(geo, distance):
    entries = exchange_plan(geo)[distance]
    level, _, row = entries[-1]
    rows = row + geo.band[level][1]
    return (rows, max(count for _, count, _ in entries) * 3 * LANES)


def attention_kernel(geo, lats, blocks, place, ring, own, others, we, wqkv, scale, wo, gain, wb, out, around, listed, keys):
    lat, lon = place[0], place[1]
    rows, width = out.shape
    cells = width // C
    total = ring.shape[1]
    around[:, 0:total] = ring[...]
    around[:, total:] = ring[:, 0 : around.shape[1] - total]
    field = around[:, pl.ds(pl.multiple_of(lon * (geo.cells[4] * C), LANES), width)]
    count = geo.rows[4]
    for source, shift in ((own, 0), (others, count)):
        for pair in range(total // LANES):
            value = source[:, pair * LANES : (pair + 1) * LANES].astype(F32)
            for side in range(2):
                at = 2 * count * (2 * pair + side) + shift
                listed[at : at + count, :] = value[:, side * C : (side + 1) * C]
    keys[...] = listed[...].astype(BF16)
    own = jnp.concatenate([field[:, C * c : C * (c + 1)] for c in range(cells)], 0)
    count = own.shape[0]
    embedded = mxu(own.astype(BF16), we[...])
    queries = mxu(embedded.astype(BF16), wqkv[:, 0:E]).astype(BF16)
    lane = lax.broadcasted_iota(jnp.int32, (1, E), 1)
    block = keys.shape[0] // blocks
    factor = [scale[h] * (math.log2(math.e) / math.sqrt(HEAD_DIM)) for h in range(HEADS)]

    def keyvals(start):
        spread = mxu(keys[pl.ds(start, block), :], we[...]).astype(BF16)
        both = mxu(spread, wqkv[:, E : 3 * E]).astype(BF16)
        return both[:, 0:E], both[:, E : 2 * E]

    def scores_of(h, k):
        mine = (lane >= h * HEAD_DIM) & (lane < (h + 1) * HEAD_DIM)
        q = jnp.where(mine, queries, jnp.zeros_like(queries))
        return lax.dot_general(q, k, (((1,), (1,)), ((), ())), preferred_element_type=F32)

    def masked(h, value):
        mine = (lane >= h * HEAD_DIM) & (lane < (h + 1) * HEAD_DIM)
        return jnp.where(mine, value, jnp.zeros_like(value))

    if blocks == 1:
        k, v = keyvals(0)
        attended = jnp.zeros((count, E), F32)
        for h in range(HEADS):
            s = scores_of(h, k)
            w = jnp.exp2((s - jnp.max(s, -1, keepdims=True)) * factor[h])
            total = jnp.sum(w, -1, keepdims=True)
            attended = attended + masked(h, mxu(w.astype(BF16), v) / total)
    else:

        def one_block(b, carry):
            peaks, totals, sums = carry
            k, v = keyvals(pl.multiple_of(b * block, 16))
            new_peaks, new_totals = [], []
            shrunk = jnp.zeros((count, E), F32)
            for h in range(HEADS):
                s = scores_of(h, k)
                peak = jnp.maximum(peaks[h], jnp.max(s, -1, keepdims=True))
                shrink = jnp.exp2((peaks[h] - peak) * factor[h])
                w = jnp.exp2((s - peak) * factor[h])
                new_peaks.append(peak)
                new_totals.append(totals[h] * shrink + jnp.sum(w, -1, keepdims=True))
                shrunk = shrunk + masked(h, sums * shrink + mxu(w.astype(BF16), v))
            return tuple(new_peaks), tuple(new_totals), shrunk

        start = (
            tuple(jnp.full((count, 1), -1e30, F32) for _ in range(HEADS)),
            tuple(jnp.zeros((count, 1), F32) for _ in range(HEADS)),
            jnp.zeros((count, E), F32),
        )
        _, totals, sums = lax.fori_loop(0, blocks, one_block, start)
        attended = jnp.zeros((count, E), F32)
        for h in range(HEADS):
            attended = attended + masked(h, sums / totals[h])
    hidden = embedded + mxu(attended.astype(BF16), wo[...])
    square = jnp.mean(hidden * hidden, -1, keepdims=True)
    normed = (hidden * lax.rsqrt(square + 1e-06) * gain[...]).astype(BF16)
    update = lax.dot_general(
        normed, wb[...], (((1,), (1,)), ((), ())), preferred_element_type=F32
    )
    back = [
        jnp.concatenate(
            [update[rows * c : rows * (c + 1), :], update[rows * (c + 1) : rows * (c + 2), :]], 1
        )
        for c in range(0, cells, 2)
    ]
    start = geo.band[4][0]
    for q, value in enumerate(back):
        at = slice(q * LANES, (q + 1) * LANES)
        out[:, at] = masked_rows(field[:, at] + value, start, geo.rows[4], lat, lats)


def synthesis_kernel(geo, lats, place, coarse, e2, o2, from_m2, from_p2, from_m3, from_p3, *refs):
    lat, parity = place[0], place[1] % 2
    part, d2, d3, d4, out, up3, up2, up1, ylow, yhigh, done, sems = refs
    bands = {2: d2, 3: d3, 4: d4}
    plan = exchange_plan(geo)

    def from_sides(level, b):
        n = geo.band[level][1]
        cols = [bands[level][b, :, LANES * p : LANES * (p + 1)] for p in range(geo.span[level][1])]
        for distance in (1, 2, 3):
            for which, count, row in plan[distance]:
                if which != level:
                    continue
                move = distance * geo.cells[level] // 2
                for p in range(count):
                    lanes = slice((b * count + p) * LANES, (b * count + p + 1) * LANES)
                    if distance == 1:
                        even = e2[row : row + n, lanes].astype(F32)
                        odd = o2[row : row + n, lanes].astype(F32)
                        low = jnp.where(parity == 0, odd, even)
                        high = jnp.where(parity == 0, even, odd)
                    else:
                        lows, highs = {2: (from_m2, from_p2), 3: (from_m3, from_p3)}[distance]
                        low = lows[row : row + n, lanes].astype(F32)
                        high = highs[row : row + n, lanes].astype(F32)
                    cols[p] = cols[p] + low
                    cols[p + move] = cols[p + move] + high
        return jnp.concatenate(cols, 1)

    uppers = {4: coarse, 3: up3, 2: up2, 1: up1}
    for level in (4, 3, 2):
        begin, pairs = geo.span[level]
        below = level - 1
        start, rows = geo.band[below]
        matrix = synthesis_matrix(start, rows, *geo.band[level])
        matrix = masked_rows(matrix, start, geo.rows[below], lat, lats)
        width = pairs * LANES
        for one, two, y in (
            (uppers[level][...], from_sides(level, 1), ylow),
            (from_sides(level, 0), from_sides(level, 2), yhigh),
        ):
            h, l = two_terms(jnp.concatenate([one, two], 0))
            y[0:rows, 0:width] = dot3(matrix, h, l)
        target = uppers[below]
        first, out_pairs = geo.span[below]

        step = best_step(rows)
        left = first_half(step)

        def joined(c, carry):
            row = pl.multiple_of(c * step, step)
            pair = synthesis(
                columns(ylow, row, step, pairs), columns(yhigh, row, step, pairs), begin, left
            )
            for q in range(out_pairs):
                put(target, row, q, pair(first + 2 * q))
            return carry

        lax.fori_loop(0, rows // step, joined, 0)

    n = geo.band[1][1]
    half = geo.rows[0] // 2
    for block in range(2):
        w = 0 if block == 0 else n - LANES
        matrix = synthesis_matrix(half * block, half, geo.band[1][0] + w, LANES)
        h, l = two_terms(up1[w : w + LANES, :])
        ylow[half * block : half * (block + 1), :] = dot3(matrix[:, 0:LANES], h, l)
    begin, pairs = geo.span[1]
    most = 112

    def last(row, count):
        left = first_half(count)
        pair = synthesis_of_lows(columns(ylow, row, count), begin, left)
        for q in range(geo.cells[0] // 2):
            more = part[pl.ds(row, count), pl.ds(LANES * q, LANES)]
            put(done, row, q, (pair(2 * q) + more).astype(BF16))

    def store(i, count):
        part = pl.ds(pl.multiple_of(i * most, 16), count)
        return pltpu.make_async_copy(done.at[part, :], out.at[part, :], sems.at[i])

    whole, rest = geo.rows[0] // most, geo.rows[0] % most

    def chunk(i, carry):
        last(pl.multiple_of(i * most, 16), most)
        store(i, most).start()
        return carry

    lax.fori_loop(0, whole, chunk, 0)
    if rest:
        last(whole * most, rest)
        store(whole, rest).start()
    for i in range(whole):
        store(i, most).wait()
    if rest:
        store(whole, rest).wait()


def call(kernel, out_shape, scratch, *args, cost=20_000_000, grant=24, raw=(), raw_out=(), stay=()):
    vmem = pl.BlockSpec(memory_space=pltpu.VMEM)
    smem = pl.BlockSpec(memory_space=pltpu.SMEM)
    anywhere = pl.BlockSpec(memory_space=pl.ANY)
    specs = [smem if a.ndim == 1 and a.size < 16 else vmem for a in args]
    for at in raw:
        specs[at] = anywhere
    held = lambda a: pltpu.with_memory_space_constraint(a, pltpu.HBM)
    args = [held(a) if i in stay else a for i, a in enumerate(args)]
    outs = [anywhere if i in raw_out else vmem for i in range(len(out_shape))]
    return pl.pallas_call(
        kernel,
        out_shape=tuple(out_shape),
        in_specs=specs,
        out_specs=tuple(outs),
        scratch_shapes=scratch,
        compiler_params=pltpu.CompilerParams(vmem_limit_bytes=grant << 20),
        cost_estimate=pl.CostEstimate(flops=cost, bytes_accessed=1 << 20, transcendentals=0),
    )(*args)


def shape(dims, dtype=F32):
    return jax.ShapeDtypeStruct(dims, dtype)


def per_device(mesh_shape, state_field, skip_gain, embed_weight, qkv_weight, head_scale, out_weight, norm_gain, back_weight):
    return program(
        mesh_shape, state_field, skip_gain, embed_weight, qkv_weight, head_scale, out_weight, norm_gain, back_weight
    )


def program(mesh_shape, state_field, skip_gain, embed_weight, qkv_weight, head_scale, out_weight, norm_gain, back_weight):
    lons, lats = mesh_shape["lon"], mesh_shape["lat"]
    rows, width = state_field.shape
    geo = Geometry(rows, width // C)
    lat, lon = lax.axis_index("lat"), lax.axis_index("lon")
    place = jnp.stack([lat, lon]).astype(jnp.int32)

    even_pairs = [(i, i ^ 1) for i in range(lons)]
    odd_pairs = [(i, (i + 1 if i % 2 else i - 1) % lons) for i in range(lons)]
    swap = [(i, lats - 1 - i) for i in range(lats)]

    def shifted(value, by):
        return lax.ppermute(value, "lon", [(i, (i + by) % lons) for i in range(lons)])

    wide = SIDE * C
    extended = NEAR + rows + NEAR
    side_e, side_o, edge = call(
        sides_kernel,
        [shape(side_shape(rows), BF16)] * 2 + [shape((HALO, width), BF16)],
        [pltpu.VMEM((2, rows, LANES), BF16), pltpu.SemaphoreType.DMA((5,))],
        place,
        state_field,
        raw=(1,),
        stay=(1,),
        cost=1_000_000,
    )
    edge = lax.ppermute(edge, "lat", swap)
    side_e = lax.ppermute(side_e, "lon", even_pairs)
    side_o = lax.ppermute(side_o, "lon", odd_pairs)

    w = [None] + [geo.span[level][1] * LANES for level in (1, 2, 3, 4)]
    low = lambda level, lanes: pltpu.VMEM((geo.low[level][1], w[lanes]), F32)
    bands = [(3, geo.band[level][1], w[level]) for level in (1, 2, 3, 4)]
    ll4, d2, d3, d4, deep_e, deep_o, p2, m2, p3, m3 = call(
        functools.partial(analysis_kernel, geo, lats),
        [shape((geo.low[4][1], w[4]))]
        + [shape(dims) for dims in bands[1:]]
        + [shape(plan_shape(geo, d), BF16) for d in (1, 1, 2, 2, 3, 3)],
        [
            pltpu.VMEM((geo.extended, width), BF16),
            pltpu.VMEM((geo.low[1][1], width), F32),
            low(1, 1),
            pltpu.VMEM((geo.low[1][1], w[1]), BF16),
            pltpu.VMEM((geo.low[1][1], w[1]), BF16),
            low(2, 1),
            low(2, 2),
            low(3, 2),
            low(3, 3),
            low(4, 3),
        ]
        + [pltpu.VMEM((geo.band[level][1], w[level - 1]), F32) for level in (2, 3, 4)]
        + [pltpu.SemaphoreType.DMA((geo.low[1][1] // 112,))],
        place,
        edge,
        skip_gain,
        state_field,
        raw=(3,),
        stay=(3,),
    )
    corner, beside = call(
        functools.partial(corners_kernel, geo),
        [shape((NEAR, 2 * wide), BF16), shape((rows, 2 * wide), BF16)],
        [],
        place,
        side_e,
        side_o,
        cost=100_000,
    )
    corner = lax.ppermute(corner, "lat", swap)
    count = geo.band[1][1]
    inner, lo_rim, hi_rim = call(
        functools.partial(inner_kernel, geo, lats),
        [shape(bands[0]), shape((count, 2 * wide)), shape((count, 2 * wide))],
        [
            pltpu.VMEM((extended, width), BF16),
            pltpu.VMEM((count, width), F32),
            pltpu.VMEM((count, width), F32),
            pltpu.SemaphoreType.DMA,
        ],
        place,
        edge,
        skip_gain,
        state_field,
        raw=(3,),
        stay=(3,),
    )
    ends = 2 * edge_pairs() * LANES
    (part,) = call(
        functools.partial(first_level_kernel, geo, lats),
        [shape((rows, width))],
        [
            pltpu.VMEM((extended, 2 * wide), BF16),
            pltpu.VMEM((count, 2 * wide), F32),
            pltpu.VMEM((count, 2 * wide), F32),
            pltpu.VMEM((3, count, ends), F32),
            pltpu.VMEM((rows, w[1]), F32),
            pltpu.VMEM((rows, w[1]), F32),
            pltpu.VMEM((2 * LANES, w[1]), BF16),
            pltpu.VMEM((2 * LANES, w[1]), BF16),
        ],
        place,
        beside,
        corner,
        skip_gain,
        inner,
        lo_rim,
        hi_rim,
        grant=30,
    )

    merged, size = ll4, 1
    total = geo.cells[4] * lons * C
    while size < lons:
        other = lax.ppermute(merged, "lon", [(i, i ^ size) for i in range(lons)])
        more = geo.cells[4] * C * size
        dims = (merged.shape[0], merged.shape[1] + more)
        if 2 * size < lons:
            (merged,) = call(
                functools.partial(merge_kernel, size, more), [shape(dims)], [], place, merged, other, cost=100_000
            )
        else:
            ring, tokens = call(
                functools.partial(last_merge_kernel, geo, size, more),
                [shape((dims[0], total)), shape((geo.rows[4], total), BF16)],
                [pltpu.VMEM(dims, F32)],
                place,
                merged,
                other,
                cost=100_000,
            )
        size = 2 * size
    others = lax.ppermute(tokens, "lat", swap)

    deep_e = lax.ppermute(deep_e, "lon", even_pairs)
    deep_o = lax.ppermute(deep_o, "lon", odd_pairs)
    from_m2, from_p2 = shifted(p2, 2), shifted(m2, -2)
    from_m3, from_p3 = shifted(p3, 3), shifted(m3, -3)

    key_count = 2 * geo.rows[4] * geo.cells[4] * lons
    blocks = key_count // 928 if key_count % 928 == 0 else 1
    (coarse,) = call(
        functools.partial(attention_kernel, geo, lats, blocks),
        [shape((geo.low[4][1], w[4]))],
        [
            pltpu.VMEM((geo.low[4][1], total + 6 * C), F32),
            pltpu.VMEM((key_count, C), F32),
            pltpu.VMEM((key_count, C), BF16),
        ],
        place,
        ring,
        tokens,
        others,
        embed_weight,
        qkv_weight,
        head_scale,
        out_weight,
        norm_gain[None],
        back_weight.T,
        cost=200_000_000,
        grant=40,
    )

    (out,) = call(
        functools.partial(synthesis_kernel, geo, lats),
        [shape((rows, width), BF16)],
        [pltpu.VMEM((geo.band[level][1], w[level]), F32) for level in (3, 2, 1)]
        + [
            pltpu.VMEM((rows, w[1]), F32),
            pltpu.VMEM((geo.band[1][1], w[2]), F32),
            pltpu.VMEM((rows, width), BF16),
            pltpu.SemaphoreType.DMA((rows // 112 + 1,)),
        ],
        place,
        coarse,
        deep_e,
        deep_o,
        from_m2,
        from_p2,
        from_m3,
        from_p3,
        part,
        d2,
        d3,
        d4,
        raw_out=(0,),
        grant=30,
    )
    return out


def solution(mesh):
    in_specs = (P("lat", ("member", "lon")), P(), P(), P(), P(), P(), P(), P())
    out_specs = P("lat", ("member", "lon"))
    return jax.shard_map(
        functools.partial(per_device, dict(mesh.shape)),
        mesh=mesh,
        in_specs=in_specs,
        out_specs=out_specs,
        check_vma=False,
    )
```

```python
import copy
import functools
import math

import jax
import jax.numpy as jnp
import numpy as np
from jax import lax
from jax.experimental import pallas as pl
from jax.experimental.pallas import tpu as pltpu
from jax.sharding import PartitionSpec as P


C = 64
HEADS = 8
HEAD_DIM = 32
E = 256
LANES = 128
HALO = 96
LEAD = 16

LOW = np.array(
    [
        -0.010597401784997278,
        0.032883011666982945,
        0.030841381835986965,
        -0.18703481171888114,
        -0.02798376941698385,
        0.6308807679295904,
        0.7148465705525415,
        0.23037781330885523,
    ]
)
HIGH = np.array([(-1.0) ** j * LOW[7 - j] for j in range(8)])


F32 = jnp.float32
BF16 = jnp.bfloat16


def two_terms(value):
    top = value.astype(BF16)
    return top, (value - top.astype(F32)).astype(BF16)


def masked_rows(matrix, start, count, lat, lats):
    row = lax.broadcasted_iota(jnp.int32, matrix.shape, 0) + (start + lat * count)
    return jnp.where((row >= 0) & (row < count * lats), matrix, 0.0)


def banded(shape, low, high, row_factor, column_factor, offset):
    row = lax.broadcasted_iota(jnp.int32, shape, 0)
    column = lax.broadcasted_iota(jnp.int32, shape, 1)
    tap = row_factor * row + column_factor * column + offset
    if high is not None:
        second = column >= shape[1] // 2
        tap = jnp.where(second, tap - column_factor * (shape[1] // 2), tap)
    matrix = jnp.zeros(shape, F32)
    for t in range(8):
        value = F32(low[t]) if high is None else jnp.where(second, F32(high[t]), F32(low[t]))
        matrix = jnp.where(tap == t, value, matrix)
    return matrix


def analysis_matrix(taps, out_start, out_rows, in_start, in_rows):
    return banded((out_rows, in_rows), taps, None, -2, 1, in_start + 3 - 2 * out_start)


def synthesis_matrix(out_start, out_rows, in_start, in_rows):
    shape = (out_rows, 2 * in_rows)
    return banded(shape, LOW, HIGH, 1, -2, out_start - 2 * in_start + 3)


def mxu(a, b):
    return jnp.dot(a, b, preferred_element_type=F32)


def dot3(matrix, vh, vl):
    mh, ml = two_terms(matrix)
    return mxu(mh, vh) + mxu(mh, vl) + mxu(ml, vh)


def first_half(rows):
    return lax.broadcasted_iota(jnp.int32, (rows, LANES), 1) < C


def half_turn(value):
    return None if value is None else pltpu.roll(value, C, 1)


def pick(left, a, b):
    if a is None and b is None:
        return None
    return jnp.where(left, 0.0 if a is None else a, 0.0 if b is None else b)


def plus(a, b, factor):
    if b is None:
        return a
    if a is None:
        return b * factor
    return a + b * factor


class Memo:
    def __init__(self, make):
        self.make, self.known = make, {}

    def __call__(self, n):
        if n not in self.known:
            self.known[n] = self.make(n)
        return self.known[n]


def analysis(cols, start, left):
    turned = Memo(lambda i: half_turn(cols[i]) if 0 <= i < len(cols) else None)
    plain = lambda i: cols[i] if 0 <= i < len(cols) else None
    if start % 2 == 0:
        at = lambda n: n - 1 - start // 2
        u = Memo(lambda n: pick(left, turned(at(n) - 1), plain(at(n))))
        w = Memo(lambda n: pick(left, plain(at(n)), turned(at(n) + 1)))
    else:
        at = lambda n: n - (start + 3) // 2
        u = Memo(lambda n: pick(left, plain(at(n)), turned(at(n) + 1)))
        w = Memo(lambda n: pick(left, turned(at(n)), plain(at(n) + 1)))

    def band(taps):
        def make(k):
            total = None
            for step in range(4):
                total = plus(total, u(k + step), float(taps[2 * step]))
                total = plus(total, w(k + step), float(taps[2 * step + 1]))
            return total

        return make

    return band(LOW), band(HIGH)


def synthesis(lows, highs, start, left):
    parity = start % 2

    def cells(cols):
        col = lambda k: cols[(k - start) // 2] if 0 <= k - start < 2 * len(cols) else None
        turned = Memo(lambda k: half_turn(col(k)))

        def at(k):
            if k % 2 == parity:
                return col(k)
            return pick(left, turned(k - 1), turned(k + 1))

        return Memo(at)

    sources = ((cells(lows), LOW), (cells(highs), HIGH))

    def output(first):
        def make(n):
            total = None
            for step in range(4):
                for source, taps in sources:
                    total = plus(total, source(n - step), float(taps[2 * step + first]))
            return total

        return Memo(make)

    u, w = output(0), output(1)
    u_turned, w_turned = Memo(lambda n: half_turn(u(n))), Memo(lambda n: half_turn(w(n)))

    def pair(m):
        if m % 2:
            n = (m + 3) // 2
            if n % 2 == parity:
                return pick(left, u(n), w_turned(n))
            return pick(left, u_turned(n - 1), w(n - 1))
        n = m // 2 + 1
        if n % 2 == parity:
            return pick(left, w(n), u(n))
        return pick(left, w_turned(n - 1), u_turned(n + 1))

    return pair


def synthesis_of_lows(lows, start, left):
    def dup(k):
        i = (k - start) // 2
        if not 0 <= i < len(lows):
            return None
        turned = rolled(i)
        return jnp.where(left, lows[i], turned) if (k - start) % 2 == 0 else jnp.where(left, turned, lows[i])

    rolled = Memo(lambda i: half_turn(lows[i]))
    both = Memo(dup)

    def tap(t):
        return F32(LOW[t]) if 0 <= t < 8 else F32(0.0)

    weights = [jnp.where(left[0:8], tap(7 - 2 * i), tap(8 - 2 * i)) for i in range(5)]
    weights = [jnp.concatenate([v] * (left.shape[0] // 8), 0) for v in weights]

    def pair(m):
        total = None
        for i in range(5):
            cell = both(m // 2 - 2 + i)
            if cell is not None:
                total = cell * weights[i] if total is None else total + cell * weights[i]
        return total

    return pair


def columns(ref, row, rows, count=None):
    count = ref.shape[-1] // LANES if count is None else count
    return [ref[pl.ds(row, rows), pl.ds(LANES * p, LANES)] for p in range(count)]


def put(ref, row, p, value, lead=()):
    ref[lead + (pl.ds(row, value.shape[0]), pl.ds(LANES * p, LANES))] = value


class Geometry:
    def __init__(self, rows, cells):
        self.rows = [rows >> level for level in range(5)]
        self.cells = [cells >> level for level in range(5)]
        up = lambda value, step: -(-value // step) * step
        self.band = [
            None,
            (-4, up(self.rows[1] + 4, 120)),
            (0, up(self.rows[2] + 3, 8)),
            (-3, up(self.rows[3] + 6, 8)),
            (0, up(self.rows[4] + 3, 8)),
        ]
        self.low = [
            None,
            (-52, up(self.rows[1] + 97, 112)),
            (-24, up(self.rows[2] + 45, 88)),
            (-11, up(self.rows[3] + 20, 8)),
            (0, up(self.rows[4] + 3, 8)),
        ]
        self.skip = [None] + [self.band[level][0] - self.low[level][0] for level in (1, 2, 3, 4)]
        self.span = [None, (-2, self.cells[1] // 2 + 2)]
        for level in (2, 3, 4):
            self.span.append((-3, self.cells[level] // 2 + 3))
        self.extended = max(
            LEAD + 2 * HALO + rows, 2 * (self.low[1][1] - 112) + 256
        )


    def placed(self, lat):
        here = copy.copy(self)
        shift = jnp.where(lat == 0, 0, -3)
        here.band, here.low = list(self.band), list(self.low)
        for level in (2, 4):
            for ranges in (here.band, here.low):
                ranges[level] = (ranges[level][0] + shift, ranges[level][1])
        return here


STEP = 240
SIDE = 8
NEAR = 16


def best_step(rows, most=None):
    return max(s for s in range(8, (most or STEP) + 1, 8) if rows % s == 0)


def low_rows(geo, level, source, source_start, target):
    first, pairs = geo.span[level]
    rows = geo.low[level][1]
    step = best_step(rows, 336)
    left = first_half(step)

    def body(c, carry):
        row = pl.multiple_of(c * step, step)
        low, _ = analysis(columns(source, row, step), source_start, left)
        for q in range(pairs):
            put(target, row, q, low(first + 2 * q))
        return carry

    lax.fori_loop(0, rows // step, body, 0)


def band_rows(geo, level, lo, skip, hi, source_start, gain, bands):
    first, pairs = geo.span[level]
    rows = geo.band[level][1]
    step = best_step(rows)
    left = first_half(step)

    def body(c, carry):
        row = pl.multiple_of(c * step, step)
        g = []
        for b in range(3):
            one = gain[level - 1, b : b + 1, :]
            g.append(jnp.broadcast_to(jnp.concatenate([one, one], 1), (step, LANES)))
        _, high = analysis(columns(lo, row + skip, step), source_start, left)
        for q in range(pairs):
            put(bands, row, q, high(first + 2 * q) * g[0], (0,))
        low, high = analysis(columns(hi, row, step), source_start, left)
        for q in range(pairs):
            put(bands, row, q, low(first + 2 * q) * g[1], (1,))
            put(bands, row, q, high(first + 2 * q) * g[2], (2,))
        return carry

    lax.fori_loop(0, rows // step, body, 0)


def analysis_kernel(geo, lats, place, edge, gain, x, *refs):
    lat, parity = place[0], place[1] % 2
    geo = geo.placed(lat)
    ll4, d2, d3, d4, send_e, send_o, p2, m2, p3, m3 = refs[:10]
    ext, la, g1, gh, gl, lo2, g2, lo3, g3, lo4, hi2, hi3, hi4, sems = refs[10:]
    rows = geo.rows[0]
    start, count = geo.low[1]
    width = x.shape[1]
    begin = LEAD + HALO
    blocks = count // 112
    cuts = [0] + [min(rows, 224 * b + 256 - begin) for b in range(blocks - 1)] + [rows]
    copies = []
    for i in range(blocks):
        part = pl.ds(cuts[i], cuts[i + 1] - cuts[i])
        to = pl.ds(begin + cuts[i], cuts[i + 1] - cuts[i])
        copies.append(pltpu.make_async_copy(x.at[part, :], ext.at[to, :], sems.at[i]))
        copies[-1].start()
    top = slice(LEAD, begin)
    bottom = slice(begin + rows, begin + rows + HALO)
    ext[0:LEAD, :] = jnp.zeros((LEAD, width), BF16)
    tail = geo.extended - (LEAD + 2 * HALO + rows)
    if tail:
        ext[geo.extended - tail :, :] = jnp.zeros((tail, width), BF16)

    @pl.when(lat == 0)
    def _():
        ext[top, :] = jnp.zeros((HALO, width), BF16)
        ext[bottom, :] = edge[...]

    @pl.when(lat != 0)
    def _():
        ext[top, :] = edge[...]
        ext[bottom, :] = jnp.zeros((HALO, width), BF16)

    base = analysis_matrix(LOW, start, 112, 0 - LEAD - HALO, 256)
    for b in range(blocks):
        copies[b].wait()
        mh, ml = two_terms(masked_rows(base, start + 112 * b, geo.rows[1], lat, lats))
        data = ext[224 * b : 224 * b + 256, :]
        la[112 * b : 112 * b + 112, :] = mxu(mh, data) + mxu(ml, data)
    low_rows(geo, 1, la, 0, g1)
    gh[...], gl[...] = two_terms(g1[...])
    out_start, out_rows = geo.low[2]
    for b in range(out_rows // 88):
        at = min(176 * b, count - 192)
        window = slice(at, at + 192)
        matrix = analysis_matrix(LOW, out_start + 88 * b, 88, start + at, 192)
        matrix = masked_rows(matrix, out_start + 88 * b, geo.rows[2], lat, lats)
        lo2[88 * b : 88 * b + 88, :] = dot3(matrix, gh[window, :], gl[window, :])
    low_rows(geo, 2, lo2, geo.span[1][0], g2)
    for level, source, lo, target in ((3, g2, lo3, g3), (4, g3, lo4, ll4)):
        vh, vl = two_terms(source[...])
        matrix = analysis_matrix(LOW, *geo.low[level], *geo.low[level - 1])
        matrix = masked_rows(matrix, geo.low[level][0], geo.rows[level], lat, lats)
        lo[...] = dot3(matrix, vh, vl)
        low_rows(geo, level, lo, geo.span[level - 1][0], target)
    d = {2: d2, 3: d3, 4: d4}
    for level, lo, hi in ((2, lo2, hi2), (3, lo3, hi3), (4, lo4, hi4)):
        deep_bands(geo, lats, lat, level, {2: (gh, gl), 3: g2, 4: g3}[level], lo, hi, gain, d[level])

    def fill(distance, to_left, to_right):
        for level, count, row in exchange_plan(geo)[distance]:
            n = geo.band[level][1]
            move = distance * geo.cells[level] // 2
            for b in range(3):
                lanes = slice(b * count * LANES, (b + 1) * count * LANES)
                to_left[row : row + n, lanes] = d[level][b, :, 0 : count * LANES].astype(BF16)
                to_right[row : row + n, lanes] = d[level][
                    b, :, move * LANES : (move + count) * LANES
                ].astype(BF16)

    @pl.when(parity == 0)
    def _():
        fill(1, send_o, send_e)

    @pl.when(parity != 0)
    def _():
        fill(1, send_e, send_o)

    fill(2, m2, p2)
    fill(3, m3, p3)


def deep_bands(geo, lats, lat, level, source, lo, hi, gain, bands):
    start, count = geo.band[level]
    in_start = geo.low[level - 1][0]
    if level == 2:
        at, size = 32, 2 * count + 32
        vh, vl = source[0][at : at + size, :], source[1][at : at + size, :]
    else:
        at, size = 0, source.shape[0]
        vh, vl = two_terms(source[...])
    matrix = analysis_matrix(HIGH, start, count, in_start + at, size)
    matrix = masked_rows(matrix, start, geo.rows[level], lat, lats)
    hi[...] = dot3(matrix, vh, vl)
    skip = geo.skip[level]
    band_rows(geo, level, lo, skip, hi, geo.span[level - 1][0], gain, bands)


def side_shape(rows):
    tall = side_split(rows)
    return (rows + tall // 3, 3 * LANES)


def side_split(rows):
    return -(-(-(-rows // 2)) // 48) * 48


def sides_kernel(place, x, side_e, side_o, edge, ends, sems):
    lat, parity = place[0], place[1] % 2
    rows, width = x.shape
    lanes = 3 * LANES
    tall = side_split(rows)
    third = tall // 3
    at = pl.multiple_of(jnp.where(lat == 0, rows - HALO, 0), NEAR)
    strip = pltpu.make_async_copy(x.at[pl.ds(at, HALO), :], edge, sems.at[4])
    strip.start()

    def both(low, high):
        body = pl.ds(0, rows)
        copies = [
            pltpu.make_async_copy(x.at[:, pl.ds(lanes, LANES)], ends.at[0], sems.at[0]),
            pltpu.make_async_copy(x.at[:, pl.ds(width - lanes - LANES, LANES)], ends.at[1], sems.at[1]),
            pltpu.make_async_copy(x.at[:, pl.ds(0, lanes)], low.at[body, :], sems.at[2]),
            pltpu.make_async_copy(x.at[:, pl.ds(width - lanes, lanes)], high.at[body, :], sems.at[3]),
        ]
        for copy in copies:
            copy.start()
        for side, out in ((0, low), (1, high)):
            copies[side].wait()
            one = ends[side, 0:tall, :].astype(F32)
            two = ends[side, tall:rows, :].astype(F32)
            if side:
                one = half_turn(one)
            else:
                two = half_turn(two)
            two = jnp.concatenate([two, jnp.zeros((2 * tall - rows, LANES), F32)], 0)
            mixed = jnp.where(lax.broadcasted_iota(jnp.int32, (tall, LANES), 1) < C, one, two)
            for b in range(3):
                block = mixed[third * b : third * (b + 1), :].astype(BF16)
                out[rows : rows + third, b * LANES : (b + 1) * LANES] = block
        copies[2].wait()
        copies[3].wait()

    @pl.when(parity == 0)
    def _():
        both(side_o, side_e)

    @pl.when(parity != 0)
    def _():
        both(side_e, side_o)

    strip.wait()


def unpack_side(side, rows, out, row, at_left):
    lanes = 3 * LANES
    tall = side_split(rows)
    third = tall // 3
    half = jnp.concatenate(
        [side[rows : rows + third, b * LANES : (b + 1) * LANES].astype(F32) for b in range(3)], 0
    )
    is_left = lax.broadcasted_iota(jnp.int32, (tall, LANES), 1) < C
    turned = half_turn(half)
    if at_left:
        one, two = jnp.where(is_left, 0.0, turned), jnp.where(is_left, 0.0, half)
        pairs, end = slice(LANES, LANES + lanes), slice(0, LANES)
    else:
        one, two = jnp.where(is_left, half, 0.0), jnp.where(is_left, turned, 0.0)
        pairs, end = slice(0, lanes), slice(lanes, lanes + LANES)
    base = 0 if at_left else SIDE * C
    out[row : row + rows, base + pairs.start : base + pairs.stop] = side[0:rows, :]
    out[row : row + tall, base + end.start : base + end.stop] = one.astype(BF16)
    out[row + tall : row + rows, base + end.start : base + end.stop] = two[0 : rows - tall].astype(BF16)


def corners_kernel(geo, place, side_e, side_o, out, ext):
    lat, parity = place[0], place[1] % 2
    rows = geo.rows[0]

    @pl.when(parity == 0)
    def _():
        unpack_side(side_o, rows, ext, 0, True)
        unpack_side(side_e, rows, ext, 0, False)

    @pl.when(parity != 0)
    def _():
        unpack_side(side_e, rows, ext, 0, True)
        unpack_side(side_o, rows, ext, 0, False)

    at = jnp.where(lat == 0, rows - NEAR, 0)
    out[...] = ext[pl.ds(pl.multiple_of(at, NEAR), NEAR), :]


def merge_kernel(size, more, place, mine, other, out):
    width = mine.shape[1]

    def add(lower, upper):
        out[:, 0:more] = lower[:, 0:more]
        out[:, more:width] = lower[:, more:] + upper[:, 0 : width - more]
        out[:, width:] = upper[:, width - more :]

    lower_half = (place[1] // size) % 2 == 0

    @pl.when(lower_half)
    def _():
        add(mine, other)

    @pl.when(jnp.logical_not(lower_half))
    def _():
        add(other, mine)


def last_merge_kernel(geo, size, more, place, mine, other, ring, tokens, merged):
    merge_kernel(size, more, place, mine, other, merged)
    around = ring.shape[1]
    fold = merged.shape[1] - around
    ring[:, 0:fold] = merged[:, 0:fold] + merged[:, around:]
    ring[:, fold:] = merged[:, fold:around]
    count = geo.rows[4]
    own = jnp.where(place[0] == 0, ring[0:count, :], ring[3 : 3 + count, :])
    tokens[...] = own.astype(BF16)


def latitude_bands(geo, lats, lat, ext, la, ha):
    start, count = geo.band[1]
    low = analysis_matrix(LOW, start, 120, -NEAR, 256)
    high = analysis_matrix(HIGH, start, 120, -NEAR, 256)
    for b in range(count // 120):
        data = ext[240 * b : 240 * b + 256, :]
        for matrix, out in ((low, la), (high, ha)):
            mh, ml = two_terms(masked_rows(matrix, start + 120 * b, geo.rows[1], lat, lats))
            out[120 * b : 120 * b + 120, :] = mxu(mh, data) + mxu(ml, data)


def first_bands(row, los, his, start, groups, gain, bands):
    step = los[0].shape[0]
    left = first_half(step)
    g = []
    for b in range(3):
        one = gain[0, b : b + 1, :]
        g.append(jnp.broadcast_to(jnp.concatenate([one, one], 1), (step, LANES)))
    _, high = analysis(los, start, left)
    for q, k in groups:
        put(bands, row, q, high(k) * g[0], (0,))
    low, high = analysis(his, start, left)
    for q, k in groups:
        put(bands, row, q, low(k) * g[1], (1,))
        put(bands, row, q, high(k) * g[2], (2,))


def edge_pairs():
    return 2


def inner_kernel(geo, lats, place, edge, gain, x, d1, lo_rim, hi_rim, ext, la, ha, sem):
    lat = place[0]
    rows, width = x.shape
    copy = pltpu.make_async_copy(x, ext.at[pl.ds(NEAR, rows), :], sem)
    copy.start()

    @pl.when(lat == 0)
    def _():
        ext[0:NEAR, :] = jnp.zeros((NEAR, width), BF16)
        ext[NEAR + rows :, :] = edge[0:NEAR, :]

    @pl.when(lat != 0)
    def _():
        ext[0:NEAR, :] = edge[HALO - NEAR :, :]
        ext[NEAR + rows :, :] = jnp.zeros((NEAR, width), BF16)

    copy.wait()
    latitude_bands(geo, lats, lat, ext, la, ha)
    rim = SIDE * C
    for out, source in ((lo_rim, la), (hi_rim, ha)):
        out[:, 0:rim] = source[:, 0:rim]
        out[:, rim:] = source[:, width - rim :]
    first, pairs = geo.span[1]
    ends = edge_pairs()
    groups = [(q, first + 2 * q) for q in range(ends, pairs - ends)]
    step = best_step(geo.band[1][1])

    def body(c, carry):
        row = pl.multiple_of(c * step, step)
        first_bands(row, columns(la, row, step), columns(ha, row, step), 0, groups, gain, d1)
        return carry

    lax.fori_loop(0, geo.band[1][1] // step, body, 0)


def first_level_kernel(geo, lats, place, beside, corner, gain, inner, lo_rim, hi_rim, part, ext, lo_side, hi_side, d1, la, ha, xh, xl):
    lat = place[0]
    rows, _ = part.shape
    lanes = SIDE * C
    top, bottom = slice(0, NEAR), slice(NEAR + rows, 2 * NEAR + rows)

    def rims(near, far):
        ext[far, :] = jnp.zeros((NEAR, 2 * lanes), BF16)
        ext[near, :] = corner[...]

    @pl.when(lat == 0)
    def _():
        rims(bottom, top)

    @pl.when(lat != 0)
    def _():
        rims(top, bottom)

    ext[NEAR : NEAR + rows, :] = beside[...]
    start, count = geo.band[1]
    latitude_bands(geo, lats, lat, ext, lo_side, hi_side)
    first, pairs = geo.span[1]
    ends = edge_pairs()
    step = best_step(count)
    near = SIDE // 2

    def body(c, carry):
        row = pl.multiple_of(c * step, step)
        sources = [columns(ref, row, step) for ref in (lo_side, hi_side, lo_rim, hi_rim)]
        lo_s, hi_s, lo_r, hi_r = sources
        groups = [(q, first + 2 * q) for q in range(ends)]
        first_bands(
            row, lo_s[:near] + lo_r[:near], hi_s[:near] + hi_r[:near], -SIDE, groups, gain, d1
        )
        groups = [(ends + q, first + 2 * (pairs - ends + q)) for q in range(ends)]
        begin = geo.cells[0] - SIDE
        first_bands(
            row, lo_r[near:] + lo_s[near:], hi_r[near:] + hi_s[near:], begin, groups, gain, d1
        )
        return carry

    lax.fori_loop(0, count // step, body, 0)
    rim, whole = ends * LANES, pairs * LANES

    def terms(b, window, to):
        for lanes_to, source, lanes_from in (
            (slice(0, rim), d1, slice(0, rim)),
            (slice(rim, whole - rim), inner, slice(rim, whole - rim)),
            (slice(whole - rim, whole), d1, slice(rim, 2 * rim)),
        ):
            h, l = two_terms(source[b, window, lanes_from])
            xh[to, lanes_to], xl[to, lanes_to] = h, l

    half = rows // 2
    ylow, yhigh = la, ha
    used = slice(0, whole)
    upper, lower = slice(0, LANES), slice(LANES, 2 * LANES)
    for block in range(2):
        w = 0 if block == 0 else count - LANES
        window = slice(w, w + LANES)
        target = slice(half * block, half * (block + 1))
        matrix = synthesis_matrix(half * block, half, start + w, LANES)
        sh, sl = two_terms(matrix)
        terms(0, window, upper)
        terms(2, window, lower)
        yhigh[target, used] = mxu(sh, xh[...]) + mxu(sh, xl[...]) + mxu(sl, xh[...])
        terms(1, window, lower)
        sh, sl = sh[:, LANES:], sl[:, LANES:]
        vh, vl = xh[lower, :], xl[lower, :]
        ylow[target, used] = mxu(sh, vh) + mxu(sh, vl) + mxu(sl, vh)

    begin, pairs = geo.span[1]
    most = rows

    def chunk(i, carry):
        row = pl.multiple_of(i * most, 8)
        pair = synthesis(
            columns(ylow, row, most, pairs), columns(yhigh, row, most, pairs), begin, first_half(most)
        )
        for q in range(geo.cells[0] // 2):
            put(part, row, q, pair(2 * q))
        return carry

    lax.fori_loop(0, rows // most, chunk, 0)


def exchange_plan(geo):
    plan = {}
    for distance in (1, 2, 3):
        entries, row = [], 0
        for level in (3, 4, 2):
            count = geo.span[level][1] - distance * geo.cells[level] // 2
            if count > 0:
                entries.append((level, count, row))
                row += -(-geo.band[level][1] // 16) * 16
        plan[distance] = entries
    return plan


def plan_shape(geo, distance):
    entries = exchange_plan(geo)[distance]
    level, _, row = entries[-1]
    rows = row + geo.band[level][1]
    return (rows, max(count for _, count, _ in entries) * 3 * LANES)


def attention_kernel(geo, lats, blocks, place, ring, own, others, we, wqkv, scale, wo, gain, wb, out, around, listed, keys):
    lat, lon = place[0], place[1]
    geo = geo.placed(lat)
    rows, width = out.shape
    cells = width // C
    total = ring.shape[1]
    around[:, 0:total] = ring[...]
    around[:, total:] = ring[:, 0 : around.shape[1] - total]
    field = around[:, pl.ds(pl.multiple_of(lon * (geo.cells[4] * C), LANES), width)]
    count = geo.rows[4]
    for source, shift in ((own, 0), (others, count)):
        for pair in range(total // LANES):
            value = source[:, pair * LANES : (pair + 1) * LANES].astype(F32)
            for side in range(2):
                at = 2 * count * (2 * pair + side) + shift
                listed[at : at + count, :] = value[:, side * C : (side + 1) * C]
    keys[...] = listed[...].astype(BF16)
    own = jnp.concatenate([field[:, C * c : C * (c + 1)] for c in range(cells)], 0)
    count = own.shape[0]
    embedded = mxu(own.astype(BF16), we[...])
    queries = mxu(embedded.astype(BF16), wqkv[:, 0:E]).astype(BF16)
    lane = lax.broadcasted_iota(jnp.int32, (1, E), 1)
    block = keys.shape[0] // blocks
    factor = [scale[h] * (math.log2(math.e) / math.sqrt(HEAD_DIM)) for h in range(HEADS)]

    def keyvals(start):
        spread = mxu(keys[pl.ds(start, block), :], we[...]).astype(BF16)
        both = mxu(spread, wqkv[:, E : 3 * E]).astype(BF16)
        return both[:, 0:E], both[:, E : 2 * E]

    def scores_of(h, k):
        mine = (lane >= h * HEAD_DIM) & (lane < (h + 1) * HEAD_DIM)
        q = jnp.where(mine, queries, jnp.zeros_like(queries))
        return lax.dot_general(q, k, (((1,), (1,)), ((), ())), preferred_element_type=F32)

    def masked(h, value):
        mine = (lane >= h * HEAD_DIM) & (lane < (h + 1) * HEAD_DIM)
        return jnp.where(mine, value, jnp.zeros_like(value))

    if blocks == 1:
        k, v = keyvals(0)
        attended = jnp.zeros((count, E), F32)
        for h in range(HEADS):
            s = scores_of(h, k)
            w = jnp.exp2((s - jnp.max(s, -1, keepdims=True)) * factor[h])
            total = jnp.sum(w, -1, keepdims=True)
            attended = attended + masked(h, mxu(w.astype(BF16), v) / total)
    else:

        def one_block(b, carry):
            peaks, totals, sums = carry
            k, v = keyvals(pl.multiple_of(b * block, 16))
            new_peaks, new_totals = [], []
            shrunk = jnp.zeros((count, E), F32)
            for h in range(HEADS):
                s = scores_of(h, k)
                peak = jnp.maximum(peaks[h], jnp.max(s, -1, keepdims=True))
                shrink = jnp.exp2((peaks[h] - peak) * factor[h])
                w = jnp.exp2((s - peak) * factor[h])
                new_peaks.append(peak)
                new_totals.append(totals[h] * shrink + jnp.sum(w, -1, keepdims=True))
                shrunk = shrunk + masked(h, sums * shrink + mxu(w.astype(BF16), v))
            return tuple(new_peaks), tuple(new_totals), shrunk

        start = (
            tuple(jnp.full((count, 1), -1e30, F32) for _ in range(HEADS)),
            tuple(jnp.zeros((count, 1), F32) for _ in range(HEADS)),
            jnp.zeros((count, E), F32),
        )
        _, totals, sums = lax.fori_loop(0, blocks, one_block, start)
        attended = jnp.zeros((count, E), F32)
        for h in range(HEADS):
            attended = attended + masked(h, sums / totals[h])
    hidden = embedded + mxu(attended.astype(BF16), wo[...])
    square = jnp.mean(hidden * hidden, -1, keepdims=True)
    normed = (hidden * lax.rsqrt(square + 1e-06) * gain[...]).astype(BF16)
    update = lax.dot_general(
        normed, wb[...], (((1,), (1,)), ((), ())), preferred_element_type=F32
    )
    back = [
        jnp.concatenate(
            [update[rows * c : rows * (c + 1), :], update[rows * (c + 1) : rows * (c + 2), :]], 1
        )
        for c in range(0, cells, 2)
    ]
    start = geo.band[4][0]
    for q, value in enumerate(back):
        at = slice(q * LANES, (q + 1) * LANES)
        out[:, at] = masked_rows(field[:, at] + value, start, geo.rows[4], lat, lats)


def synthesis_kernel(geo, lats, place, coarse, e2, o2, from_m2, from_p2, from_m3, from_p3, *refs):
    lat, parity = place[0], place[1] % 2
    geo = geo.placed(lat)
    part, d2, d3, d4, out, up3, up2, up1, ylow, yhigh, done, sems = refs
    bands = {2: d2, 3: d3, 4: d4}
    plan = exchange_plan(geo)

    def from_sides(level, b):
        n = geo.band[level][1]
        cols = [bands[level][b, :, LANES * p : LANES * (p + 1)] for p in range(geo.span[level][1])]
        for distance in (1, 2, 3):
            for which, count, row in plan[distance]:
                if which != level:
                    continue
                move = distance * geo.cells[level] // 2
                for p in range(count):
                    lanes = slice((b * count + p) * LANES, (b * count + p + 1) * LANES)
                    if distance == 1:
                        even = e2[row : row + n, lanes].astype(F32)
                        odd = o2[row : row + n, lanes].astype(F32)
                        low = jnp.where(parity == 0, odd, even)
                        high = jnp.where(parity == 0, even, odd)
                    else:
                        lows, highs = {2: (from_m2, from_p2), 3: (from_m3, from_p3)}[distance]
                        low = lows[row : row + n, lanes].astype(F32)
                        high = highs[row : row + n, lanes].astype(F32)
                    cols[p] = cols[p] + low
                    cols[p + move] = cols[p + move] + high
        return jnp.concatenate(cols, 1)

    uppers = {4: coarse, 3: up3, 2: up2, 1: up1}
    for level in (4, 3, 2):
        begin, pairs = geo.span[level]
        below = level - 1
        start, rows = geo.band[below]
        matrix = synthesis_matrix(start, rows, *geo.band[level])
        matrix = masked_rows(matrix, start, geo.rows[below], lat, lats)
        width = pairs * LANES
        for one, two, y in (
            (uppers[level][...], from_sides(level, 1), ylow),
            (from_sides(level, 0), from_sides(level, 2), yhigh),
        ):
            h, l = two_terms(jnp.concatenate([one, two], 0))
            y[0:rows, 0:width] = dot3(matrix, h, l)
        target = uppers[below]
        first, out_pairs = geo.span[below]

        step = best_step(rows)
        left = first_half(step)

        def joined(c, carry):
            row = pl.multiple_of(c * step, step)
            pair = synthesis(
                columns(ylow, row, step, pairs), columns(yhigh, row, step, pairs), begin, left
            )
            for q in range(out_pairs):
                put(target, row, q, pair(first + 2 * q))
            return carry

        lax.fori_loop(0, rows // step, joined, 0)

    n = geo.band[1][1]
    half = geo.rows[0] // 2
    for block in range(2):
        w = 0 if block == 0 else n - LANES
        matrix = synthesis_matrix(half * block, half, geo.band[1][0] + w, LANES)
        h, l = two_terms(up1[w : w + LANES, :])
        ylow[half * block : half * (block + 1), :] = dot3(matrix[:, 0:LANES], h, l)
    begin, pairs = geo.span[1]
    most = 112

    def last(row, count):
        left = first_half(count)
        pair = synthesis_of_lows(columns(ylow, row, count), begin, left)
        for q in range(geo.cells[0] // 2):
            more = part[pl.ds(row, count), pl.ds(LANES * q, LANES)]
            put(done, row, q, (pair(2 * q) + more).astype(BF16))

    def store(i, count):
        part = pl.ds(pl.multiple_of(i * most, 16), count)
        return pltpu.make_async_copy(done.at[part, :], out.at[part, :], sems.at[i])

    whole, rest = geo.rows[0] // most, geo.rows[0] % most

    def chunk(i, carry):
        last(pl.multiple_of(i * most, 16), most)
        store(i, most).start()
        return carry

    lax.fori_loop(0, whole, chunk, 0)
    if rest:
        last(whole * most, rest)
        store(whole, rest).start()
    for i in range(whole):
        store(i, most).wait()
    if rest:
        store(whole, rest).wait()


def call(kernel, out_shape, scratch, *args, cost=20_000_000, grant=24, raw=(), raw_out=(), stay=()):
    vmem = pl.BlockSpec(memory_space=pltpu.VMEM)
    smem = pl.BlockSpec(memory_space=pltpu.SMEM)
    anywhere = pl.BlockSpec(memory_space=pl.ANY)
    specs = [smem if a.ndim == 1 and a.size < 16 else vmem for a in args]
    for at in raw:
        specs[at] = anywhere
    held = lambda a: pltpu.with_memory_space_constraint(a, pltpu.HBM)
    args = [held(a) if i in stay else a for i, a in enumerate(args)]
    outs = [anywhere if i in raw_out else vmem for i in range(len(out_shape))]
    return pl.pallas_call(
        kernel,
        out_shape=tuple(out_shape),
        in_specs=specs,
        out_specs=tuple(outs),
        scratch_shapes=scratch,
        compiler_params=pltpu.CompilerParams(vmem_limit_bytes=grant << 20),
        cost_estimate=pl.CostEstimate(flops=cost, bytes_accessed=1 << 20, transcendentals=0),
    )(*args)


def shape(dims, dtype=F32):
    return jax.ShapeDtypeStruct(dims, dtype)


def per_device(mesh_shape, state_field, skip_gain, embed_weight, qkv_weight, head_scale, out_weight, norm_gain, back_weight):
    return program(
        mesh_shape, state_field, skip_gain, embed_weight, qkv_weight, head_scale, out_weight, norm_gain, back_weight
    )


def program(mesh_shape, state_field, skip_gain, embed_weight, qkv_weight, head_scale, out_weight, norm_gain, back_weight):
    lons, lats = mesh_shape["lon"], mesh_shape["lat"]
    rows, width = state_field.shape
    geo = Geometry(rows, width // C)
    lat, lon = lax.axis_index("lat"), lax.axis_index("lon")
    place = jnp.stack([lat, lon]).astype(jnp.int32)

    even_pairs = [(i, i ^ 1) for i in range(lons)]
    odd_pairs = [(i, (i + 1 if i % 2 else i - 1) % lons) for i in range(lons)]
    swap = [(i, lats - 1 - i) for i in range(lats)]

    def shifted(value, by):
        return lax.ppermute(value, "lon", [(i, (i + by) % lons) for i in range(lons)])

    wide = SIDE * C
    extended = NEAR + rows + NEAR
    side_e, side_o, edge = call(
        sides_kernel,
        [shape(side_shape(rows), BF16)] * 2 + [shape((HALO, width), BF16)],
        [pltpu.VMEM((2, rows, LANES), BF16), pltpu.SemaphoreType.DMA((5,))],
        place,
        state_field,
        raw=(1,),
        stay=(1,),
        cost=1_000_000,
    )
    edge = lax.ppermute(edge, "lat", swap)
    side_e = lax.ppermute(side_e, "lon", even_pairs)
    side_o = lax.ppermute(side_o, "lon", odd_pairs)

    w = [None] + [geo.span[level][1] * LANES for level in (1, 2, 3, 4)]
    low = lambda level, lanes: pltpu.VMEM((geo.low[level][1], w[lanes]), F32)
    bands = [(3, geo.band[level][1], w[level]) for level in (1, 2, 3, 4)]
    ll4, d2, d3, d4, deep_e, deep_o, p2, m2, p3, m3 = call(
        functools.partial(analysis_kernel, geo, lats),
        [shape((geo.low[4][1], w[4]))]
        + [shape(dims) for dims in bands[1:]]
        + [shape(plan_shape(geo, d), BF16) for d in (1, 1, 2, 2, 3, 3)],
        [
            pltpu.VMEM((geo.extended, width), BF16),
            pltpu.VMEM((geo.low[1][1], width), F32),
            low(1, 1),
            pltpu.VMEM((geo.low[1][1], w[1]), BF16),
            pltpu.VMEM((geo.low[1][1], w[1]), BF16),
            low(2, 1),
            low(2, 2),
            low(3, 2),
            low(3, 3),
            low(4, 3),
        ]
        + [pltpu.VMEM((geo.band[level][1], w[level - 1]), F32) for level in (2, 3, 4)]
        + [pltpu.SemaphoreType.DMA((geo.low[1][1] // 112,))],
        place,
        edge,
        skip_gain,
        state_field,
        raw=(3,),
        stay=(3,),
    )
    corner, beside = call(
        functools.partial(corners_kernel, geo),
        [shape((NEAR, 2 * wide), BF16), shape((rows, 2 * wide), BF16)],
        [],
        place,
        side_e,
        side_o,
        cost=100_000,
    )
    corner = lax.ppermute(corner, "lat", swap)
    count = geo.band[1][1]
    inner, lo_rim, hi_rim = call(
        functools.partial(inner_kernel, geo, lats),
        [shape(bands[0]), shape((count, 2 * wide)), shape((count, 2 * wide))],
        [
            pltpu.VMEM((extended, width), BF16),
            pltpu.VMEM((count, width), F32),
            pltpu.VMEM((count, width), F32),
            pltpu.SemaphoreType.DMA,
        ],
        place,
        edge,
        skip_gain,
        state_field,
        raw=(3,),
        stay=(3,),
    )
    ends = 2 * edge_pairs() * LANES
    (part,) = call(
        functools.partial(first_level_kernel, geo, lats),
        [shape((rows, width))],
        [
            pltpu.VMEM((extended, 2 * wide), BF16),
            pltpu.VMEM((count, 2 * wide), F32),
            pltpu.VMEM((count, 2 * wide), F32),
            pltpu.VMEM((3, count, ends), F32),
            pltpu.VMEM((rows, w[1]), F32),
            pltpu.VMEM((rows, w[1]), F32),
            pltpu.VMEM((2 * LANES, w[1]), BF16),
            pltpu.VMEM((2 * LANES, w[1]), BF16),
        ],
        place,
        beside,
        corner,
        skip_gain,
        inner,
        lo_rim,
        hi_rim,
        grant=30,
    )

    merged, size = ll4, 1
    total = geo.cells[4] * lons * C
    while size < lons:
        other = lax.ppermute(merged, "lon", [(i, i ^ size) for i in range(lons)])
        more = geo.cells[4] * C * size
        dims = (merged.shape[0], merged.shape[1] + more)
        if 2 * size < lons:
            (merged,) = call(
                functools.partial(merge_kernel, size, more), [shape(dims)], [], place, merged, other, cost=100_000
            )
        else:
            ring, tokens = call(
                functools.partial(last_merge_kernel, geo, size, more),
                [shape((dims[0], total)), shape((geo.rows[4], total), BF16)],
                [pltpu.VMEM(dims, F32)],
                place,
                merged,
                other,
                cost=100_000,
            )
        size = 2 * size
    others = lax.ppermute(tokens, "lat", swap)

    deep_e = lax.ppermute(deep_e, "lon", even_pairs)
    deep_o = lax.ppermute(deep_o, "lon", odd_pairs)
    from_m2, from_p2 = shifted(p2, 2), shifted(m2, -2)
    from_m3, from_p3 = shifted(p3, 3), shifted(m3, -3)

    key_count = 2 * geo.rows[4] * geo.cells[4] * lons
    blocks = key_count // 928 if key_count % 928 == 0 else 1
    (coarse,) = call(
        functools.partial(attention_kernel, geo, lats, blocks),
        [shape((geo.low[4][1], w[4]))],
        [
            pltpu.VMEM((geo.low[4][1], total + 6 * C), F32),
            pltpu.VMEM((key_count, C), F32),
            pltpu.VMEM((key_count, C), BF16),
        ],
        place,
        ring,
        tokens,
        others,
        embed_weight,
        qkv_weight,
        head_scale,
        out_weight,
        norm_gain[None],
        back_weight.T,
        cost=200_000_000,
        grant=40,
    )

    (out,) = call(
        functools.partial(synthesis_kernel, geo, lats),
        [shape((rows, width), BF16)],
        [pltpu.VMEM((geo.band[level][1], w[level]), F32) for level in (3, 2, 1)]
        + [
            pltpu.VMEM((rows, w[1]), F32),
            pltpu.VMEM((geo.band[1][1], w[2]), F32),
            pltpu.VMEM((rows, width), BF16),
            pltpu.SemaphoreType.DMA((rows // 112 + 1,)),
        ],
        place,
        coarse,
        deep_e,
        deep_o,
        from_m2,
        from_p2,
        from_m3,
        from_p3,
        part,
        d2,
        d3,
        d4,
        raw_out=(0,),
        grant=30,
    )
    return out


def solution(mesh):
    in_specs = (P("lat", ("member", "lon")), P(), P(), P(), P(), P(), P(), P())
    out_specs = P("lat", ("member", "lon"))
    return jax.shard_map(
        functools.partial(per_device, dict(mesh.shape)),
        mesh=mesh,
        in_specs=in_specs,
        out_specs=out_specs,
        check_vma=False,
    )
```
